32 devices in a mesh: replica: 8 (over z, core), shard: 4 (over y, x).
Axes of the slice: x: 2, y: 2, z: 4, core: 2. Of those that a mesh axis runs over, the one named last changes fastest.
Arguments:
- tokens: bfloat16 [64, 512, 768], P(('replica', 'shard')), may hold values from -8 to 8
- lengths: int32 [64], P(('replica', 'shard')), may hold values from 256 to 512, as said below
- w_query: bfloat16 [768, 768], P('shard'), may hold values from -0.21875 to 0.21875
- b_query: bfloat16 [768], P('shard'), may hold values from -3 to 3
- w_key: bfloat16 [768, 768], P('shard'), may hold values from -0.21875 to 0.21875
- w_value: bfloat16 [768, 768], P('shard'), may hold values from -0.21875 to 0.21875
- b_value: bfloat16 [768], P('shard'), may hold values from -3 to 3
- w_attn_out: bfloat16 [768, 768], P('shard'), may hold values from -4 to 4
- b_attn_out: bfloat16 [768], P('shard'), may hold values from -3 to 3
- gain_one: bfloat16 [768], P('shard'), may hold values from 0.099609375 to 1.8984375
- shift_one: bfloat16 [768], P('shard'), may hold values from -2 to 2
- w_expand: bfloat16 [768, 3072], P('shard'), may hold values from -0.21875 to 0.21875
- b_expand: bfloat16 [3072], P('shard'), may hold values from -3 to 3
- w_contract: bfloat16 [3072, 768], P('shard'), may hold values from -0.109375 to 0.109375
- b_contract: bfloat16 [768], P('shard'), may hold values from -3 to 3
- gain_two: bfloat16 [768], P('shard'), may hold values from 0.099609375 to 1.8984375
- shift_two: bfloat16 [768], P('shard'), may hold values from -2 to 2
- w_colbert: bfloat16 [768, 128], P('shard'), may hold values from -0.21875 to 0.21875
- cotangent: bfloat16 [64, 512, 128], P(('replica', 'shard')), may hold values from -48 to 48
Outputs:
- embeddings: bfloat16 [64, 512, 128], P(('replica', 'shard'))
- grad_tokens: bfloat16 [64, 512, 768], P(('replica', 'shard'))
- grad_w_query: float32 [768, 768], P('shard')
- grad_b_query: float32 [768], P('shard')
- grad_w_key: float32 [768, 768], P('shard')
- grad_w_value: float32 [768, 768], P('shard')
- grad_b_value: float32 [768], P('shard')
- grad_w_attn_out: float32 [768, 768], P('shard')
- grad_b_attn_out: float32 [768], P('shard')
- grad_gain_one: float32 [768], P('shard')
- grad_shift_one: float32 [768], P('shard')
- grad_w_expand: float32 [768, 3072], P('shard')
- grad_b_expand: float32 [3072], P('shard')
- grad_w_contract: float32 [3072, 768], P('shard')
- grad_b_contract: float32 [768], P('shard')
- grad_gain_two: float32 [768], P('shard')
- grad_shift_two: float32 [768], P('shard')
- grad_w_colbert: float32 [768, 128], P('shard')
- rms_values: float32 [3], replicated
The draws below stay inside these ranges and needn't reach their ends.
Inputs may be any that keep to these rules, and one draw needn't show every extreme that they name: `lengths`: valid leading positions of each sequence; some sequence has 512 of them and some has 256.
All inputs are finite; a program needn't handle non-finite values.
Results may differ from the reference program's by a relative error of at most 0.017.
Values may be sent and summed in bfloat16 or wider, within the bound.
No kernel may reach another device: no remote copies, remote signals or barrier semaphores. Data moves between devices by JAX's collectives and lax.ppermute only.
A program may use at most 256 MiB of HBM per device.

```python
import jax
import jax.numpy as jnp
from jax import lax

D = 768
HEADS = 12
HEAD_DIM = 64
FF = 3072
OUT = 128
LEN = 512
SEQS = 64


def draw_lengths(key, part):
    key_values, key_order = jax.random.split(jax.random.fold_in(key, 17))
    values = jax.random.randint(key_values, (SEQS,), LEN // 2, LEN + 1)
    order = jax.random.permutation(key_order, SEQS)
    values = jnp.where(order == 0, LEN, values)
    values = jnp.where(order == 1, LEN // 2, values)
    return values.astype(jnp.int32)


def draw_tokens(key, part):
    inner = jax.random.fold_in(key, 29)
    place = jnp.arange(SEQS, dtype=jnp.float32) / max(SEQS - 1, 1)
    base = jnp.clip(jax.random.normal(inner, (SEQS, LEN, D), jnp.float32), -4.0, 4.0)
    factor = jnp.exp(place * jnp.log(1.8))
    return (base * factor[:, None, None]).astype(jnp.bfloat16)


def shard_levels(own_key, shape, cuts, low, largest):
    loudness, own = 1.0, jax.random.fold_in(own_key, 6)
    for axis_at, blocks in cuts:
        heights = jnp.exp(jax.random.uniform(jax.random.fold_in(own, axis_at), (blocks,), jnp.float32, low / len(cuts), largest / len(cuts)))
        loudness = loudness * jnp.repeat(heights, shape[axis_at] // blocks).reshape([-1 if axis == axis_at else 1 for axis in range(len(shape))])
    return loudness


def gaussian(own_key, shape, scale, reach, cuts=(), held_as=jnp.bfloat16):
    entries = scale * jax.random.normal(own_key, shape, jnp.float32)
    if cuts:
        entries = entries * shard_levels(own_key, shape, cuts, -0.22, 0.18)
    return jnp.clip(entries, -reach, reach).astype(held_as)


def setup_inputs(seed: int = 0) -> dict:
    key_of = jax.random.split(jax.random.key(seed), 20)
    return {
        "tokens": draw_tokens(jax.random.fold_in(key_of[19], 71), 0),
        "lengths": draw_lengths(jax.random.fold_in(key_of[19], 71), 0),
        "w_query": gaussian(key_of[2], (D, D), D ** -0.5, 0.21875, ((0, 4),)),
        "b_query": gaussian(key_of[3], (D,), 0.5, 3.0, ((0, 4),)),
        "w_key": gaussian(key_of[4], (D, D), D ** -0.5, 0.21875, ((0, 4),)),
        "w_value": gaussian(key_of[5], (D, D), D ** -0.5, 0.21875, ((0, 4),)),
        "b_value": gaussian(key_of[6], (D,), 0.5, 3.0, ((0, 4),)),
        "w_attn_out": gaussian(key_of[7], (D, D), (max(1, LEN // 256)) ** -0.5, 4.0, ((0, 4),)),
        "b_attn_out": gaussian(key_of[8], (D,), 0.5, 3.0, ((0, 4),)),
        "gain_one": jnp.clip(1.0 + 0.18 * jax.random.normal(key_of[9], (D,), jnp.float32), 0.099609375, 1.8984375).astype(jnp.bfloat16),
        "shift_one": gaussian(key_of[10], (D,), 0.3, 2.0, ((0, 4),)),
        "w_expand": gaussian(key_of[11], (D, FF), D ** -0.5, 0.21875, ((0, 4),)),
        "b_expand": gaussian(key_of[12], (FF,), 0.5, 3.0, ((0, 4),)),
        "w_contract": gaussian(key_of[13], (FF, D), FF ** -0.5, 0.109375, ((0, 4),)),
        "b_contract": gaussian(key_of[14], (D,), 0.5, 3.0, ((0, 4),)),
        "gain_two": jnp.clip(1.0 + 0.18 * jax.random.normal(key_of[15], (D,), jnp.float32), 0.099609375, 1.8984375).astype(jnp.bfloat16),
        "shift_two": gaussian(key_of[16], (D,), 0.3, 2.0, ((0, 4),)),
        "w_colbert": gaussian(key_of[17], (D, OUT), D ** -0.5, 0.21875, ((0, 4),)),
        "cotangent": gaussian(key_of[18], (SEQS, LEN, OUT), 8.0, 48.0, ((0, 32),)),
    }


norm_epsilon = 1e-12
masked_score = -1e+30

@jax.custom_vjp
def low(v):
    return lax.optimization_barrier(v.astype(jnp.bfloat16)).astype(jnp.float32)

@jax.custom_vjp
def low_back(v):
    return v

def low_keep(v):
    return (low(v), None)

def low_pass(kept, grad):
    return (grad,)

def back_keep(v):
    return (v, None)

def back_low(kept, grad):
    return (low(grad),)
low.defvjp(low_keep, low_pass)
low_back.defvjp(back_keep, back_low)

def matmul(left, right):
    return jnp.dot(left, right, precision=lax.Precision.HIGHEST, preferred_element_type=jnp.float32)

def layer_norm(summed, gain, shift):
    center = summed - lax.optimization_barrier(jnp.mean(summed, axis=-1, keepdims=True))
    inverse = lax.rsqrt(lax.optimization_barrier(jnp.mean(center * center, axis=-1, keepdims=True)) + norm_epsilon)
    return center * inverse * gain + shift

def attention(queries, keys_seq, values_seq, valid_keys):
    seq_len = queries.shape[0]
    heads_q = queries.reshape(seq_len, HEADS, HEAD_DIM)
    heads_k = keys_seq.reshape(seq_len, HEADS, HEAD_DIM)
    heads_v = values_seq.reshape(seq_len, HEADS, HEAD_DIM)
    scores = jnp.einsum('qhd,khd->hqk', heads_q, heads_k, precision=lax.Precision.HIGHEST) * HEAD_DIM ** (-0.5)
    scores = low_back(scores)
    scores = jnp.where(valid_keys[None, None, :], scores, masked_score)
    weights = low(jax.nn.softmax(scores, axis=-1))
    context = jnp.einsum('hqk,khd->qhd', weights, heads_v, precision=lax.Precision.HIGHEST)
    return context.reshape(seq_len, HEADS * HEAD_DIM)

def sequence_forward(params, inputs, length):
    w_query, b_query, w_key, w_value, b_value, w_attn_out, b_attn_out, gain_one, shift_one, w_expand, b_expand, w_contract, b_contract, gain_two, shift_two, w_colbert = params
    seq_len = inputs.shape[0]
    valid = jnp.arange(seq_len, dtype=jnp.int32) < length
    valid_f = valid.astype(jnp.float32)[:, None]
    queries = low(low_back(matmul(inputs, w_query) + b_query))
    keys_seq = low(low_back(matmul(inputs, w_key)))
    values_seq = low(low_back(matmul(inputs, w_value) + b_value))
    context = low(low_back(attention(queries, keys_seq, values_seq, valid)))
    attended = low_back(matmul(context, w_attn_out) + b_attn_out)
    hidden_one = layer_norm(inputs + attended, gain_one, shift_one)
    expanded = low_back(matmul(low(hidden_one), w_expand) + b_expand)
    activated = low(jax.nn.gelu(expanded, approximate=False))
    contracted = low_back(matmul(activated, w_contract) + b_contract)
    hidden_two = layer_norm(hidden_one + contracted, gain_two, shift_two)
    projected = low_back(matmul(low(hidden_two), w_colbert))
    normalized = projected * lax.rsqrt(lax.optimization_barrier(jnp.sum(projected * projected, axis=-1, keepdims=True)) + norm_epsilon)
    embedded = jnp.where(valid[:, None], normalized, 0.0)
    squares = jnp.stack([jnp.sum(inputs * inputs * valid_f), jnp.sum(attended * attended * valid_f), jnp.sum(contracted * contracted * valid_f)])
    return (embedded, squares)

def reference(tokens, lengths, w_query, b_query, w_key, w_value, b_value, w_attn_out, b_attn_out, gain_one, shift_one, w_expand, b_expand, w_contract, b_contract, gain_two, shift_two, w_colbert, cotangent):
    params = tuple((weight.astype(jnp.float32) for weight in (w_query, b_query, w_key, w_value, b_value, w_attn_out, b_attn_out, gain_one, shift_one, w_expand, b_expand, w_contract, b_contract, gain_two, shift_two, w_colbert)))

    def per_sequence(carry, item):
        grads_sum, squares_sum = carry
        inputs, length, grad_out = item

        def closed(weights, rows):
            return sequence_forward(weights, rows, length)
        embedded, pullback, squares = jax.vjp(closed, params, inputs.astype(jnp.float32), has_aux=True)
        grad_params, grad_inputs = pullback(grad_out.astype(jnp.float32))
        new_grads = tuple((total + part for total, part in zip(grads_sum, grad_params)))
        return ((new_grads, squares_sum + squares), (embedded.astype(jnp.bfloat16), grad_inputs.astype(jnp.bfloat16)))
    start = (tuple((jnp.zeros_like(weight) for weight in params)), jnp.zeros((3,), jnp.float32))
    (grads, squares), (embeddings, grad_tokens) = lax.scan(per_sequence, start, (tokens, lengths, cotangent))
    count = jnp.sum(lengths).astype(jnp.float32)
    rms_values = jnp.sqrt(squares / (count * D))
    g_wq, g_bq, g_wk, g_wv, g_bv, g_wo, g_bo, g_ga, g_sa, g_we, g_be, g_wc, g_bc, g_gb, g_sb, g_wp = grads
    return (embeddings, grad_tokens, g_wq, g_bq, g_wk, g_wv, g_bv, g_wo, g_bo, g_ga, g_sa, g_we, g_be, g_wc, g_bc, g_gb, g_sb, g_wp, rms_values)
```

```python
from functools import partial

import jax
import jax.numpy as jnp
from jax import lax
from jax.sharding import PartitionSpec as P

HEADS = 12
HEAD_DIM = 64


norm_epsilon = 1e-12
masked_score = -1e30


def product(left, right):
    return jnp.dot(left, right, preferred_element_type=jnp.float32)


def product_left_t(left, right):
    return lax.dot_general(
        left, right, (((0,), (0,)), ((), ())), preferred_element_type=jnp.float32
    )


def product_right_t(left, right):
    return lax.dot_general(
        left, right, (((1,), (1,)), ((), ())), preferred_element_type=jnp.float32
    )


def layer_norm(summed, gain, shift):
    center = summed - jnp.mean(summed, axis=-1, keepdims=True)
    inverse = lax.rsqrt(jnp.mean(center * center, axis=-1, keepdims=True) + norm_epsilon)
    normed = center * inverse
    return (normed * gain.astype(jnp.float32) + shift.astype(jnp.float32), normed, inverse)


def norm_backward(grad_out, gain, normed, inverse):
    scaled = grad_out * gain.astype(jnp.float32)
    grad_in = inverse * (
        scaled
        - jnp.mean(scaled, axis=-1, keepdims=True)
        - normed * jnp.mean(scaled * normed, axis=-1, keepdims=True)
    )
    return (grad_in, jnp.sum(grad_out * normed, axis=0), jnp.sum(grad_out, axis=0))


def block_layout(seq_len):
    block_rows = min(512, seq_len)
    return (block_rows, seq_len // block_rows)


def attend_sequence(item):
    queries, keys_seq, values_seq, length = item
    seq_len = queries.shape[0]
    block_rows, block_count = block_layout(seq_len)
    score_scale = HEAD_DIM ** (-0.5)
    valid_keys = jnp.arange(seq_len, dtype=jnp.int32) < length
    heads_k = keys_seq.reshape(seq_len, HEADS, HEAD_DIM)
    heads_v = values_seq.reshape(seq_len, HEADS, HEAD_DIM)

    def one_block(query_block):
        scores = (
            jnp.einsum("qhd,khd->hqk", query_block, heads_k, preferred_element_type=jnp.float32)
            * score_scale
        )
        scores = jnp.where(valid_keys[None, None, :], scores, masked_score)
        highest = jnp.max(scores, axis=-1, keepdims=True)
        exponent = jnp.exp(scores - highest)
        totals = jnp.sum(exponent, axis=-1, keepdims=True)
        weights_low = (exponent / totals).astype(jnp.bfloat16)
        context = jnp.einsum(
            "hqk,khd->qhd", weights_low, heads_v, preferred_element_type=jnp.float32
        )
        return (
            context.astype(jnp.bfloat16).reshape(block_rows, HEADS * HEAD_DIM),
            (highest + jnp.log(totals))[..., 0],
        )

    blocks = queries.reshape(block_count, block_rows, HEADS, HEAD_DIM)
    context, logsum = lax.map(one_block, blocks)
    return (context.reshape(seq_len, HEADS * HEAD_DIM), logsum)


def attend_backward(item):
    queries, keys_seq, values_seq, length, logsum, grad_context = item
    seq_len = queries.shape[0]
    block_rows, block_count = block_layout(seq_len)
    score_scale = HEAD_DIM ** (-0.5)
    valid_keys = jnp.arange(seq_len, dtype=jnp.int32) < length
    heads_k = keys_seq.reshape(seq_len, HEADS, HEAD_DIM)
    heads_v = values_seq.reshape(seq_len, HEADS, HEAD_DIM)
    query_blocks = queries.reshape(block_count, block_rows, HEADS, HEAD_DIM)
    grad_blocks = grad_context.reshape(block_count, block_rows, HEADS, HEAD_DIM)

    def block_step(carry, piece):
        grad_keys, grad_values = carry
        query_block, grad_block, logsum_block = piece
        scores = (
            jnp.einsum("qhd,khd->hqk", query_block, heads_k, preferred_element_type=jnp.float32)
            * score_scale
        )
        scores = jnp.where(valid_keys[None, None, :], scores, masked_score)
        weights = jnp.exp(scores - logsum_block[..., None])
        weights_low = weights.astype(jnp.bfloat16)
        grad_values = grad_values + jnp.einsum(
            "hqk,qhd->khd", weights_low, grad_block, preferred_element_type=jnp.float32
        )
        grad_weights = jnp.einsum(
            "qhd,khd->hqk", grad_block, heads_v, preferred_element_type=jnp.float32
        )
        grad_scores = weights * (
            grad_weights - jnp.sum(weights * grad_weights, axis=-1, keepdims=True)
        )
        grad_scores = grad_scores.astype(jnp.bfloat16)
        grad_query = (
            jnp.einsum("hqk,khd->qhd", grad_scores, heads_k, preferred_element_type=jnp.float32)
            * score_scale
        )
        grad_keys = (
            grad_keys
            + jnp.einsum(
                "hqk,qhd->khd", grad_scores, query_block, preferred_element_type=jnp.float32
            )
            * score_scale
        )
        return ((grad_keys, grad_values), grad_query)

    zeros = jnp.zeros((seq_len, HEADS, HEAD_DIM), jnp.float32)
    (grad_keys, grad_values), grad_query = lax.scan(
        block_step, (zeros, zeros), (query_blocks, grad_blocks, logsum)
    )
    width = HEADS * HEAD_DIM
    return (
        grad_query.reshape(seq_len, width).astype(jnp.bfloat16),
        grad_keys.reshape(seq_len, width).astype(jnp.bfloat16),
        grad_values.reshape(seq_len, width).astype(jnp.bfloat16),
    )


def shard_partners(distance):
    return [(i, i ^ distance) for i in range(lax.axis_size("shard"))]


def replica_partners(distance):
    return [(i, i ^ distance) for i in range(lax.axis_size("replica"))]


def gather_rows(own):
    shards = lax.axis_size("shard")
    mine = lax.axis_index("shard")
    core = lax.axis_index("replica") % 2
    rows, width = own.shape
    half = rows // 2
    sent = lax.dynamic_slice_in_dim(own, core * half, half, 0)
    full = jnp.zeros((shards * rows, width), own.dtype)
    full = lax.dynamic_update_slice_in_dim(full, own, mine * rows, 0)
    for distance in range(1, shards):
        near = lax.ppermute(sent, "shard", shard_partners(distance))
        far = lax.ppermute(near, "replica", replica_partners(1))
        start = (mine ^ distance) * rows
        full = lax.dynamic_update_slice_in_dim(full, near, start + core * half, 0)
        full = lax.dynamic_update_slice_in_dim(full, far, start + (1 - core) * half, 0)
    return full


def reduce_rows(part):
    shards = lax.axis_size("shard")
    replicas = lax.axis_size("replica")
    mine = lax.axis_index("shard")
    core = lax.axis_index("replica") % 2
    half = part.shape[0] // (2 * shards)

    def block(distance, which):
        return lax.dynamic_slice_in_dim(part, ((mine ^ distance) * 2 + which) * half, half, 0)

    given = jnp.concatenate([block(d, 1 - core) for d in range(shards)]).astype(jnp.bfloat16)
    taken = lax.ppermute(given, "replica", replica_partners(1))
    sums = [
        block(d, core).astype(jnp.bfloat16).astype(jnp.float32)
        + taken[d * half : (d + 1) * half].astype(jnp.float32)
        for d in range(shards)
    ]
    total = sums[0]
    for distance in range(1, shards):
        total = total + lax.ppermute(
            sums[distance].astype(jnp.bfloat16), "shard", shard_partners(distance)
        ).astype(jnp.float32)
    distance = 2
    low = total.astype(jnp.bfloat16)
    while distance < replicas:
        other = lax.ppermute(low, "replica", replica_partners(distance))
        low = (low.astype(jnp.float32) + other.astype(jnp.float32)).astype(jnp.bfloat16)
        distance *= 2
    other = lax.ppermute(low, "replica", replica_partners(1))
    first = jnp.where(core == 0, low, other)
    second = jnp.where(core == 0, other, low)
    return jnp.concatenate([first, second]).astype(jnp.float32)


def sum_everywhere(part):
    for axis in ("replica", "shard"):
        distance = 1
        while distance < lax.axis_size(axis):
            pairs = [(i, i ^ distance) for i in range(lax.axis_size(axis))]
            part = part + lax.ppermute(part, axis, pairs)
            distance *= 2
    return part


def per_device(
    tokens,
    lengths,
    w_query,
    b_query,
    w_key,
    w_value,
    b_value,
    w_attn_out,
    b_attn_out,
    gain_one,
    shift_one,
    w_expand,
    b_expand,
    w_contract,
    b_contract,
    gain_two,
    shift_two,
    w_colbert,
    cotangent,
):
    seq_count, seq_len, width = tokens.shape
    row_count = seq_count * seq_len
    shards = lax.axis_size("shard")
    part = width // shards
    ff = b_expand.shape[0] * shards
    small = jnp.stack(
        [b_query, b_value, b_attn_out, gain_one, shift_one, b_contract, gain_two, shift_two]
        + [b_expand[i * part : (i + 1) * part] for i in range(ff // width)]
    )
    small = lax.all_gather(small, "shard", axis=0)
    query_b, value_b, out_b, gain_a, shift_a, contract_b, gain_b, shift_b = [
        small[:, i].reshape(width) for i in range(8)
    ]
    expand_b = small[:, 8:].reshape(ff)
    attn_w = gather_rows(jnp.concatenate([w_query, w_key, w_value], axis=1))
    query_w, key_w, value_w = [attn_w[:, i * width : (i + 1) * width] for i in range(3)]
    mid_w = gather_rows(jnp.concatenate([w_attn_out, w_expand, w_colbert], axis=1))
    out_w, expand_w, colbert_w = (
        mid_w[:, :width],
        mid_w[:, width : width + ff],
        mid_w[:, width + ff :],
    )
    contract_w = gather_rows(w_contract)
    inputs = tokens.reshape(row_count, width)
    positions = jnp.arange(seq_len, dtype=jnp.int32)
    valid_f = (positions[None, :] < lengths[:, None]).astype(jnp.float32).reshape(row_count, 1)
    queries = (product(inputs, query_w) + query_b.astype(jnp.float32)).astype(jnp.bfloat16)
    keys_all = product(inputs, key_w).astype(jnp.bfloat16)
    values_all = (product(inputs, value_w) + value_b.astype(jnp.float32)).astype(jnp.bfloat16)
    seq_shape = (seq_count, seq_len, width)
    context, logsum = lax.map(
        attend_sequence,
        (
            queries.reshape(seq_shape),
            keys_all.reshape(seq_shape),
            values_all.reshape(seq_shape),
            lengths,
        ),
    )
    context = context.reshape(row_count, width)
    attended = product(context, out_w) + out_b.astype(jnp.float32)
    inputs_f = inputs.astype(jnp.float32)
    hidden_one, normed_one, inverse_one = layer_norm(inputs_f + attended, gain_a, shift_a)
    hidden_low = hidden_one.astype(jnp.bfloat16)
    expanded = product(hidden_low, expand_w) + expand_b.astype(jnp.float32)
    activated = jax.nn.gelu(expanded, approximate=False).astype(jnp.bfloat16)
    contracted = product(activated, contract_w) + contract_b.astype(jnp.float32)
    hidden_two, normed_two, inverse_two = layer_norm(hidden_one + contracted, gain_b, shift_b)
    hidden_two_low = hidden_two.astype(jnp.bfloat16)
    projected = product(hidden_two_low, colbert_w)
    inverse_len = lax.rsqrt(jnp.sum(projected * projected, axis=-1, keepdims=True) + norm_epsilon)
    normalized = projected * inverse_len
    embeddings = (normalized * valid_f).astype(jnp.bfloat16).reshape(seq_count, seq_len, -1)
    squares = jnp.stack(
        [
            jnp.sum(inputs_f * inputs_f * valid_f),
            jnp.sum(attended * attended * valid_f),
            jnp.sum(contracted * contracted * valid_f),
        ]
    )
    grad_norm = cotangent.reshape(row_count, -1).astype(jnp.float32) * valid_f
    grad_projected = (
        inverse_len
        * (grad_norm - normalized * jnp.sum(normalized * grad_norm, axis=-1, keepdims=True))
    ).astype(jnp.bfloat16)
    grad_colbert = product_left_t(hidden_two_low, grad_projected)
    grad_hidden_two = product_right_t(grad_projected, colbert_w)
    grad_sum_two, grad_gain_two, grad_shift_two = norm_backward(
        grad_hidden_two, gain_b, normed_two, inverse_two
    )
    grad_contracted = grad_sum_two.astype(jnp.bfloat16)
    grad_contract_b = jnp.sum(grad_contracted, axis=0, dtype=jnp.float32)
    grad_contract_w = product_left_t(activated, grad_contracted)
    grad_activated = product_right_t(grad_contracted, contract_w)
    unused, gelu_back = jax.vjp(partial(jax.nn.gelu, approximate=False), expanded)
    grad_expanded = gelu_back(grad_activated)[0].astype(jnp.bfloat16)
    grad_expand_b = jnp.sum(grad_expanded, axis=0, dtype=jnp.float32)
    grad_expand_w = product_left_t(hidden_low, grad_expanded)
    r_wc = reduce_rows(grad_contract_w)
    grad_hidden_one = grad_sum_two + product_right_t(grad_expanded, expand_w)
    grad_sum_one, grad_gain_one, grad_shift_one = norm_backward(
        grad_hidden_one, gain_a, normed_one, inverse_one
    )
    grad_attended = grad_sum_one.astype(jnp.bfloat16)
    grad_out_b = jnp.sum(grad_attended, axis=0, dtype=jnp.float32)
    grad_out_w = product_left_t(context, grad_attended)
    r_mid = reduce_rows(
        jnp.concatenate([grad_out_w, grad_expand_w, grad_colbert], axis=1)
    )
    grad_context = product_right_t(grad_attended, out_w).astype(jnp.bfloat16)
    grad_queries, grad_keys, grad_values = lax.map(
        attend_backward,
        (
            queries.reshape(seq_shape),
            keys_all.reshape(seq_shape),
            values_all.reshape(seq_shape),
            lengths,
            logsum,
            grad_context.reshape(seq_shape),
        ),
    )
    grad_queries = grad_queries.reshape(row_count, width)
    grad_keys = grad_keys.reshape(row_count, width)
    grad_values = grad_values.reshape(row_count, width)
    grad_query_b = jnp.sum(grad_queries, axis=0, dtype=jnp.float32)
    grad_value_b = jnp.sum(grad_values, axis=0, dtype=jnp.float32)
    grad_query_w = product_left_t(inputs, grad_queries)
    grad_key_w = product_left_t(inputs, grad_keys)
    grad_value_w = product_left_t(inputs, grad_values)
    r_attn = reduce_rows(jnp.concatenate([grad_query_w, grad_key_w, grad_value_w], axis=1))
    sums = jnp.concatenate([squares, jnp.sum(valid_f)[None], jnp.zeros(width - 4, jnp.float32)])
    vectors = jnp.stack(
        [
            grad_query_b,
            grad_value_b,
            grad_out_b,
            grad_gain_one,
            grad_shift_one,
            grad_contract_b,
            grad_gain_two,
            grad_shift_two,
            sums,
        ]
    )
    vectors = jnp.concatenate([vectors, grad_expand_b.reshape(ff // width, width)])
    vectors = sum_everywhere(vectors)
    rms_values = jnp.sqrt(vectors[8, :3] / (vectors[8, 3] * width))
    r_be = lax.dynamic_slice_in_dim(
        vectors[9:].reshape(ff), lax.axis_index("shard") * (ff // shards), ff // shards
    )
    own = lax.dynamic_slice_in_dim(vectors, lax.axis_index("shard") * part, part, 1)
    r_bq, r_bv, r_bo, r_ga, r_sa, r_bc, r_gb, r_sb = [own[i] for i in range(8)]
    grad_inputs = (
        grad_sum_one
        + product_right_t(grad_queries, query_w)
        + product_right_t(grad_keys, key_w)
        + product_right_t(grad_values, value_w)
    )
    grad_tokens = grad_inputs.astype(jnp.bfloat16).reshape(seq_count, seq_len, width)
    r_wq, r_wk, r_wv = [r_attn[:, i * width : (i + 1) * width] for i in range(3)]
    r_wo, r_we, r_wp = (
        r_mid[:, :width],
        r_mid[:, width : width + ff],
        r_mid[:, width + ff :],
    )
    return (
        embeddings,
        grad_tokens,
        r_wq,
        r_bq,
        r_wk,
        r_wv,
        r_bv,
        r_wo,
        r_bo,
        r_ga,
        r_sa,
        r_we,
        r_be,
        r_wc,
        r_bc,
        r_gb,
        r_sb,
        r_wp,
        rms_values,
    )


def solution(mesh):
    placed = (
        P(("replica", "shard"), None, None),
        P(("replica", "shard")),
        P("shard", None),
        P("shard"),
        P("shard", None),
        P("shard", None),
        P("shard"),
        P("shard", None),
        P("shard"),
        P("shard"),
        P("shard"),
        P("shard", None),
        P("shard"),
        P("shard", None),
        P("shard"),
        P("shard"),
        P("shard"),
        P("shard", None),
        P(("replica", "shard"), None, None),
    )
    return jax.shard_map(
        per_device,
        mesh=mesh,
        in_specs=placed,
        out_specs=(
            P(("replica", "shard"), None, None),
            P(("replica", "shard"), None, None),
            P("shard", None),
            P("shard"),
            P("shard", None),
            P("shard", None),
            P("shard"),
            P("shard", None),
            P("shard"),
            P("shard"),
            P("shard"),
            P("shard", None),
            P("shard"),
            P("shard", None),
            P("shard"),
            P("shard"),
            P("shard"),
            P("shard", None),
            P(),
        ),
        check_vma=False,
    )
```

```python
from functools import partial

import jax
import jax.numpy as jnp
from jax import lax
from jax.experimental import pallas as pl
from jax.experimental.pallas import tpu as pltpu
from jax.sharding import PartitionSpec as P

HEADS = 12
HEAD_DIM = 64
GROUP_HEADS = 4
GROUP = GROUP_HEADS * HEAD_DIM
PAIR = 2 * HEAD_DIM
EXTRA = 16
BLOCK = 256
CHUNK = 512
SCALE = HEAD_DIM**-0.5
VMEM_LIMIT = 52 * 1024 * 1024

norm_epsilon = 1e-12
masked_score = -1e30
f32 = jnp.float32
bf16 = jnp.bfloat16


def product(left, right):
    return jnp.dot(left, right, preferred_element_type=f32)


def product_left_t(left, right):
    return lax.dot_general(left, right, (((0,), (0,)), ((), ())), preferred_element_type=f32)


def product_right_t(left, right):
    return lax.dot_general(left, right, (((1,), (1,)), ((), ())), preferred_element_type=f32)


def shard_partners(distance):
    return [(i, i ^ distance) for i in range(lax.axis_size("shard"))]


def replica_partners(distance):
    return [(i, i ^ distance) for i in range(lax.axis_size("replica"))]


def after(value, *earlier):
    return lax.optimization_barrier((value, *jax.tree.leaves(earlier)))[0]


def shard_bits():
    distance, bits = 1, []
    while distance < lax.axis_size("shard"):
        bits.append(distance)
        distance *= 2
    return bits


class Gather:
    def __init__(self, own, sent, order):
        self.own = own
        self.near = {0: sent}
        self.order = order
        self.direct = {}
        self.far = {}

    def first(self):
        return self.direct[self.order[0]]

    def start(self, *earlier):
        sent = after(self.near[0], *earlier)
        self.direct = {d: lax.ppermute(sent, "shard", shard_partners(d)) for d in self.order}

    def relay(self, *earlier):
        self.near[self.order[0]] = after(self.first(), *earlier)
        for distance in self.order[1:]:
            for d, piece in list(self.near.items()):
                if d:
                    self.near[d | distance] = lax.ppermute(piece, "shard", shard_partners(distance))
                else:
                    self.near[distance] = after(self.direct[distance], *earlier)

    def swap(self, *earlier):
        for d in range(1, len(self.near)):
            self.near[d] = after(self.near[d], *earlier)
            self.far[d] = lax.ppermute(self.near[d], "replica", replica_partners(1))
        return [self.near[d] for d in range(1, len(self.near))]

    def pieces(self):
        distances = range(1, len(self.near))
        return (self.own, *[self.near[d] for d in distances], *[self.far[d] for d in distances])


def piece_count(shards):
    return 2 * shards - 1


def piece_copies(place, pieces, target, sems, columns=None):
    mine, core = place[0], place[1]
    shards = (len(pieces) + 1) // 2
    rows = pieces[0].shape[0]
    half = rows // 2

    def one(at, source, start, size):
        source = source if columns is None else source.at[:, columns]
        start = pl.multiple_of(start, 16)
        source = source if source.shape[0] == size else source.at[pl.ds(0, size)]
        return pltpu.make_async_copy(source, target.at[pl.ds(start, size)], sems.at[at])

    copies = [one(0, pieces[0], mine * rows, rows)]
    for d in range(1, shards):
        start = (mine ^ d) * rows
        copies.append(one(d, pieces[d], start + core * half, half))
        copies.append(one(shards + d - 1, pieces[shards + d - 1], start + (1 - core) * half, half))
    return copies


def load_pieces(place, *sets):
    copies = [copy for one in sets for copy in piece_copies(place, *one)]
    for copy in copies:
        copy.start()
    for copy in copies:
        copy.wait()


def store_pieces(place, total, mine_ref, peer_ref, extra=None):
    mine, core = place[0], place[1]
    shards = mine_ref.shape[0]
    half = total.shape[0] // (2 * shards)
    for d in range(shards):
        start = (mine ^ d) * 2
        for ref, which in ((mine_ref, core), (peer_ref, 1 - core)):
            at = pl.multiple_of((start + which) * half, 8)
            ref[d, 0:half] = total[pl.ds(at, half), :].astype(bf16)
            if extra is not None:
                ref[d, half:] = extra


def kernel_call(body, name, grid, in_specs, out_specs, out_shape, scratch, flops, moved, prefetch=2):
    return pl.pallas_call(
        body,
        name=name,
        grid_spec=pltpu.PrefetchScalarGridSpec(
            num_scalar_prefetch=prefetch,
            grid=grid,
            in_specs=in_specs,
            out_specs=out_specs,
            scratch_shapes=scratch,
        ),
        out_shape=out_shape,
        compiler_params=pltpu.CompilerParams(
            dimension_semantics=("arbitrary",) * len(grid), vmem_limit_bytes=VMEM_LIMIT
        ),
        cost_estimate=pl.CostEstimate(flops=flops, bytes_accessed=moved, transcendentals=0),
    )


def anywhere(count):
    return [pl.BlockSpec(memory_space=pl.ANY)] * count


def rows_spec(rows, width, column=0):
    return pl.BlockSpec((rows, width), lambda i, *_: (i, column))


def whole_spec(*shape):
    return pl.BlockSpec(shape, lambda *_: (0,) * len(shape))


def shaped(shape, dtype):
    return jax.ShapeDtypeStruct(shape, dtype)


def lanes(rows, width):
    return lax.broadcasted_iota(jnp.int32, (rows, width), 1)


def rows_of(rows, width):
    return lax.broadcasted_iota(jnp.int32, (rows, width), 0)


def attend_kernel(shards, place, lengths, x_ref, bias_ref, *refs):
    count = piece_count(shards)
    pieces, (qkv_ref, context_ref, logsum_ref, weight, sems) = refs[:count], refs[count:]
    step = pl.program_id(0)

    @pl.when(step == 0)
    def _():
        load_pieces(place, (pieces, weight, sems))

    length = lengths[step]
    seq_len = x_ref.shape[0]
    qkv = (product(x_ref[...], weight[...]) + bias_ref[0:1, :]).astype(bf16)
    qkv_ref[...] = qkv
    lane = lanes(seq_len, PAIR)
    padded = rows_of(seq_len, PAIR) >= length
    logsums = jnp.zeros((seq_len, PAIR), f32)
    for pair in range(GROUP_HEADS // 2):
        at = pair * PAIR
        queries = qkv[:, at : at + PAIR].astype(f32) * SCALE
        keys = qkv[:, GROUP + at : GROUP + at + PAIR].astype(f32)
        values = qkv[:, 2 * GROUP + at : 2 * GROUP + at + PAIR].astype(f32)
        halves = []
        for head in range(2):
            own = (lane >= HEAD_DIM) == (head == 1)
            free = HEAD_DIM * (1 - head)
            one = jnp.where(lane == free, 1.0, 0.0)
            q = jnp.where(own, queries, one).astype(bf16)
            k = jnp.where(own, keys, jnp.where(padded, one * masked_score, 0.0)).astype(bf16)
            v = jnp.where(own, values, one).astype(bf16)
            scores = product_right_t(q, k)
            highest = jnp.max(scores, axis=-1, keepdims=True)
            exponent = jnp.exp(scores - highest).astype(bf16)
            summed = product(exponent, v)
            totals = summed[:, free : free + 1]
            halves.append(summed * (1.0 / totals))
            logsums = jnp.where(lane == 2 * pair + head, highest + jnp.log(totals), logsums)
        context = jnp.where(lane < HEAD_DIM, halves[0], halves[1])
        context_ref[:, at : at + PAIR] = context.astype(bf16)
    logsum_ref[...] = logsums


def attend(place, lengths, x, bias, pieces, shards, seq_len):
    rows, width = x.shape
    own = pieces[0]
    return kernel_call(
        partial(attend_kernel, shards),
        "attend",
        (rows // seq_len,),
        [rows_spec(seq_len, width), whole_spec(8, 3 * GROUP)] + anywhere(len(pieces)),
        [rows_spec(seq_len, 3 * GROUP), rows_spec(seq_len, GROUP), rows_spec(seq_len, PAIR)],
        [shaped((rows, 3 * GROUP), bf16), shaped((rows, GROUP), bf16), shaped((rows, PAIR), f32)],
        [
            pltpu.VMEM((width, own.shape[1]), bf16),
            pltpu.SemaphoreType.DMA((piece_count(shards),)),
        ],
        2 * rows * width * 3 * GROUP + 16 * rows * seq_len * PAIR * GROUP_HEADS,
        rows * (width + 6 * GROUP) * 2,
    )(place, lengths, x, bias, *pieces)


def split_low(value):
    high = value.astype(bf16).astype(f32)
    return high, value - high


def attend_back_kernel(
    shards,
    extra,
    place,
    lengths,
    x_ref,
    qkv_ref,
    context_ref,
    grad_ref,
    logsum_ref,
    *refs,
):
    if extra:
        before, refs = refs[:2], refs[2:]
    grads_ref, bias_ref, mine_ref, peer_ref, kept, total = refs
    step = pl.program_id(0)
    length = lengths[step]
    seq_len = qkv_ref.shape[0]
    lane = lanes(seq_len, PAIR)
    padded = rows_of(seq_len, PAIR) >= length
    for pair in range(GROUP_HEADS // 2):
        at = pair * PAIR
        queries = qkv_ref[:, at : at + PAIR].astype(f32) * SCALE
        keys = qkv_ref[:, GROUP + at : GROUP + at + PAIR].astype(f32)
        values = qkv_ref[:, 2 * GROUP + at : 2 * GROUP + at + PAIR].astype(f32)
        context = context_ref[:, at : at + PAIR].astype(f32)
        grad_low = grad_ref[:, at : at + PAIR]
        grad = grad_low.astype(f32)
        grad_context = grad * context
        grad_q, grad_k, grad_v = 0.0, [], []
        for head in range(2):
            own = (lane >= HEAD_DIM) == (head == 1)
            free = HEAD_DIM * (1 - head)
            first, second, third = lane == free, lane == free + 1, lane == free + 2
            logsum = logsum_ref[:, 2 * pair + head : 2 * pair + head + 1]
            delta = jnp.sum(jnp.where(own, grad_context, 0.0), axis=-1, keepdims=True)
            log_high, log_low = split_low(logsum)
            delta_high, delta_low = split_low(delta)
            one = jnp.where(first, 1.0, 0.0)
            other = jnp.where(second | third, 1.0, 0.0)
            low_lanes = jnp.where(second, -log_high, jnp.where(third, -log_low, one))
            q = jnp.where(own, queries, low_lanes).astype(bf16)
            k_lanes = jnp.where(padded, one * masked_score, 0.0) + other
            k = jnp.where(own, keys, k_lanes).astype(bf16)
            low_lanes = jnp.where(second, -delta_high, jnp.where(third, -delta_low, 0.0))
            g = jnp.where(own, grad, low_lanes).astype(bf16)
            v = jnp.where(own, values, other).astype(bf16)
            weights = jnp.exp(product_right_t(k, q))
            weights_low = weights.astype(bf16)
            grad_scores = (weights * product_right_t(v, g)).astype(bf16)
            grad_v.append(product(weights_low, grad_low))
            grad_k.append(product(grad_scores, q))
            only = jnp.where(own, keys, 0.0).astype(bf16)
            grad_q = grad_q + product_left_t(grad_scores, only)
        pieces = (
            grad_q * SCALE,
            jnp.where(lane < HEAD_DIM, grad_k[0], grad_k[1]),
            jnp.where(lane < HEAD_DIM, grad_v[0], grad_v[1]),
        )
        for which, piece in enumerate(pieces):
            columns = slice(which * GROUP + at, which * GROUP + at + PAIR)
            grads_ref[:, columns] = piece.astype(bf16)
    kept[pl.ds(pl.multiple_of(step * seq_len, 16), seq_len), :] = grads_ref[...]

    @pl.when(step == pl.num_programs(0) - 1)
    def _():
        grads = kept[...]
        sums = jnp.sum(grads.astype(f32), axis=0, keepdims=True)
        bias_ref[...] = jnp.broadcast_to(sums, bias_ref.shape)
        total[...] = product_left_t(x_ref[...], grads)
        rows = None
        if extra:
            all_sums = [ref[0:1, :] for ref in before] + [sums]
            row = rows_of(EXTRA, GROUP)
            rows = jnp.concatenate(
                [
                    jnp.where(
                        row == 0, one[:, :GROUP], jnp.where(row == 1, one[:, 2 * GROUP :], 0.0)
                    )
                    for one in all_sums
                ],
                axis=1,
            ).astype(bf16)
        store_pieces(place, total, mine_ref, peer_ref, rows)


def attend_back(place, lengths, x, qkv, context, grad, logsum, group, before, shards, seq_len):
    rows, width = x.shape
    half = width // (2 * shards) + (EXTRA if before else 0)
    piece = shaped((shards, half, 3 * GROUP), bf16)
    return kernel_call(
        partial(attend_back_kernel, shards, bool(before)),
        "attend_back",
        (rows // seq_len,),
        [
            whole_spec(rows, width),
            rows_spec(seq_len, 3 * GROUP),
            rows_spec(seq_len, GROUP),
            rows_spec(seq_len, GROUP, group),
            rows_spec(seq_len, PAIR),
        ]
        + [whole_spec(8, 3 * GROUP)] * len(before),
        [
            rows_spec(seq_len, 3 * GROUP),
            whole_spec(8, 3 * GROUP),
            whole_spec(*piece.shape),
            whole_spec(*piece.shape),
        ],
        [shaped((rows, 3 * GROUP), bf16), shaped((8, 3 * GROUP), f32), piece, piece],
        [pltpu.VMEM((rows, 3 * GROUP), bf16), pltpu.VMEM((width, 3 * GROUP), f32)],
        2 * rows * width * 3 * GROUP + 40 * rows * seq_len * PAIR * GROUP_HEADS,
        rows * (2 * width + 9 * GROUP) * 2,
    )(place, lengths, x, qkv, context, grad, logsum, *before)


def gelu_and_slope(u):
    size = jnp.abs(u)
    t = 1.0 / (1.0 + (0.3275911 * 0.7071067811865476) * size)
    bell = jnp.exp(-0.5 * u * u)
    poly = 0.5 * 1.061405429
    for factor in (-1.453152027, 1.421413741, -0.284496736, 0.254829592):
        poly = poly * t + 0.5 * factor
    tail = poly * t * bell
    share = jnp.where(u >= 0, 1.0 - tail, tail)
    return u * share, share + (u * 0.3989422804014327) * bell


def valid_rows(lengths, step, rows, seq_len):
    first = step * rows
    seq = first // seq_len
    at = rows_of(rows, 1) + (first - seq * seq_len)
    return (at < lengths[seq]).astype(f32)


def expand_kernel(shards, seq_len, place, lengths, x_ref, c0, c1, c2, small_ref, expand_b, *refs):
    count = piece_count(shards)
    out_pieces, expand_pieces, refs = refs[:count], refs[count : 2 * count], refs[2 * count :]
    normed_ref, inverse_ref, low_ref, active_ref, slope_ref, squares_ref = refs[:6]
    out_w, expand_w, sems = refs[6:]
    step = pl.program_id(0)
    width = x_ref.shape[1]

    @pl.when(step == 0)
    def _():
        load_pieces(
            place,
            (out_pieces, out_w, sems.at[0]),
            (expand_pieces, expand_w, sems.at[1]),
        )
        squares_ref[...] = jnp.zeros_like(squares_ref)

    rows = x_ref.shape[0]
    attended = small_ref[2:3, :]
    for group, ref in enumerate((c0, c1, c2)):
        attended = attended + product(ref[...], out_w[group * GROUP : (group + 1) * GROUP, :width])
    x = x_ref[...].astype(f32)
    valid = valid_rows(lengths, step, rows, seq_len)
    squares_ref[0:1, :] += jnp.sum(x * x * valid, axis=0, keepdims=True)
    squares_ref[1:2, :] += jnp.sum(attended * attended * valid, axis=0, keepdims=True)
    summed = x + attended
    center = summed - jnp.mean(summed, axis=-1, keepdims=True)
    inverse = lax.rsqrt(jnp.mean(center * center, axis=-1, keepdims=True) + norm_epsilon)
    normed = center * inverse
    normed_ref[...] = normed
    inverse_ref[...] = inverse
    low = (normed * small_ref[3:4, :] + small_ref[4:5, :]).astype(bf16)
    low_ref[...] = low
    for at in range(0, expand_w.shape[1], CHUNK):
        columns = slice(at, at + CHUNK)
        active, slope = gelu_and_slope(product(low, expand_w[:, columns]) + expand_b[0:1, columns])
        active_ref[:, columns] = active.astype(bf16)
        slope_ref[:, columns] = slope.astype(bf16)


def expand(place, lengths, x, contexts, small, expand_b, out_pieces, expand_pieces, shards, seq_len):
    rows, width = x.shape
    ff = expand_b.shape[1]
    return kernel_call(
        partial(expand_kernel, shards, seq_len),
        "expand",
        (rows // BLOCK,),
        [rows_spec(BLOCK, width)]
        + [rows_spec(BLOCK, GROUP)] * 3
        + [whole_spec(*small.shape), whole_spec(*expand_b.shape)]
        + anywhere(2 * piece_count(shards)),
        [
            rows_spec(BLOCK, width),
            rows_spec(BLOCK, 1),
            rows_spec(BLOCK, width),
            rows_spec(BLOCK, ff),
            rows_spec(BLOCK, ff),
            whole_spec(8, width),
        ],
        [
            shaped((rows, width), f32),
            shaped((rows, 1), f32),
            shaped((rows, width), bf16),
            shaped((rows, ff), bf16),
            shaped((rows, ff), bf16),
            shaped((8, width), f32),
        ],
        [
            pltpu.VMEM((width, out_pieces[0].shape[1]), bf16),
            pltpu.VMEM((width, ff), bf16),
            pltpu.SemaphoreType.DMA((2, piece_count(shards))),
        ],
        6 * rows * width * (width + ff),
        rows * (6 * width + 2 * ff) * 2,
    )(place, lengths, x, *contexts, small, expand_b, *out_pieces, *expand_pieces)


def contract_kernel(
    shards, seq_len, place, lengths, active_ref, slope_ref, normed_ref, small_ref, cotangent_ref, *refs
):
    count = piece_count(shards)
    contract_pieces, out_pieces, refs = refs[:count], refs[count : 2 * count], refs[2 * count :]
    embed_ref, sum_ref, low_ref, grad_ref, sums_ref, expand_sums, colbert_ref = refs[:7]
    contract_w, colbert_w, sems = refs[7:]
    step = pl.program_id(0)
    rows, width = normed_ref.shape
    out = colbert_w.shape[1]

    @pl.when(step == 0)
    def _():
        load_pieces(
            place,
            (contract_pieces, contract_w, sems.at[0]),
            (out_pieces, colbert_w, sems.at[1], pl.ds(width, out)),
        )
        sums_ref[...] = jnp.zeros_like(sums_ref)
        expand_sums[...] = jnp.zeros_like(expand_sums)
        colbert_ref[...] = jnp.zeros_like(colbert_ref)

    contracted = product(active_ref[...], contract_w[...]) + small_ref[5:6, :]
    valid = valid_rows(lengths, step, rows, seq_len)
    sums_ref[0:1, :] += jnp.sum(contracted * contracted * valid, axis=0, keepdims=True)
    hidden_one = normed_ref[...] * small_ref[3:4, :] + small_ref[4:5, :]
    summed = hidden_one + contracted
    center = summed - jnp.mean(summed, axis=-1, keepdims=True)
    inverse = lax.rsqrt(jnp.mean(center * center, axis=-1, keepdims=True) + norm_epsilon)
    normed = center * inverse
    gain = small_ref[6:7, :]
    hidden_low = (normed * gain + small_ref[7:8, :]).astype(bf16)
    projected = product(hidden_low, colbert_w[...])
    inverse_len = lax.rsqrt(jnp.sum(projected * projected, axis=-1, keepdims=True) + norm_epsilon)
    normalized = projected * inverse_len
    embed_ref[...] = (normalized * valid).astype(bf16)
    grad_norm = cotangent_ref[...].astype(f32) * valid
    grad_projected = (
        inverse_len
        * (grad_norm - normalized * jnp.sum(normalized * grad_norm, axis=-1, keepdims=True))
    ).astype(bf16)
    colbert_ref[...] += product_left_t(hidden_low, grad_projected)
    grad_hidden = product_right_t(grad_projected, colbert_w[...])
    sums_ref[1:2, :] += jnp.sum(grad_hidden * normed, axis=0, keepdims=True)
    sums_ref[2:3, :] += jnp.sum(grad_hidden, axis=0, keepdims=True)
    scaled = grad_hidden * gain
    grad_sum = inverse * (
        scaled
        - jnp.mean(scaled, axis=-1, keepdims=True)
        - normed * jnp.mean(scaled * normed, axis=-1, keepdims=True)
    )
    sum_ref[...] = grad_sum
    low = grad_sum.astype(bf16)
    low_ref[...] = low
    sums_ref[3:4, :] += jnp.sum(low.astype(f32), axis=0, keepdims=True)
    for at in range(0, contract_w.shape[0], CHUNK):
        columns = slice(at, at + CHUNK)
        grad = product_right_t(low, contract_w[columns, :]) * slope_ref[:, columns].astype(f32)
        grad = grad.astype(bf16)
        grad_ref[:, columns] = grad
        expand_sums[0:1, columns] += jnp.sum(grad.astype(f32), axis=0, keepdims=True)


def contract(
    place, lengths, active, slope, normed, small, cotangent, contract_pieces, out_pieces, shards, seq_len
):
    rows, width = normed.shape
    ff = active.shape[1]
    out = cotangent.shape[1]
    return kernel_call(
        partial(contract_kernel, shards, seq_len),
        "contract",
        (rows // BLOCK,),
        [
            rows_spec(BLOCK, ff),
            rows_spec(BLOCK, ff),
            rows_spec(BLOCK, width),
            whole_spec(*small.shape),
            rows_spec(BLOCK, out),
        ]
        + anywhere(2 * piece_count(shards)),
        [
            rows_spec(BLOCK, out),
            rows_spec(BLOCK, width),
            rows_spec(BLOCK, width),
            rows_spec(BLOCK, ff),
            whole_spec(8, width),
            whole_spec(8, ff),
            whole_spec(width, out),
        ],
        [
            shaped((rows, out), bf16),
            shaped((rows, width), f32),
            shaped((rows, width), bf16),
            shaped((rows, ff), bf16),
            shaped((8, width), f32),
            shaped((8, ff), f32),
            shaped((width, out), f32),
        ],
        [
            pltpu.VMEM((ff, width), bf16),
            pltpu.VMEM((width, out), bf16),
            pltpu.SemaphoreType.DMA((2, piece_count(shards))),
        ],
        4 * rows * width * (ff + 2 * out),
        rows * (6 * width + 3 * ff) * 2,
    )(place, lengths, active, slope, normed, small, cotangent, *contract_pieces, *out_pieces)


def contract_grad_kernel(shards, place, active_ref, grad_ref, mine_ref, peer_ref, total):
    step = pl.program_id(0)
    at = pl.multiple_of(step * CHUNK, CHUNK)
    total[pl.ds(at, CHUNK), :] = product_left_t(active_ref[...], grad_ref[...])

    @pl.when(step == pl.num_programs(0) - 1)
    def _():
        store_pieces(place, total, mine_ref, peer_ref)


def contract_grad(place, active, grad, shards):
    rows, ff = active.shape
    width = grad.shape[1]
    piece = shaped((shards, ff // (2 * shards), width), bf16)
    return kernel_call(
        partial(contract_grad_kernel, shards),
        "contract_grad",
        (ff // CHUNK,),
        [pl.BlockSpec((rows, CHUNK), lambda i, *_: (0, i)), whole_spec(rows, width)],
        [whole_spec(*piece.shape), whole_spec(*piece.shape)],
        [piece, piece],
        [pltpu.VMEM((ff, width), f32)],
        2 * rows * width * ff,
        (rows * (width + ff) + width * ff) * 2,
        prefetch=1,
    )(place, active, grad)


def expand_grad_kernel(shards, place, low_ref, grad_ref, mine_ref, peer_ref, total):
    total[...] = product_left_t(low_ref[...], grad_ref[...])
    store_pieces(place, total, mine_ref, peer_ref)


def expand_grad(place, low, grad, shards):
    rows, ff = grad.shape
    width = low.shape[1]
    half = width // (2 * shards)
    piece = shaped((shards, half, ff), bf16)
    spec = pl.BlockSpec((shards, half, CHUNK), lambda i, *_: (0, 0, i))
    return kernel_call(
        partial(expand_grad_kernel, shards),
        "expand_grad",
        (ff // CHUNK,),
        [whole_spec(rows, width), pl.BlockSpec((rows, CHUNK), lambda i, *_: (0, i))],
        [spec, spec],
        [piece, piece],
        [pltpu.VMEM((width, CHUNK), f32)],
        2 * rows * width * ff,
        (rows * (width + ff) + width * ff) * 2,
        prefetch=1,
    )(place, low, grad)


def attended_grad_kernel(
    shards,
    place,
    lengths,
    sum_ref,
    grad_ref,
    normed_ref,
    inverse_ref,
    small_ref,
    c0,
    c1,
    c2,
    squares_ref,
    sums_ref,
    expand_sums,
    colbert_ref,
    *refs,
):
    count = piece_count(shards)
    expand_pieces, out_pieces, refs = refs[:count], refs[count : 2 * count], refs[2 * count :]
    next_ref, context_ref, mine_ref, peer_ref = refs[:4]
    expand_w, out_w, own_sums, kept, total, sems = refs[4:]
    step = pl.program_id(0)
    rows, width = normed_ref.shape

    @pl.when(step == 0)
    def _():
        load_pieces(
            place,
            (expand_pieces, expand_w, sems.at[0]),
            (out_pieces, out_w, sems.at[1]),
        )
        own_sums[...] = jnp.zeros_like(own_sums)

    normed = normed_ref[...]
    grad_hidden = sum_ref[...] + product_right_t(grad_ref[...], expand_w[...])
    own_sums[1:2, :] += jnp.sum(grad_hidden * normed, axis=0, keepdims=True)
    own_sums[2:3, :] += jnp.sum(grad_hidden, axis=0, keepdims=True)
    scaled = grad_hidden * small_ref[3:4, :]
    grad_sum = inverse_ref[...] * (
        scaled
        - jnp.mean(scaled, axis=-1, keepdims=True)
        - normed * jnp.mean(scaled * normed, axis=-1, keepdims=True)
    )
    next_ref[...] = grad_sum
    low = grad_sum.astype(bf16)
    kept[pl.ds(pl.multiple_of(step * rows, 16), rows), :] = low
    own_sums[0:1, :] += jnp.sum(low.astype(f32), axis=0, keepdims=True)
    context_ref[...] = product_right_t(low, out_w[:, :width]).astype(bf16)

    @pl.when(step == pl.num_programs(0) - 1)
    def _():
        grads = kept[...]
        for group, ref in enumerate((c0, c1, c2)):
            total[group * GROUP : (group + 1) * GROUP, :width] = product_left_t(ref[...], grads)
        total[:, width:] = colbert_ref[...]
        positions = 0
        for seq in range(lengths.shape[0]):
            positions = positions + lengths[seq]
        row = rows_of(EXTRA, width)
        extra = jnp.zeros((EXTRA, width), f32) + positions.astype(f32)
        lines = [
            own_sums[0:1, :],
            own_sums[1:2, :],
            own_sums[2:3, :],
            sums_ref[3:4, :],
            sums_ref[1:2, :],
            sums_ref[2:3, :],
            squares_ref[0:1, :],
            squares_ref[1:2, :],
            sums_ref[0:1, :],
        ]
        lines += [expand_sums[0:1, at : at + width] for at in range(0, expand_sums.shape[1], width)]
        for at, line in enumerate(lines):
            extra = jnp.where(row == at, line, extra)
        blank = jnp.zeros((EXTRA, total.shape[1] - width), f32)
        extra = jnp.concatenate([extra, blank], axis=1).astype(bf16)
        store_pieces(place, total, mine_ref, peer_ref, extra)


def attended_grad(
    place,
    lengths,
    grad_sum,
    grad,
    normed,
    inverse,
    small,
    contexts,
    squares,
    sums,
    expand_sums,
    colbert,
    expand_pieces,
    out_pieces,
    shards,
):
    rows, width = normed.shape
    ff = grad.shape[1]
    out = colbert.shape[1]
    piece = shaped((shards, width // (2 * shards) + EXTRA, width + out), bf16)
    return kernel_call(
        partial(attended_grad_kernel, shards),
        "attended_grad",
        (rows // BLOCK,),
        [
            rows_spec(BLOCK, width),
            rows_spec(BLOCK, ff),
            rows_spec(BLOCK, width),
            rows_spec(BLOCK, 1),
            whole_spec(*small.shape),
        ]
        + [whole_spec(rows, GROUP)] * 3
        + [
            whole_spec(*squares.shape),
            whole_spec(*sums.shape),
            whole_spec(*expand_sums.shape),
            whole_spec(width, out),
        ]
        + anywhere(2 * piece_count(shards)),
        [
            rows_spec(BLOCK, width),
            rows_spec(BLOCK, width),
            whole_spec(*piece.shape),
            whole_spec(*piece.shape),
        ],
        [shaped((rows, width), f32), shaped((rows, width), bf16), piece, piece],
        [
            pltpu.VMEM((width, ff), bf16),
            pltpu.VMEM((width, width + out), bf16),
            pltpu.VMEM((8, width), f32),
            pltpu.VMEM((rows, width), bf16),
            pltpu.VMEM((width, width + out), f32),
            pltpu.SemaphoreType.DMA((2, piece_count(shards))),
        ],
        2 * rows * width * (ff + 2 * width),
        rows * (8 * width + ff) * 2,
    )(
        place,
        lengths,
        grad_sum,
        grad,
        normed,
        inverse,
        small,
        *contexts,
        squares,
        sums,
        expand_sums,
        colbert,
        *expand_pieces,
        *out_pieces,
    )


def tokens_grad_kernel(shards, place, sum_ref, g0, g1, g2, *refs):
    count = piece_count(shards)
    pieces, (out_ref, weight, sems) = refs[: 3 * count], refs[3 * count :]

    @pl.when(pl.program_id(0) == 0)
    def _():
        load_pieces(
            place,
            *[
                (pieces[group * count : (group + 1) * count], weight.at[group], sems.at[group])
                for group in range(3)
            ],
        )

    grad = sum_ref[...]
    for group, ref in enumerate((g0, g1, g2)):
        grad = grad + product_right_t(ref[...], weight[group])
    out_ref[...] = grad.astype(bf16)


def tokens_grad(place, grad_sum, grads, pieces, shards):
    rows, width = grad_sum.shape
    return kernel_call(
        partial(tokens_grad_kernel, shards),
        "tokens_grad",
        (rows // BLOCK,),
        [rows_spec(BLOCK, width)] + [rows_spec(BLOCK, 3 * GROUP)] * 3 + anywhere(3 * piece_count(shards)),
        rows_spec(BLOCK, width),
        shaped((rows, width), bf16),
        [
            pltpu.VMEM((3, width, 3 * GROUP), bf16),
            pltpu.SemaphoreType.DMA((3, piece_count(shards))),
        ],
        6 * rows * width * width,
        rows * 12 * width,
        prefetch=1,
    )(place, grad_sum, *grads, *[piece for one in pieces for piece in one])


def block_sum_kernel(keep_ref, *refs):
    kept, sent, keep_ref, other_ref, out_refs = keep_ref[0], keep_ref[1], refs[0], refs[1], refs[2:]
    for ref, blocks in zip(out_refs, (kept, sent)):
        for at, block in enumerate(blocks):
            ref[at] = (keep_ref[block].astype(f32) + other_ref[block].astype(f32)).astype(bf16)


def block_sum(one, other, kept, sent):
    shards, half, width = one.shape
    columns = 768 if width % 768 == 0 else width

    def spec(count):
        return pl.BlockSpec((count, half, columns), lambda i: (0, 0, i))

    counts = [len(blocks) for blocks in (kept, sent) if blocks]
    return kernel_call(
        partial(block_sum_kernel, (kept, sent)),
        "block_sum",
        (width // columns,),
        [spec(shards), spec(shards)],
        [spec(count) for count in counts],
        [shaped((count, half, width), bf16) for count in counts],
        [],
        one.size,
        one.size * 6,
        prefetch=0,
    )(one, other)


def low_sum(one, other):
    return (one.astype(f32) + other.astype(f32)).astype(bf16)


def reduction(mine, peer, order, halved):
    replicas = lax.axis_size("replica")
    held = mine
    hold = yield peer
    other = after(lax.ppermute(peer, "replica", replica_partners(1)), hold)
    distances = list(range(held.shape[0]))
    for bit in order:
        kept = [i for i, d in enumerate(distances) if not d & bit]
        sent = [i for i, d in enumerate(distances) if d & bit]
        held, given = block_sum(held, other, kept, sent)
        distances = [distances[i] for i in kept]
        hold = yield given
        other = after(lax.ppermute(given, "shard", shard_partners(bit)), hold)
    low = low_sum(held[0], other[0])
    at = lax.axis_index("replica")
    bits = []
    distance = 2
    while distance < replicas:
        bits.append(distance)
        distance *= 2
    if not halved:
        for bit in bits:
            hold = yield low
            low = low_sum(low, after(lax.ppermute(low, "replica", replica_partners(bit)), hold))
    else:
        for bit in bits:
            half = low.shape[1] // 2
            upper = ((at & bit) != 0).astype(jnp.int32)
            given = lax.dynamic_slice_in_dim(low, (1 - upper) * half, half, 1)
            low = lax.dynamic_slice_in_dim(low, upper * half, half, 1)
            hold = yield given
            low = low_sum(low, after(lax.ppermute(given, "replica", replica_partners(bit)), hold))
        for bit in reversed(bits):
            hold = yield low
            other = after(lax.ppermute(low, "replica", replica_partners(bit)), hold)
            upper = (at & bit) != 0
            low = jnp.concatenate(
                [jnp.where(upper, other, low), jnp.where(upper, low, other)], axis=1
            )
    hold = yield low
    yield (low, after(lax.ppermute(low, "replica", replica_partners(1)), hold))


def in_order(core, low, other, half):
    low, other = low[:half], other[:half]
    first = jnp.where(core == 0, low, other)
    second = jnp.where(core == 0, other, low)
    return jnp.concatenate([first, second]).astype(f32)


def by_shard(parts):
    mine = lax.axis_index("shard")
    shards = len(parts)
    distance = 1
    while distance < shards:
        swap = (mine & distance) != 0
        parts = [jnp.where(swap, parts[i ^ distance], parts[i]) for i in range(shards)]
        distance *= 2
    return jnp.stack(parts, axis=1)


def per_device(
    tokens,
    lengths,
    w_query,
    b_query,
    w_key,
    w_value,
    b_value,
    w_attn_out,
    b_attn_out,
    gain_one,
    shift_one,
    w_expand,
    b_expand,
    w_contract,
    b_contract,
    gain_two,
    shift_two,
    w_colbert,
    cotangent,
):
    seq_count, seq_len, width = tokens.shape
    rows = seq_count * seq_len
    shards = lax.axis_size("shard")
    part = width // shards
    half = part // 2
    mine = lax.axis_index("shard")
    core = lax.axis_index("replica") % 2
    ff = b_expand.shape[0] * shards
    out = w_colbert.shape[1]
    groups = width // GROUP
    place = jnp.stack([mine, core]).astype(jnp.int32)
    x = tokens.reshape(rows, width)

    small = jnp.stack(
        [b_query, b_value, b_attn_out, gain_one, shift_one, b_contract, gain_two, shift_two]
        + [b_expand[i * part : (i + 1) * part] for i in range(ff // width)]
    )
    lines = small.shape[0]

    def core_half(own):
        rows = own.shape[0] // 2
        return lax.dynamic_slice_in_dim(own, core * rows, rows, 0)

    bits = shard_bits()
    own_attn, attn_gather = [], []
    for group in range(groups):
        columns = slice(group * GROUP, (group + 1) * GROUP)
        own = jnp.concatenate([w_query[:, columns], w_key[:, columns], w_value[:, columns]], axis=1)
        own_attn.append(own)
        sent = core_half(own)
        if group == 0:
            flat = jnp.pad(small.reshape(-1), (0, EXTRA * 3 * GROUP - small.size))
            sent = jnp.concatenate([sent, flat.reshape(EXTRA, 3 * GROUP)])
        attn_gather.append(Gather(own, sent, bits[::-1] if group % 2 else bits))
    own_out = jnp.concatenate([w_attn_out, w_colbert], axis=1)
    out_gather = Gather(own_out, core_half(own_out), bits[::-1])
    expand_gather = Gather(w_expand, core_half(w_expand), bits)
    contract_gather = Gather(w_contract, core_half(w_contract), bits[::-1])

    first_gather = attn_gather[0]
    first_gather.start()
    early = first_gather.first()
    for gather in attn_gather[1:]:
        gather.start(early)
    first_gather.relay()
    early = attn_gather[1].first()
    for gather in (out_gather, expand_gather):
        gather.start(early)
    attn_gather[1].relay()
    first_gather.swap()
    parts = [small] + [
        first_gather.near[d][half:].reshape(-1)[: lines * part].reshape(lines, part)
        for d in range(1, shards)
    ]
    small = by_shard(parts).astype(f32)
    expand_b = jnp.broadcast_to(jnp.swapaxes(small[8:], 0, 1).reshape(1, ff), (8, ff))
    small = small[:8].reshape(8, width)

    qkvs, contexts, logsums = [], [], []
    for group in range(groups):
        columns = slice(group * GROUP, (group + 1) * GROUP)
        bias = jnp.concatenate(
            [small[0:1, columns], jnp.zeros((1, GROUP), f32), small[1:2, columns]], axis=1
        )
        bias = jnp.broadcast_to(bias, (8, 3 * GROUP))
        earlier = [expand_gather.near[0]]
        if group + 1 < groups:
            earlier.append(attn_gather[group + 1].first())
        qkv, context, logsum = attend(
            place, lengths, after(x, *earlier), bias, attn_gather[group].pieces(), shards, seq_len
        )
        hold = logsum
        if group + 1 < groups:
            if group + 2 < groups:
                attn_gather[group + 2].relay(hold)
            attn_gather[group + 1].swap(hold)
        if group == 0:
            out_gather.relay(hold)
            contract_gather.start(hold)
        if group == 1:
            expand_gather.relay(hold)
        if group == groups - 1:
            out_gather.swap(hold)
            expand_gather.swap(hold)
            contract_gather.relay(hold)
        qkvs.append(qkv)
        contexts.append(context)
        logsums.append(logsum)
    out_pieces = out_gather.pieces()
    expand_pieces = expand_gather.pieces()
    normed, inverse, hidden_low, active, slope, squares = expand(
        place, lengths, x, contexts, small, expand_b, out_pieces, expand_pieces, shards, seq_len
    )
    contract_gather.swap(squares)
    contract_pieces = contract_gather.pieces()
    embeddings, grad_sum, grad_contracted, grad_expanded, sums, expand_sums, colbert = contract(
        place,
        lengths,
        active,
        slope,
        normed,
        small,
        cotangent.reshape(rows, out),
        contract_pieces,
        out_pieces,
        shards,
        seq_len,
    )
    running, finals = {}, {}

    def advance(hold, *names):
        sent = []
        for name in names:
            value = running[name].send(hold)
            if isinstance(value, tuple):
                finals[name] = value
            else:
                sent.append(value)
        return sent

    pieces = contract_grad(place, active, grad_contracted, shards)
    running["contract"] = reduction(*pieces, bits, True)
    sent = [next(running["contract"])]
    pieces = expand_grad(place, after(hidden_low, sent), grad_expanded, shards)
    running["expand"] = reduction(*pieces, bits[::-1], True)
    sent = [next(running["expand"])] + advance(pieces, "contract")
    grad_sum, grad_context, *pieces = attended_grad(
        place,
        lengths,
        after(grad_sum, sent),
        grad_expanded,
        normed,
        inverse,
        small,
        contexts,
        squares,
        sums,
        expand_sums,
        colbert,
        expand_pieces,
        out_pieces,
        shards,
    )
    running["out"] = reduction(*pieces, bits, False)
    sent = [next(running["out"])] + advance(grad_context, "expand")
    grads, biases = [], []
    plan = (("contract", "out"), ("contract", "expand", "out", 0), ("contract", "expand", "out", 0, 1))
    for group in range(groups):
        grad, bias, *pieces = attend_back(
            place,
            lengths,
            x,
            qkvs[group],
            contexts[group],
            after(grad_context, sent),
            logsums[group],
            group,
            biases if group == groups - 1 else [],
            shards,
            seq_len,
        )
        grads.append(grad)
        biases.append(bias)
        running[group] = reduction(*pieces, bits[::-1] if group % 2 else bits, False)
        sent = [next(running[group])] + advance(bias, *plan[group])
    grad_tokens = tokens_grad(
        place,
        after(grad_sum, sent),
        grads,
        [gather.pieces() for gather in attn_gather],
        shards,
    )
    while len(finals) < len(running):
        advance(grad_tokens, *[name for name in running if name not in finals])
    r_contract, r_expand, r_out = finals["contract"], finals["expand"], finals["out"]
    r_attn = [finals[group] for group in range(groups)]

    def own(vector):
        size = vector.shape[0] // shards
        return lax.dynamic_slice_in_dim(vector, mine * size, size, 0)

    extra = r_out[0][half:, :width].astype(f32)
    r_bo, r_ga, r_sa, r_bc, r_gb, r_sb = [own(extra[i]) for i in range(6)]
    lines = 9 + ff // width
    r_be = own(extra[9:lines].reshape(ff))
    count = extra[lines, 0]
    rms_values = jnp.sqrt(jnp.sum(extra[6:9], axis=1) / (count * width))
    extra = r_attn[-1][0][half:].astype(f32)
    r_bq, r_bv = own(extra[0]), own(extra[1])
    r_attn = [in_order(core, *one, half) for one in r_attn]
    r_wq, r_wk, r_wv = [
        jnp.concatenate([one[:, i * GROUP : (i + 1) * GROUP] for one in r_attn], axis=1)
        for i in range(3)
    ]
    r_out = in_order(core, *r_out, half)
    r_we = in_order(core, *r_expand, half)
    r_wc = in_order(core, *r_contract, w_contract.shape[0] // 2)
    return (
        embeddings.reshape(seq_count, seq_len, out),
        grad_tokens.reshape(seq_count, seq_len, width),
        r_wq,
        r_bq,
        r_wk,
        r_wv,
        r_bv,
        r_out[:, :width],
        r_bo,
        r_ga,
        r_sa,
        r_we,
        r_be,
        r_wc,
        r_bc,
        r_gb,
        r_sb,
        r_out[:, width:],
        rms_values,
    )


def solution(mesh):
    rows = P(("replica", "shard"), None, None)
    matrix, vector = P("shard", None), P("shard")
    weights = (
        matrix,
        vector,
        matrix,
        matrix,
        vector,
        matrix,
        vector,
        vector,
        vector,
        matrix,
        vector,
        matrix,
        vector,
        vector,
        vector,
        matrix,
    )
    return jax.shard_map(
        per_device,
        mesh=mesh,
        in_specs=(rows, P(("replica", "shard")), *weights, rows),
        out_specs=(rows, rows, *weights, P()),
        check_vma=False,
    )
```

```python
from functools import partial

import jax
import jax.numpy as jnp
from jax import lax
from jax.experimental import pallas as pl
from jax.experimental.pallas import tpu as pltpu
from jax.sharding import PartitionSpec as P

HEADS = 12
HEAD_DIM = 64
GROUP_HEADS = 4
GROUP = GROUP_HEADS * HEAD_DIM
PAIR = 2 * HEAD_DIM
EXTRA = 16
BLOCK = 256
CHUNK = 512
SCALE = HEAD_DIM**-0.5
VMEM_LIMIT = 52 * 1024 * 1024

norm_epsilon = 1e-12
masked_score = -1e30
f32 = jnp.float32
bf16 = jnp.bfloat16


def product(left, right):
    return jnp.dot(left, right, preferred_element_type=f32)


def product_left_t(left, right):
    return lax.dot_general(left, right, (((0,), (0,)), ((), ())), preferred_element_type=f32)


def product_right_t(left, right):
    return lax.dot_general(left, right, (((1,), (1,)), ((), ())), preferred_element_type=f32)


def shard_partners(distance):
    return [(i, i ^ distance) for i in range(lax.axis_size("shard"))]


def replica_partners(distance):
    return [(i, i ^ distance) for i in range(lax.axis_size("replica"))]


def after(value, *earlier):
    return lax.optimization_barrier((value, *jax.tree.leaves(earlier)))[0]


def shard_bits():
    distance, bits = 1, []
    while distance < lax.axis_size("shard"):
        bits.append(distance)
        distance *= 2
    return bits


def gather_halves(sent):
    return lax.all_gather(sent, "shard", axis=0)


def other_halves(near):
    return near, lax.ppermute(near, "replica", replica_partners(1))


def halves_copies(core, near, far, columns, target, sems):
    shards, half = near.shape[:2]
    copies = []
    for shard in range(shards):
        for ref, which in ((near, core), (far, 1 - core)):
            rows = pl.ds(pl.multiple_of((2 * shard + which) * half, 16), half)
            copies.append(
                pltpu.make_async_copy(
                    ref.at[shard, :, columns], target.at[rows], sems.at[len(copies)]
                )
            )
    return copies


class Gather:
    def __init__(self, own, sent, order=None):
        self.own = own
        self.sent = sent
        self.order = order
        self.near = {}
        self.far = {}

    def start(self, *earlier):
        sent = after(self.sent, *earlier)
        distances = self.order or range(1, lax.axis_size("shard"))
        for d in distances:
            self.near[d] = lax.ppermute(sent, "shard", shard_partners(d))

    def relay(self, *earlier):
        known = [self.order[0]]
        for distance in self.order[1:]:
            for d in known:
                piece = after(self.near[d], *earlier)
                self.near[d | distance] = lax.ppermute(piece, "shard", shard_partners(distance))
            known += [distance] + [d | distance for d in known]

    def swap(self, *earlier, distances=None):
        for d in distances or [d for d in self.near if d not in self.far]:
            piece = after(self.near[d], *earlier)
            self.far[d] = lax.ppermute(piece, "replica", replica_partners(1))

    def pieces(self):
        distances = range(1, lax.axis_size("shard"))
        return (*self.own, *[self.near[d] for d in distances], *[self.far[d] for d in distances])


def piece_count(shards, own):
    return own + 2 * (shards - 1)


def piece_copies(place, pieces, own, target, sems, first=0):
    mine, core = place[0], place[1]
    near = pieces[len(own) :]
    shards = len(near) // 2 + 1
    rows = pieces[0].shape[0]
    half = rows // 2
    copies = []

    def add(source, target):
        copies.append(pltpu.make_async_copy(source, target, sems.at[len(copies)]))

    place_at = 0
    for ref, columns in zip(pieces, own):
        at, width = columns or (0, ref.shape[1])
        if width != ref.shape[1]:
            ref = ref.at[:, pl.ds(at, width)]
        start = pl.multiple_of(mine * rows, 16)
        add(ref, target.at[pl.ds(start, rows), pl.ds(place_at, width)])
        place_at += width
    for d in range(1, shards):
        start = (mine ^ d) * rows
        for ref, which in ((near[d - 1], core), (near[shards + d - 2], 1 - core)):
            if ref.shape != (half, place_at):
                ref = ref.at[pl.ds(0, half), pl.ds(first, place_at)]
            add(ref, target.at[pl.ds(pl.multiple_of(start + which * half, 16), half)])
    return copies


def load_all(copies):
    for copy in copies:
        copy.start()
    for copy in copies:
        copy.wait()


def load_pieces(place, *sets):
    load_all([copy for one in sets for copy in piece_copies(place, *one)])


def store_pieces(mine, core, total, mine_ref, peer_ref, extra=None):
    shards = mine_ref.shape[0]
    half = total.shape[0] // (2 * shards)
    for d in range(shards):
        start = (mine ^ d) * 2
        for ref, which in ((mine_ref, core), (peer_ref, 1 - core)):
            at = pl.multiple_of((start + which) * half, 8)
            ref[d, 0:half] = total[pl.ds(at, half), :].astype(bf16)
            if extra is not None:
                ref[d, half:] = extra


def kernel_call(body, name, grid, in_specs, out_specs, out_shape, scratch, flops, moved, prefetch=2):
    return pl.pallas_call(
        body,
        name=name,
        grid_spec=pltpu.PrefetchScalarGridSpec(
            num_scalar_prefetch=prefetch,
            grid=grid,
            in_specs=in_specs,
            out_specs=out_specs,
            scratch_shapes=scratch,
        ),
        out_shape=out_shape,
        compiler_params=pltpu.CompilerParams(
            dimension_semantics=("arbitrary",) * len(grid), vmem_limit_bytes=VMEM_LIMIT
        ),
        cost_estimate=pl.CostEstimate(flops=flops, bytes_accessed=moved, transcendentals=0),
    )


def anywhere(count):
    return [pl.BlockSpec(memory_space=pl.ANY)] * count


def rows_spec(rows, width, column=0):
    return pl.BlockSpec((rows, width), lambda i, *_: (i, column))


def whole_spec(*shape):
    return pl.BlockSpec(shape, lambda *_: (0,) * len(shape))


def shaped(shape, dtype):
    return jax.ShapeDtypeStruct(shape, dtype)


def lanes(rows, width):
    return lax.broadcasted_iota(jnp.int32, (rows, width), 1)


def rows_of(rows, width):
    return lax.broadcasted_iota(jnp.int32, (rows, width), 0)


def attend_kernel(shards, group, place, lengths, x_ref, bias_ref, *refs):
    count = piece_count(shards, 3)
    pieces, (qkv_ref, context_ref, logsum_ref, weight, sems) = refs[:count], refs[count:]
    step = pl.program_id(0)

    @pl.when(step == 0)
    def _():
        first = max(group - 1, 0) * 3 * GROUP
        load_pieces(place, (pieces, [(group * GROUP, GROUP)] * 3, weight, sems, first))

    length = lengths[step]
    seq_len = x_ref.shape[0]
    columns = slice(group * GROUP, (group + 1) * GROUP)
    no_bias = jnp.zeros((1, GROUP), f32)
    bias = jnp.concatenate([bias_ref[0:1, columns], no_bias, bias_ref[1:2, columns]], axis=1)
    qkv = (product(x_ref[...], weight[...]) + bias).astype(bf16)
    qkv_ref[...] = qkv
    lane = lanes(seq_len, PAIR)
    padded = rows_of(seq_len, PAIR) >= length
    logsums = jnp.zeros((seq_len, PAIR), f32)
    for pair in range(GROUP_HEADS // 2):
        at = pair * PAIR
        queries = qkv[:, at : at + PAIR].astype(f32) * SCALE
        keys = qkv[:, GROUP + at : GROUP + at + PAIR].astype(f32)
        values = qkv[:, 2 * GROUP + at : 2 * GROUP + at + PAIR].astype(f32)
        halves = []
        for head in range(2):
            own = (lane >= HEAD_DIM) == (head == 1)
            free = HEAD_DIM * (1 - head)
            one = jnp.where(lane == free, 1.0, 0.0)
            q = jnp.where(own, queries, one).astype(bf16)
            k = jnp.where(own, keys, jnp.where(padded, one * masked_score, 0.0)).astype(bf16)
            v = jnp.where(own, values, one).astype(bf16)
            scores = product_right_t(q, k)
            highest = jnp.max(scores, axis=-1, keepdims=True)
            exponent = jnp.exp(scores - highest).astype(bf16)
            summed = product(exponent, v)
            totals = summed[:, free : free + 1]
            halves.append(summed * (1.0 / totals))
            logsums = jnp.where(lane == 2 * pair + head, highest + jnp.log(totals), logsums)
        context = jnp.where(lane < HEAD_DIM, halves[0], halves[1])
        context_ref[:, at : at + PAIR] = context.astype(bf16)
    logsum_ref[...] = logsums


def attend(place, lengths, x, bias, pieces, group, shards, seq_len):
    rows, width = x.shape
    return kernel_call(
        partial(attend_kernel, shards, group),
        "attend",
        (rows // seq_len,),
        [rows_spec(seq_len, width), whole_spec(8, width)] + anywhere(len(pieces)),
        [rows_spec(seq_len, 3 * GROUP), rows_spec(seq_len, GROUP), rows_spec(seq_len, PAIR)],
        [shaped((rows, 3 * GROUP), bf16), shaped((rows, GROUP), bf16), shaped((rows, PAIR), f32)],
        [
            pltpu.VMEM((width, 3 * GROUP), bf16),
            pltpu.SemaphoreType.DMA((piece_count(shards, 3),)),
        ],
        2 * rows * width * 3 * GROUP + 16 * rows * seq_len * PAIR * GROUP_HEADS,
        rows * (width + 6 * GROUP) * 2,
    )(place, lengths, x, bias, *pieces)


def split_low(value):
    high = value.astype(bf16).astype(f32)
    return high, value - high


def query_value_lines(before, sums):
    row = rows_of(EXTRA, GROUP)
    parts = [
        jnp.where(row == 0, one[:, :GROUP], jnp.where(row == 1, one[:, 2 * GROUP :], 0.0))
        for one in [ref[0:1, :] for ref in before] + [sums]
    ]
    return jnp.concatenate(parts, axis=1)


def vector_lines(lengths, own_sums, sums, squares, expand_sums, columns):
    width = own_sums.shape[1]
    positions = 0
    for seq in range(lengths.shape[0]):
        positions = positions + lengths[seq]
    lines = [own_sums[at : at + 1, :] for at in (0, 1, 2)]
    lines += [sums[at : at + 1, :] for at in (3, 1, 2)]
    lines += [squares[0:1, :], squares[1:2, :], sums[0:1, :]]
    lines += [expand_sums[0:1, at : at + width] for at in range(0, expand_sums.shape[1], width)]
    row = rows_of(EXTRA, width)
    extra = jnp.zeros((EXTRA, width), f32) + positions.astype(f32)
    for at, line in enumerate(lines):
        extra = jnp.where(row == at, line, extra)
    return jnp.concatenate([extra, jnp.zeros((EXTRA, columns - width), f32)], axis=1)


def attend_back_kernel(
    shards,
    before_count,
    with_out,
    place,
    lengths,
    x_ref,
    qkv_ref,
    context_ref,
    grad_ref,
    logsum_ref,
    *refs,
):
    before, refs = refs[:before_count], refs[before_count:]
    if with_out:
        (contexts, grad_low_ref, own_sums, sums_ref, squares, expand_sums, colbert), refs = (
            (refs[:3], *refs[3:9]),
            refs[9:],
        )
    grads_ref, bias_ref, mine_ref, peer_ref, kept, total = refs
    step = pl.program_id(0)
    length = lengths[step]
    seq_len = qkv_ref.shape[0]
    lane = lanes(seq_len, PAIR)
    padded = rows_of(seq_len, PAIR) >= length
    for pair in range(GROUP_HEADS // 2):
        at = pair * PAIR
        queries = qkv_ref[:, at : at + PAIR].astype(f32) * SCALE
        keys = qkv_ref[:, GROUP + at : GROUP + at + PAIR].astype(f32)
        values = qkv_ref[:, 2 * GROUP + at : 2 * GROUP + at + PAIR].astype(f32)
        context = context_ref[:, at : at + PAIR].astype(f32)
        grad_low = grad_ref[:, at : at + PAIR]
        grad = grad_low.astype(f32)
        grad_context = grad * context
        grad_q, grad_k, grad_v = 0.0, [], []
        for head in range(2):
            own = (lane >= HEAD_DIM) == (head == 1)
            free = HEAD_DIM * (1 - head)
            first, second, third = lane == free, lane == free + 1, lane == free + 2
            logsum = logsum_ref[:, 2 * pair + head : 2 * pair + head + 1]
            delta = jnp.sum(jnp.where(own, grad_context, 0.0), axis=-1, keepdims=True)
            log_high, log_low = split_low(logsum)
            delta_high, delta_low = split_low(delta)
            one = jnp.where(first, 1.0, 0.0)
            other = jnp.where(second | third, 1.0, 0.0)
            low_lanes = jnp.where(second, -log_high, jnp.where(third, -log_low, one))
            q = jnp.where(own, queries, low_lanes).astype(bf16)
            k_lanes = jnp.where(padded, one * masked_score, 0.0) + other
            k = jnp.where(own, keys, k_lanes).astype(bf16)
            low_lanes = jnp.where(second, -delta_high, jnp.where(third, -delta_low, 0.0))
            g = jnp.where(own, grad, low_lanes).astype(bf16)
            v = jnp.where(own, values, other).astype(bf16)
            weights = jnp.exp(product_right_t(k, q))
            weights_low = weights.astype(bf16)
            grad_scores = (weights * product_right_t(v, g)).astype(bf16)
            grad_v.append(product(weights_low, grad_low))
            grad_k.append(product(grad_scores, q))
            only = jnp.where(own, keys, 0.0).astype(bf16)
            grad_q = grad_q + product_left_t(grad_scores, only)
        pieces = (
            grad_q * SCALE,
            jnp.where(lane < HEAD_DIM, grad_k[0], grad_k[1]),
            jnp.where(lane < HEAD_DIM, grad_v[0], grad_v[1]),
        )
        for which, piece in enumerate(pieces):
            columns = slice(which * GROUP + at, which * GROUP + at + PAIR)
            grads_ref[:, columns] = piece.astype(bf16)
    kept[pl.ds(pl.multiple_of(step * seq_len, 16), seq_len), :] = grads_ref[...]

    @pl.when(step == pl.num_programs(0) - 1)
    def _():
        grads = kept[...]
        sums = jnp.sum(grads.astype(f32), axis=0, keepdims=True)
        bias_ref[...] = jnp.broadcast_to(sums, bias_ref.shape)
        width = x_ref.shape[1]
        total[:, : 3 * GROUP] = product_left_t(x_ref[...], grads)
        extra = None
        if with_out:
            at = 3 * GROUP
            for group, ref in enumerate(contexts):
                total[group * GROUP : (group + 1) * GROUP, at : at + width] = product_left_t(
                    ref[...], grad_low_ref[...]
                )
            total[:, at + width :] = colbert[...]
            extra = vector_lines(
                lengths, own_sums, sums_ref, squares, expand_sums, total.shape[1]
            ).astype(bf16)
        elif before_count:
            extra = query_value_lines(before, sums).astype(bf16)
        store_pieces(place[0], place[1], total, mine_ref, peer_ref, extra)


def attend_back(
    place, lengths, x, qkv, context, grad, logsum, group, before, with_out, shards, seq_len
):
    rows, width = x.shape
    half = width // (2 * shards) + (EXTRA if before or with_out else 0)
    columns = 3 * GROUP + (width + with_out[-1].shape[1] if with_out else 0)
    piece = shaped((shards, half, columns), bf16)
    return kernel_call(
        partial(attend_back_kernel, shards, len(before), bool(with_out)),
        "attend_back",
        (rows // seq_len,),
        [
            whole_spec(rows, width),
            rows_spec(seq_len, 3 * GROUP),
            rows_spec(seq_len, GROUP),
            rows_spec(seq_len, GROUP, group),
            rows_spec(seq_len, PAIR),
        ]
        + [whole_spec(*one.shape) for one in (*before, *with_out)],
        [
            rows_spec(seq_len, 3 * GROUP),
            whole_spec(8, 3 * GROUP),
            whole_spec(*piece.shape),
            whole_spec(*piece.shape),
        ],
        [shaped((rows, 3 * GROUP), bf16), shaped((8, 3 * GROUP), f32), piece, piece],
        [pltpu.VMEM((rows, 3 * GROUP), bf16), pltpu.VMEM((width, columns), f32)],
        2 * rows * width * columns + 40 * rows * seq_len * PAIR * GROUP_HEADS,
        rows * (2 * width + 9 * GROUP) * 2,
    )(place, lengths, x, qkv, context, grad, logsum, *before, *with_out)


def gelu_and_slope(u):
    share = 0.5 * lax.erf(u * 0.7071067811865476) + 0.5
    return u * share, share + (u * 0.3989422804014327) * jnp.exp(-0.5 * (u * u))


def valid_rows(lengths, step, rows, seq_len):
    first = step * rows
    seq = first // seq_len
    at = rows_of(rows, 1) + (first - seq * seq_len)
    return (at < lengths[seq]).astype(f32)


def out_expand_copies(place, near, far, out_w, expand_w, sems):
    width, ff = out_w.shape[1], expand_w.shape[1]
    first = near.shape[2] - ff
    copies = halves_copies(place[1], near, far, pl.ds(0, width), out_w, sems.at[0])
    return copies + halves_copies(place[1], near, far, pl.ds(first, ff), expand_w, sems.at[1])


def expand_kernel(shards, seq_len, place, lengths, x_ref, c0, c1, c2, small_ref, expand_b, *refs):
    near, far, refs = refs[0], refs[1], refs[2:]
    normed_ref, inverse_ref, low_ref, active_ref, slope_ref, squares_ref = refs[:6]
    out_w, expand_w, sems = refs[6:]
    step = pl.program_id(0)
    width = x_ref.shape[1]

    @pl.when(step == 0)
    def _():
        load_all(out_expand_copies(place, near, far, out_w, expand_w, sems))
        squares_ref[...] = jnp.zeros_like(squares_ref)

    rows = x_ref.shape[0]
    attended = small_ref[2:3, :]
    for group, ref in enumerate((c0, c1, c2)):
        attended = attended + product(ref[...], out_w[group * GROUP : (group + 1) * GROUP, :])
    x = x_ref[...].astype(f32)
    valid = valid_rows(lengths, step, rows, seq_len)
    squares_ref[0:1, :] += jnp.sum(x * x * valid, axis=0, keepdims=True)
    squares_ref[1:2, :] += jnp.sum(attended * attended * valid, axis=0, keepdims=True)
    summed = x + attended
    center = summed - jnp.mean(summed, axis=-1, keepdims=True)
    inverse = lax.rsqrt(jnp.mean(center * center, axis=-1, keepdims=True) + norm_epsilon)
    normed = center * inverse
    normed_ref[...] = normed
    inverse_ref[...] = inverse
    low = (normed * small_ref[3:4, :] + small_ref[4:5, :]).astype(bf16)
    low_ref[...] = low
    for at in range(0, expand_w.shape[1], CHUNK):
        columns = slice(at, at + CHUNK)
        active, slope = gelu_and_slope(product(low, expand_w[:, columns]) + expand_b[0:1, columns])
        active_ref[:, columns] = active.astype(bf16)
        slope_ref[:, columns] = slope.astype(bf16)


def expand(place, lengths, x, contexts, small, expand_b, halves, shards, seq_len):
    rows, width = x.shape
    ff = expand_b.shape[1]
    return kernel_call(
        partial(expand_kernel, shards, seq_len),
        "expand",
        (rows // BLOCK,),
        [rows_spec(BLOCK, width)]
        + [rows_spec(BLOCK, GROUP)] * 3
        + [whole_spec(*small.shape), whole_spec(*expand_b.shape)]
        + anywhere(len(halves)),
        [
            rows_spec(BLOCK, width),
            rows_spec(BLOCK, 1),
            rows_spec(BLOCK, width),
            rows_spec(BLOCK, ff),
            rows_spec(BLOCK, ff),
            whole_spec(8, width),
        ],
        [
            shaped((rows, width), f32),
            shaped((rows, 1), f32),
            shaped((rows, width), bf16),
            shaped((rows, ff), bf16),
            shaped((rows, ff), bf16),
            shaped((8, width), f32),
        ],
        [
            pltpu.VMEM((width, width), bf16),
            pltpu.VMEM((width, ff), bf16),
            pltpu.SemaphoreType.DMA((2, 2 * shards)),
        ],
        6 * rows * width * (width + ff),
        rows * (6 * width + 2 * ff) * 2,
    )(place, lengths, x, *contexts, small, expand_b, *halves)


def contract_kernel(
    shards, seq_len, place, lengths, active_ref, slope_ref, normed_ref, small_ref, cotangent_ref, *refs
):
    near, far = refs[:2]
    count = piece_count(shards, 1)
    pieces, refs = refs[2 : 2 + count], refs[2 + count :]
    embed_ref, sum_ref, low_ref, grad_ref, sums_ref, colbert_ref = refs[:6]
    contract_w, colbert_w, sems = refs[6:]
    step = pl.program_id(0)
    rows, width = normed_ref.shape
    out = colbert_w.shape[1]

    @pl.when(step == 0)
    def _():
        copies = piece_copies(place, pieces, [None], contract_w, sems.at[0])
        columns = pl.ds(width, out)
        load_all(copies + halves_copies(place[1], near, far, columns, colbert_w, sems.at[1]))
        sums_ref[...] = jnp.zeros_like(sums_ref)
        colbert_ref[...] = jnp.zeros_like(colbert_ref)

    gain_one, shift_one, bias = small_ref[3:4, :], small_ref[4:5, :], small_ref[5:6, :]
    gain, shift = small_ref[6:7, :], small_ref[7:8, :]
    blocks = [slice(at, at + BLOCK) for at in range(0, rows, BLOCK)]
    contracted = [product(active_ref[block, :], contract_w[...]) + bias for block in blocks]
    totals = [0.0, 0.0, 0.0, 0.0]
    lows = []
    for at, block in enumerate(blocks):
        valid = valid_rows(lengths, step * len(blocks) + at, BLOCK, seq_len)
        totals[0] += jnp.sum(contracted[at] * contracted[at] * valid, axis=0, keepdims=True)
        summed = normed_ref[block, :] * gain_one + shift_one + contracted[at]
        center = summed - jnp.mean(summed, axis=-1, keepdims=True)
        inverse = lax.rsqrt(jnp.mean(center * center, axis=-1, keepdims=True) + norm_epsilon)
        normed = center * inverse
        hidden_low = (normed * gain + shift).astype(bf16)
        projected = product(hidden_low, colbert_w[...])
        inverse_len = lax.rsqrt(
            jnp.sum(projected * projected, axis=-1, keepdims=True) + norm_epsilon
        )
        normalized = projected * inverse_len
        embed_ref[block, :] = (normalized * valid).astype(bf16)
        grad_norm = cotangent_ref[block, :].astype(f32) * valid
        grad_projected = (
            inverse_len
            * (grad_norm - normalized * jnp.sum(normalized * grad_norm, axis=-1, keepdims=True))
        ).astype(bf16)
        colbert_ref[...] += product_left_t(hidden_low, grad_projected)
        grad_hidden = product_right_t(grad_projected, colbert_w[...])
        grad_normed = grad_hidden * normed
        totals[1] += jnp.sum(grad_normed, axis=0, keepdims=True)
        totals[2] += jnp.sum(grad_hidden, axis=0, keepdims=True)
        scaled = grad_hidden * gain
        grad_sum = inverse * (
            scaled
            - jnp.mean(scaled, axis=-1, keepdims=True)
            - normed * jnp.mean(grad_normed * gain, axis=-1, keepdims=True)
        )
        sum_ref[block, :] = grad_sum
        low = grad_sum.astype(bf16)
        low_ref[block, :] = low
        totals[3] += jnp.sum(low.astype(f32), axis=0, keepdims=True)
        lows.append(low)
    for at, total in enumerate(totals):
        sums_ref[at : at + 1, :] += total
    for block, low in zip(blocks, lows):
        for at in range(0, contract_w.shape[0], CHUNK):
            columns = slice(at, at + CHUNK)
            grad = product_right_t(low, contract_w[columns, :])
            grad_ref[block, columns] = (grad * slope_ref[block, columns].astype(f32)).astype(bf16)


def contract(
    place, lengths, active, slope, normed, small, cotangent, halves, pieces, shards, seq_len
):
    rows, width = normed.shape
    ff = active.shape[1]
    out = cotangent.shape[1]
    return kernel_call(
        partial(contract_kernel, shards, seq_len),
        "contract",
        (rows // (2 * BLOCK),),
        [
            rows_spec(2 * BLOCK, ff),
            rows_spec(2 * BLOCK, ff),
            rows_spec(2 * BLOCK, width),
            whole_spec(*small.shape),
            rows_spec(2 * BLOCK, out),
        ]
        + anywhere(len(halves) + len(pieces)),
        [
            rows_spec(2 * BLOCK, out),
            rows_spec(2 * BLOCK, width),
            rows_spec(2 * BLOCK, width),
            rows_spec(2 * BLOCK, ff),
            whole_spec(8, width),
            whole_spec(width, out),
        ],
        [
            shaped((rows, out), bf16),
            shaped((rows, width), f32),
            shaped((rows, width), bf16),
            shaped((rows, ff), bf16),
            shaped((8, width), f32),
            shaped((width, out), f32),
        ],
        [
            pltpu.VMEM((ff, width), bf16),
            pltpu.VMEM((width, out), bf16),
            pltpu.SemaphoreType.DMA((2, 2 * shards)),
        ],
        4 * rows * width * (ff + 2 * out),
        rows * (6 * width + 3 * ff) * 2,
    )(place, lengths, active, slope, normed, small, cotangent, *halves, *pieces)


def contract_grad_kernel(place, active_ref, grad_ref, mine_ref, peer_ref, total):
    total[...] = product_left_t(active_ref[...], grad_ref[...])
    half = mine_ref.shape[1]
    for ref, which in ((mine_ref, place[1]), (peer_ref, 1 - place[1])):
        ref[0] = total[pl.ds(pl.multiple_of(which * half, 8), half), :].astype(bf16)


def contract_grad(place, active, grad, shards):
    rows, ff = active.shape
    width = grad.shape[1]
    part = ff // shards
    piece = shaped((shards, part // 2, width), bf16)
    spec = pl.BlockSpec((1, part // 2, width), lambda i, *_: (i, 0, 0))
    return kernel_call(
        contract_grad_kernel,
        "contract_grad",
        (shards,),
        [pl.BlockSpec((rows, part), lambda i, *_: (0, i)), whole_spec(rows, width)],
        [spec, spec],
        [piece, piece],
        [pltpu.VMEM((part, width), f32)],
        2 * rows * width * ff,
        (rows * (width + ff) + width * ff) * 2,
        prefetch=1,
    )(place, active, grad)


def expand_grad_kernel(shards, place, low_ref, grad_ref, mine_ref, peer_ref, sums_ref, turned, total):
    width = low_ref.shape[1]

    @pl.when(pl.program_id(0) == 0)
    def _():
        turned[:width, :] = low_ref[...].T
        turned[width:, :] = jnp.ones((EXTRA, low_ref.shape[0]), bf16)

    total[...] = product(turned[...], grad_ref[...])
    sums_ref[...] = total[width : width + 8, :]
    store_pieces(place[0], place[1], total.at[:width], mine_ref, peer_ref)


def expand_grad(place, low, grad, shards):
    rows, ff = grad.shape
    width = low.shape[1]
    half = width // (2 * shards)
    piece = shaped((shards, half, ff), bf16)
    spec = pl.BlockSpec((shards, half, CHUNK), lambda i, *_: (0, 0, i))
    return kernel_call(
        partial(expand_grad_kernel, shards),
        "expand_grad",
        (ff // CHUNK,),
        [whole_spec(rows, width), pl.BlockSpec((rows, CHUNK), lambda i, *_: (0, i))],
        [spec, spec, pl.BlockSpec((8, CHUNK), lambda i, *_: (0, i))],
        [piece, piece, shaped((8, ff), f32)],
        [pltpu.VMEM((width + EXTRA, rows), bf16), pltpu.VMEM((width + EXTRA, CHUNK), f32)],
        2 * rows * width * ff,
        (rows * (width + ff) + width * ff) * 2,
        prefetch=1,
    )(place, low, grad)


def attended_grad_kernel(
    shards, place, sum_ref, grad_ref, normed_ref, inverse_ref, small_ref, *refs
):
    near, far, refs = refs[0], refs[1], refs[2:]
    next_ref, low_ref, context_ref, sums_ref = refs[:4]
    expand_w, out_w, sems = refs[4:]
    width = normed_ref.shape[1]

    @pl.when(pl.program_id(0) == 0)
    def _():
        load_all(out_expand_copies(place, near, far, out_w, expand_w, sems))
        sums_ref[...] = jnp.zeros_like(sums_ref)

    normed = normed_ref[...]
    grad_hidden = sum_ref[...] + product_right_t(grad_ref[...], expand_w[...])
    grad_normed = grad_hidden * normed
    gain = small_ref[3:4, :]
    sums_ref[1:2, :] += jnp.sum(grad_normed, axis=0, keepdims=True)
    sums_ref[2:3, :] += jnp.sum(grad_hidden, axis=0, keepdims=True)
    scaled = grad_hidden * gain
    grad_sum = inverse_ref[...] * (
        scaled
        - jnp.mean(scaled, axis=-1, keepdims=True)
        - normed * jnp.mean(grad_normed * gain, axis=-1, keepdims=True)
    )
    next_ref[...] = grad_sum
    low = grad_sum.astype(bf16)
    low_ref[...] = low
    sums_ref[0:1, :] += jnp.sum(low.astype(f32), axis=0, keepdims=True)
    context_ref[...] = product_right_t(low, out_w[...]).astype(bf16)


def attended_grad(
    place, grad_sum, grad, normed, inverse, small, halves, shards
):
    rows, width = normed.shape
    ff = grad.shape[1]
    return kernel_call(
        partial(attended_grad_kernel, shards),
        "attended_grad",
        (rows // BLOCK,),
        [
            rows_spec(BLOCK, width),
            rows_spec(BLOCK, ff),
            rows_spec(BLOCK, width),
            rows_spec(BLOCK, 1),
            whole_spec(*small.shape),
        ]
        + anywhere(len(halves)),
        [
            rows_spec(BLOCK, width),
            rows_spec(BLOCK, width),
            rows_spec(BLOCK, width),
            whole_spec(8, width),
        ],
        [
            shaped((rows, width), f32),
            shaped((rows, width), bf16),
            shaped((rows, width), bf16),
            shaped((8, width), f32),
        ],
        [
            pltpu.VMEM((width, ff), bf16),
            pltpu.VMEM((width, width), bf16),
            pltpu.SemaphoreType.DMA((2, 2 * shards)),
        ],
        2 * rows * width * (ff + width),
        rows * (8 * width + ff) * 2,
        prefetch=1,
    )(place, grad_sum, grad, normed, inverse, small, *halves)


def tokens_grad_kernel(shards, place, sum_ref, g0, g1, g2, *refs):
    count = piece_count(shards, 3)
    pieces, (out_ref, weight, sems) = refs[: 3 * count], refs[3 * count :]

    @pl.when(pl.program_id(0) == 0)
    def _():
        load_pieces(
            place,
            *[
                (
                    pieces[group * count : (group + 1) * count],
                    [(group * GROUP, GROUP)] * 3,
                    weight.at[group],
                    sems.at[group],
                    max(group - 1, 0) * 3 * GROUP,
                )
                for group in range(3)
            ],
        )

    grad = sum_ref[...]
    for group, ref in enumerate((g0, g1, g2)):
        grad = grad + product_right_t(ref[...], weight[group])
    out_ref[...] = grad.astype(bf16)


def tokens_grad(place, grad_sum, grads, pieces, part, parts, shards):
    rows, width = grad_sum.shape
    rows //= parts
    first = part * (rows // BLOCK)

    def later(width):
        return pl.BlockSpec((BLOCK, width), lambda i, *_: (first + i, 0))

    return kernel_call(
        partial(tokens_grad_kernel, shards),
        "tokens_grad",
        (rows // BLOCK,),
        [later(width)] + [later(3 * GROUP)] * 3 + anywhere(3 * piece_count(shards, 3)),
        rows_spec(BLOCK, width),
        shaped((rows, width), bf16),
        [
            pltpu.VMEM((3, width, 3 * GROUP), bf16),
            pltpu.SemaphoreType.DMA((3, piece_count(shards, 3))),
        ],
        0,
        0,
        prefetch=1,
    )(place, grad_sum, *grads, *[piece for one in pieces for piece in one])


def split_sum_kernel(axis, counts, kept, given, upper, held, *refs):
    others, outs = refs[: len(counts)], refs[len(counts) :]
    found = [(ref, at) for ref, count in zip(others, counts) for at in range(count)]
    for out, blocks in zip(outs, [kept, *given]):
        for to, block in enumerate(blocks):
            source, at = found[block]
            if axis is None:
                one, other = held[block], source[at]
            else:
                half = held.shape[axis] // 2
                which = upper[0] if out is outs[0] else 1 - upper[0]
                half_at = pl.ds(pl.multiple_of(which * half, 128 if axis == 2 else 16), half)
                where = (half_at, slice(None)) if axis == 1 else (slice(None), half_at)
                one, other = held[(block, *where)], source[(at, *where)]
            out[to] = (one.astype(f32) + other.astype(f32)).astype(bf16)


def split_sum(held, others, kept, given, axis, upper):
    shape = list(held.shape[1:])
    if axis is not None:
        shape[axis - 1] //= 2
        if shape[axis - 1] % (128 if axis == 2 else 16):
            total = low_sum(held, jnp.concatenate(others))
            size = shape[axis - 1]
            first, second = [
                lax.dynamic_slice_in_dim(total, at * size, size, axis) for at in (upper, 1 - upper)
            ]
            return first, [jnp.stack([second[block] for block in blocks]) for blocks in given]
    outs = [shaped((len(blocks), *shape), bf16) for blocks in [kept, *given]]
    if axis is None:
        columns = 768 if shape[1] % 768 == 0 else shape[1]

        def spec(one):
            return pl.BlockSpec((one.shape[0], shape[0], columns), lambda i, *_: (0, 0, i))

        first, *rest = kernel_call(
            partial(split_sum_kernel, axis, [one.shape[0] for one in others], kept, given),
            "split_sum",
            (shape[1] // columns,),
            [spec(one) for one in (held, *others)],
            [spec(one) for one in outs],
            outs,
            [],
            0,
            0,
            prefetch=1,
        )(upper.reshape(1), held, *others)
        return first, rest
    vmem = pl.BlockSpec(memory_space=pltpu.VMEM)
    first, *rest = pl.pallas_call(
        partial(split_sum_kernel, axis, [one.shape[0] for one in others], kept, given),
        name="split_sum",
        in_specs=[pl.BlockSpec(memory_space=pltpu.SMEM)] + [vmem] * (1 + len(others)),
        out_specs=[vmem] * len(outs),
        out_shape=outs,
        compiler_params=pltpu.CompilerParams(vmem_limit_bytes=VMEM_LIMIT),
        cost_estimate=pl.CostEstimate(flops=0, bytes_accessed=0, transcendentals=0),
    )(upper.reshape(1), held, *others)
    return first, rest


def low_sum(one, other):
    return (one.astype(f32) + other.astype(f32)).astype(bf16)


def replica_bits():
    distance, bits = 2, []
    while distance < lax.axis_size("replica"):
        bits.append(distance)
        distance *= 2
    return bits


def replica_sum(low):
    at = lax.axis_index("replica")
    for bit in replica_bits():
        half = low.shape[0] // 2
        upper = ((at & bit) != 0).astype(jnp.int32)
        given = lax.dynamic_slice_in_dim(low, (1 - upper) * half, half, 0)
        low = lax.dynamic_slice_in_dim(low, upper * half, half, 0)
        hold = yield [given]
        low = low_sum(low, after(lax.ppermute(given, "replica", replica_partners(bit)), hold))
    for bit in reversed(replica_bits()):
        hold = yield [low]
        other = after(lax.ppermute(low, "replica", replica_partners(bit)), hold)
        upper = (at & bit) != 0
        low = jnp.concatenate([jnp.where(upper, other, low), jnp.where(upper, low, other)])
    hold = yield [low]
    yield (low, after(lax.ppermute(low, "replica", replica_partners(1)), hold))


def reduction(mine, peer, stages, halved_axis, parted=0):
    at = lax.axis_index("replica")
    held = mine
    hold = yield [peer]
    others = [after(lax.ppermute(peer, "replica", replica_partners(1)), hold)]
    distances = list(range(held.shape[0]))
    for step, (axis, bit) in enumerate(stages):
        partners = (shard_partners if axis == "shard" else replica_partners)(bit)
        if axis == "shard" or halved_axis:
            blocks = list(range(len(distances)))
            kept = sent = blocks
            if axis == "shard":
                kept = [i for i in blocks if not distances[i] & bit]
                sent = [i for i in blocks if distances[i] & bit]
                distances = [distances[i] for i in kept]
            half = len(sent) // 2
            given = [sent[:half], sent[half:]] if step < parted and half else [sent]
            upper = ((at & bit) != 0).astype(jnp.int32)
            held, given = split_sum(
                held, others, kept, given, None if axis == "shard" else halved_axis, upper
            )
        else:
            held = low_sum(held, others[0])
            given = [held]
        hold = yield given
        others = []
        for piece in given:
            if others:
                hold = yield others
            others.append(after(lax.ppermute(piece, axis, partners), hold))
    low = low_sum(held, others[0])[0]
    if halved_axis:
        for bit in [bit for axis, bit in reversed(stages) if axis == "replica"]:
            hold = yield [low]
            other = after(lax.ppermute(low, "replica", replica_partners(bit)), hold)
            upper = (at & bit) != 0
            low = jnp.concatenate(
                [jnp.where(upper, other, low), jnp.where(upper, low, other)], axis=halved_axis - 1
            )
    hold = yield [low]
    yield (low, after(lax.ppermute(low, "replica", replica_partners(1)), hold))


def pack_kernel(place, *refs):
    weights, vectors, outs, sems = refs[:7], refs[7:16], refs[16:20], refs[20]
    part, width = weights[0].shape
    groups = width // GROUP
    copies = []

    def add(source, columns, target):
        half = source.shape[0] // 2
        rows = pl.ds(pl.multiple_of(place[1] * half, 16), half)
        source = source.at[rows] if columns is None else source.at[rows, columns]
        copies.append(pltpu.make_async_copy(source, target, sems.at[len(copies)]))

    for group in range(groups):
        for at in range(3):
            to = (max(group - 1, 0) * 3 + at) * GROUP
            target = outs[min(group, 1)].at[pl.ds(0, part // 2), pl.ds(to, GROUP)]
            add(weights[at], pl.ds(group * GROUP, GROUP), target)
    to = 0
    for at in (3, 6, 4):
        columns = weights[at].shape[1]
        add(weights[at], None, outs[2].at[:, pl.ds(to, columns)])
        to += columns
    add(weights[5], None, outs[3])
    for copy in copies:
        copy.start()
    long = vectors[8][...].astype(f32).reshape(1, -1)
    lines = [ref[...].astype(f32).reshape(1, -1) for ref in vectors[:8]]
    lines += [long[:, at : at + part] for at in range(0, long.shape[1], part)]
    row = rows_of(EXTRA, part)
    block = jnp.zeros((EXTRA, part), f32)
    for at, line in enumerate(lines):
        block = jnp.where(row == at, line, block)
    blank = jnp.zeros((EXTRA, outs[0].shape[1] - part), f32)
    outs[0][part // 2 :, :] = jnp.concatenate([block, blank], axis=1).astype(bf16)
    for copy in copies:
        copy.wait()


def pack(place, weights, vectors):
    part, width = weights[0].shape
    groups = width // GROUP
    half = part // 2
    shapes = [(half + EXTRA, 3 * GROUP), (half, (groups - 1) * 3 * GROUP)]
    shapes += [(half, sum(weights[at].shape[1] for at in (3, 4, 6)))]
    shapes += [(weights[5].shape[0] // 2, weights[5].shape[1])]
    vmem = pl.BlockSpec(memory_space=pltpu.VMEM)
    return pl.pallas_call(
        pack_kernel,
        name="pack",
        in_specs=[pl.BlockSpec(memory_space=pltpu.SMEM)] + anywhere(7) + [vmem] * 9,
        out_specs=[vmem] * len(shapes),
        out_shape=[shaped(shape, bf16) for shape in shapes],
        scratch_shapes=[pltpu.SemaphoreType.DMA((3 * groups + 4,))],
    )(place, *weights, *vectors)


def vectors_kernel(part, place, *refs):
    parts, (small_ref, expand_ref, held, sems) = refs[:-4], refs[-4:]
    shards = len(parts)
    copies = [
        pltpu.make_async_copy(
            ref.at[pl.ds(ref.shape[0] - EXTRA, EXTRA)], held.at[place[0] ^ d], sems.at[d]
        )
        for d, ref in enumerate(parts)
    ]
    for copy in copies:
        copy.start()
    for copy in copies:
        copy.wait()
    total = 0.0
    count = expand_ref.shape[1] // shards
    for shard in range(shards):
        block = held[shard].astype(f32)
        total = total + (pltpu.roll(block, shard * part, 1) if shard else block)
        line = 0.0
        for at in range(count // part):
            one = jnp.broadcast_to(block[8 + at : 9 + at, :], (8, block.shape[1]))
            line = line + (pltpu.roll(one, at * part, 1) if at else one)
        expand_ref[:, shard * count : (shard + 1) * count] = line[:, :count]
    small_ref[...] = total[:8]


def gather_vectors(place, parts, part, ff):
    vmem = pl.BlockSpec(memory_space=pltpu.VMEM)
    width = part * len(parts)
    return pl.pallas_call(
        partial(vectors_kernel, part),
        name="gather_vectors",
        in_specs=[pl.BlockSpec(memory_space=pltpu.SMEM)] + anywhere(len(parts)),
        out_specs=[vmem, vmem],
        out_shape=[shaped((8, width), f32), shaped((8, ff), f32)],
        scratch_shapes=[
            pltpu.VMEM((len(parts), EXTRA, width), bf16),
            pltpu.SemaphoreType.DMA((len(parts),)),
        ],
    )(place, *parts)


def join_halves(place, low_ref, other_ref, columns, out_ref):
    half = out_ref.shape[0] // 2
    for ref, which in ((low_ref, place[1]), (other_ref, 1 - place[1])):
        rows = pl.ds(pl.multiple_of(which * half, 8), half)
        out_ref[rows, :] = ref[0:half, columns].astype(f32)


def finish_ffn_kernel(place, low_e, other_e, low_c, other_c, expand_ref, contract_ref):
    join_halves(place, low_e, other_e, slice(None), expand_ref)
    join_halves(place, low_c, other_c, slice(None), contract_ref)


def finish_ffn(place, expand, contract):
    vmem = pl.BlockSpec(memory_space=pltpu.VMEM)
    shapes = [(2 * one[0].shape[0], one[0].shape[1]) for one in (expand, contract)]
    return pl.pallas_call(
        finish_ffn_kernel,
        name="finish_ffn",
        in_specs=[pl.BlockSpec(memory_space=pltpu.SMEM)] + [vmem] * 4,
        out_specs=[vmem] * 2,
        out_shape=[shaped(shape, f32) for shape in shapes],
        compiler_params=pltpu.CompilerParams(vmem_limit_bytes=VMEM_LIMIT),
    )(place, *expand, *contract)


def finish_attn_kernel(part, ff, place, *refs):
    pairs, refs = refs[:6], refs[6:]
    query, key, value, attn_out, colbert, rms = refs[:6]
    vectors = refs[6:]
    half = query.shape[0] // 2
    width = query.shape[1]
    for group in range(3):
        columns = slice(group * GROUP, (group + 1) * GROUP)
        for at, ref in enumerate((query, key, value)):
            source = slice(at * GROUP, (at + 1) * GROUP)
            join_halves(place, *pairs[2 * group : 2 * group + 2], source, ref.at[:, columns])
    at = 3 * GROUP
    join_halves(place, *pairs[:2], slice(at, at + width), attn_out)
    join_halves(place, *pairs[:2], slice(at + width, None), colbert)
    extra = pairs[0][half:, :width].astype(f32)
    lines = ff // width
    parts = width // part

    def own(block):
        return pltpu.roll(block, lax.rem(width - place[0] * part, width), 1)

    turned = own(extra)
    for at, ref in enumerate(vectors[2:8]):
        ref[...] = turned[at : at + 1, :part].reshape(part)
    size = ff // parts
    first = place[0] * size
    line = first // width
    row = rows_of(EXTRA, width)
    chosen = jnp.sum(jnp.where(row == 9 + line, extra, 0.0), axis=0, keepdims=True)
    chosen = jnp.broadcast_to(chosen, (8, width))
    chosen = pltpu.roll(chosen, lax.rem(width - lax.rem(first, width), width), 1)
    vectors[8][...] = chosen[0:1, :size].reshape(size)
    count = jnp.sum(jnp.where(row == 9 + lines, extra, 0.0)) / width
    lane = lanes(8, PAIR)
    squares = jnp.zeros((8, PAIR), f32)
    for at in range(3):
        total = jnp.sum(jnp.where(row == 6 + at, extra, 0.0))
        squares = jnp.where(lane == at, total, squares)
    rms[...] = jnp.sqrt(squares / (count * width))
    extra = own(pairs[4][half:, :width].astype(f32))
    for at, ref in enumerate(vectors[:2]):
        ref[...] = extra[at : at + 1, :part].reshape(part)


def finish_attn(place, sums, part, width, ff, out):
    vmem = pl.BlockSpec(memory_space=pltpu.VMEM)
    shapes = [(part, width)] * 4 + [(part, out), (8, PAIR)] + [(part,)] * 8
    shapes += [(ff * part // width,)]
    return pl.pallas_call(
        partial(finish_attn_kernel, part, ff),
        name="finish_attn",
        in_specs=[pl.BlockSpec(memory_space=pltpu.SMEM)] + [vmem] * 6,
        out_specs=[vmem] * len(shapes),
        out_shape=[shaped(shape, f32) for shape in shapes],
        compiler_params=pltpu.CompilerParams(vmem_limit_bytes=VMEM_LIMIT),
    )(place, *[one for pair in sums for one in pair])


def per_device(
    tokens,
    lengths,
    w_query,
    b_query,
    w_key,
    w_value,
    b_value,
    w_attn_out,
    b_attn_out,
    gain_one,
    shift_one,
    w_expand,
    b_expand,
    w_contract,
    b_contract,
    gain_two,
    shift_two,
    w_colbert,
    cotangent,
):
    seq_count, seq_len, width = tokens.shape
    rows = seq_count * seq_len
    shards = lax.axis_size("shard")
    part = width // shards
    half = part // 2
    mine = lax.axis_index("shard")
    core = lax.axis_index("replica") % 2
    ff = b_expand.shape[0] * shards
    out = w_colbert.shape[1]
    groups = width // GROUP
    place = jnp.stack([mine, core]).astype(jnp.int32)
    x = tokens.reshape(rows, width)

    vectors = (b_query, b_value, b_attn_out, gain_one, shift_one, b_contract, gain_two, shift_two)
    attn_weights = (w_query, w_key, w_value)
    bits = shard_bits()
    sent = pack(
        place,
        (*attn_weights, w_attn_out, w_expand, w_contract, w_colbert),
        (*vectors, b_expand),
    )
    first_gather = Gather(attn_weights, sent[0])
    other_gather = Gather(attn_weights, sent[1])
    contract_gather = Gather((w_contract,), sent[3])
    first_gather.start()
    other_gather.start()
    first_gather.swap()
    out_near = gather_halves(sent[2])
    small, expand_b = gather_vectors(
        place, [sent[0]] + [first_gather.near[d] for d in range(1, shards)], part, ff
    )
    attn_gather = [first_gather] + [other_gather] * (groups - 1)

    qkvs, contexts, logsums = [], [], []
    for group in range(groups):
        earlier = []
        if group == 0:
            earlier = other_gather.near.values()
        qkv, context, logsum = attend(
            place,
            lengths,
            after(x, *earlier),
            small,
            attn_gather[group].pieces(),
            group,
            shards,
            seq_len,
        )
        hold = logsum
        if group == 0:
            other_gather.swap(hold)
        elif group == 1:
            contract_gather.start(hold)
            out_halves = other_halves(after(out_near, hold))
        qkvs.append(qkv)
        contexts.append(context)
        logsums.append(logsum)
    normed, inverse, hidden_low, active, slope, squares = expand(
        place,
        lengths,
        x,
        contexts,
        small,
        expand_b,
        out_halves,
        shards,
        seq_len,
    )
    contract_gather.swap(squares)
    embeddings, grad_sum, grad_contracted, grad_expanded, sums, colbert = contract(
        place,
        lengths,
        active,
        slope,
        normed,
        small,
        cotangent.reshape(rows, out),
        out_halves,
        contract_gather.pieces(),
        shards,
        seq_len,
    )
    running, finals, token = {}, {}, []

    shard_stages = [("shard", bit) for bit in bits]
    replica_stages = [("replica", bit) for bit in replica_bits()]

    def begin(name, pieces, *how):
        running[name] = reduction(*pieces, *how)
        return next(running[name])

    def advance(*names):
        sent = []
        for name in names:
            value = running[name].send(token)
            if isinstance(value, tuple):
                finals[name] = value
                sent.append(value[1])
            else:
                sent += value
        return sent

    def scatter(mine, peer, hold):
        taken = after(lax.ppermute(peer, "replica", replica_partners(1)), hold)
        total = low_sum(mine, taken)
        total = total.reshape(-1, total.shape[-1])
        return total, lax.psum_scatter(total, "shard", scatter_dimension=0, tiled=True)

    contract_parts = contract_grad(place, active, grad_contracted, shards)
    *expand_parts, expand_sums = expand_grad(
        place, after(hidden_low, contract_parts), grad_expanded, shards
    )
    sent = begin("expand", expand_parts, shard_stages[::-1] + replica_stages, 2, 1)
    token, low_c = scatter(*contract_parts, expand_sums)
    grad_sum, grad_low, grad_context, own_sums = attended_grad(
        place, after(grad_sum, token, sent), grad_expanded, normed, inverse, small, out_halves, shards
    )
    token = [own_sums]
    token = advance("expand")
    grads, biases = [], []
    plan = (("expand",), ("expand", 0), ("contract", "expand", 0, 1))
    with_out = [*contexts, grad_low, own_sums, sums, squares, expand_sums, colbert]
    last = groups - 1
    for group in range(groups):
        grad, bias, *pieces = attend_back(
            place,
            lengths,
            x,
            qkvs[group],
            contexts[group],
            after(grad_context, token),
            logsums[group],
            group,
            biases if group == last else [],
            [] if group else with_out,
            shards,
            seq_len,
        )
        grads.append(grad)
        biases.append(bias)
        stages = shard_stages if group == last else shard_stages[::-1]
        sent = begin(group, pieces, stages + replica_stages, None if group else 2)
        token = [bias]
        if group == 1:
            running["contract"] = replica_sum(after(low_c, token))
            sent += next(running["contract"])
        token = sent + advance(*plan[group])
    parts = 2
    grad_tokens = []
    for part_at in range(parts):
        grad_tokens.append(
            tokens_grad(
                place,
                after(grad_sum, token),
                grads,
                [gather.pieces() for gather in attn_gather],
                part_at,
                parts,
                shards,
            )
        )
        token = [grad_tokens[-1]]
        token = advance(last, "contract", "expand", 0, 1)
    grad_tokens = jnp.stack(grad_tokens)
    while len(finals) < len(running):
        token = advance(*[name for name in (last, 0, 1, "contract", "expand") if name not in finals])
    r_we, r_wc = finish_ffn(place, finals["expand"], finals["contract"])
    r_wq, r_wk, r_wv, r_wo, r_wp, rms_values, *r_small = finish_attn(
        place, [finals[group] for group in range(groups)], part, width, ff, out
    )
    r_bq, r_bv, r_bo, r_ga, r_sa, r_bc, r_gb, r_sb, r_be = r_small
    return (
        embeddings.reshape(seq_count, seq_len, out),
        grad_tokens.reshape(seq_count, seq_len, width),
        r_wq,
        r_bq,
        r_wk,
        r_wv,
        r_bv,
        r_wo,
        r_bo,
        r_ga,
        r_sa,
        r_we,
        r_be,
        r_wc,
        r_bc,
        r_gb,
        r_sb,
        r_wp,
        rms_values[0, :3],
    )


def solution(mesh):
    rows = P(("replica", "shard"), None, None)
    matrix, vector = P("shard", None), P("shard")
    weights = (
        matrix,
        vector,
        matrix,
        matrix,
        vector,
        matrix,
        vector,
        vector,
        vector,
        matrix,
        vector,
        matrix,
        vector,
        vector,
        vector,
        matrix,
    )
    return jax.shard_map(
        per_device,
        mesh=mesh,
        in_specs=(rows, P(("replica", "shard")), *weights, rows),
        out_specs=(rows, rows, *weights, P()),
        check_vma=False,
    )
```

```python
from functools import partial

import jax
import jax.numpy as jnp
from jax import lax
from jax.experimental import pallas as pl
from jax.experimental.pallas import tpu as pltpu
from jax.sharding import PartitionSpec as P

HEADS = 12
HEAD_DIM = 64
GROUP_HEADS = 4
GROUP = GROUP_HEADS * HEAD_DIM
PAIR = 2 * HEAD_DIM
EXTRA = 16
BLOCK = 256
CHUNK = 512
SCALE = HEAD_DIM**-0.5
VMEM_LIMIT = 52 * 1024 * 1024

norm_epsilon = 1e-12
masked_score = -1e30
f32 = jnp.float32
bf16 = jnp.bfloat16


def product(left, right):
    return jnp.dot(left, right, preferred_element_type=f32)


def product_left_t(left, right):
    return lax.dot_general(left, right, (((0,), (0,)), ((), ())), preferred_element_type=f32)


def product_right_t(left, right):
    return lax.dot_general(left, right, (((1,), (1,)), ((), ())), preferred_element_type=f32)


def shard_partners(distance):
    return [(i, i ^ distance) for i in range(lax.axis_size("shard"))]


def replica_partners(distance):
    return [(i, i ^ distance) for i in range(lax.axis_size("replica"))]


def after(value, *earlier):
    return lax.optimization_barrier((value, *jax.tree.leaves(earlier)))[0]


def shard_bits():
    distance, bits = 1, []
    while distance < lax.axis_size("shard"):
        bits.append(distance)
        distance *= 2
    return bits


def gather_halves(sent):
    return lax.all_gather(sent, "shard", axis=0)


def other_halves(near):
    return near, lax.ppermute(near, "replica", replica_partners(1))


def halves_copies(core, near, far, columns, target, sems):
    shards, half = near.shape[:2]
    copies = []
    for shard in range(shards):
        for ref, which in ((near, core), (far, 1 - core)):
            rows = pl.ds(pl.multiple_of((2 * shard + which) * half, 16), half)
            copies.append(
                pltpu.make_async_copy(
                    ref.at[shard, :, columns], target.at[rows], sems.at[len(copies)]
                )
            )
    return copies


class Gather:
    def __init__(self, own, sent, order=None):
        self.own = own
        self.sent = sent
        self.order = order
        self.near = {}
        self.far = {}

    def start(self, *earlier):
        sent = after(self.sent, *earlier)
        distances = self.order or range(1, lax.axis_size("shard"))
        for d in distances:
            self.near[d] = lax.ppermute(sent, "shard", shard_partners(d))

    def relay(self, *earlier):
        known = [self.order[0]]
        for distance in self.order[1:]:
            for d in known:
                piece = after(self.near[d], *earlier)
                self.near[d | distance] = lax.ppermute(piece, "shard", shard_partners(distance))
            known += [distance] + [d | distance for d in known]

    def swap(self, *earlier, distances=None):
        for d in distances or [d for d in self.near if d not in self.far]:
            piece = after(self.near[d], *earlier)
            self.far[d] = lax.ppermute(piece, "replica", replica_partners(1))

    def pieces(self):
        distances = range(1, lax.axis_size("shard"))
        return (*self.own, *[self.near[d] for d in distances], *[self.far[d] for d in distances])


def piece_count(shards, own):
    return own + 2 * (shards - 1)


def piece_copies(place, pieces, own, target, sems, first=0):
    mine, core = place[0], place[1]
    near = pieces[len(own) :]
    shards = len(near) // 2 + 1
    rows = pieces[0].shape[0]
    half = rows // 2
    copies = []

    def add(source, target):
        copies.append(pltpu.make_async_copy(source, target, sems.at[len(copies)]))

    place_at = 0
    for ref, columns in zip(pieces, own):
        at, width = columns or (0, ref.shape[1])
        if width != ref.shape[1]:
            ref = ref.at[:, pl.ds(at, width)]
        start = pl.multiple_of(mine * rows, 16)
        add(ref, target.at[pl.ds(start, rows), pl.ds(place_at, width)])
        place_at += width
    for d in range(1, shards):
        start = (mine ^ d) * rows
        for ref, which in ((near[d - 1], core), (near[shards + d - 2], 1 - core)):
            if ref.shape != (half, place_at):
                ref = ref.at[pl.ds(0, half), pl.ds(first, place_at)]
            add(ref, target.at[pl.ds(pl.multiple_of(start + which * half, 16), half)])
    return copies


def load_all(copies):
    for copy in copies:
        copy.start()
    for copy in copies:
        copy.wait()


def load_pieces(place, *sets):
    load_all([copy for one in sets for copy in piece_copies(place, *one)])


def store_pieces(mine, core, total, mine_ref, peer_ref, extra=None):
    shards = mine_ref.shape[0]
    half = total.shape[0] // (2 * shards)
    for d in range(shards):
        start = (mine ^ d) * 2
        for ref, which in ((mine_ref, core), (peer_ref, 1 - core)):
            at = pl.multiple_of((start + which) * half, 8)
            ref[d, 0:half] = total[pl.ds(at, half), :].astype(bf16)
            if extra is not None:
                ref[d, half:] = extra


def kernel_call(body, name, grid, in_specs, out_specs, out_shape, scratch, flops, moved, prefetch=2):
    return pl.pallas_call(
        body,
        name=name,
        grid_spec=pltpu.PrefetchScalarGridSpec(
            num_scalar_prefetch=prefetch,
            grid=grid,
            in_specs=in_specs,
            out_specs=out_specs,
            scratch_shapes=scratch,
        ),
        out_shape=out_shape,
        compiler_params=pltpu.CompilerParams(
            dimension_semantics=("arbitrary",) * len(grid), vmem_limit_bytes=VMEM_LIMIT
        ),
        cost_estimate=pl.CostEstimate(flops=flops, bytes_accessed=moved, transcendentals=0),
    )


def anywhere(count):
    return [pl.BlockSpec(memory_space=pl.ANY)] * count


def rows_spec(rows, width, column=0):
    return pl.BlockSpec((rows, width), lambda i, *_: (i, column))


def whole_spec(*shape):
    return pl.BlockSpec(shape, lambda *_: (0,) * len(shape))


def shaped(shape, dtype):
    return jax.ShapeDtypeStruct(shape, dtype)


def lanes(rows, width):
    return lax.broadcasted_iota(jnp.int32, (rows, width), 1)


def rows_of(rows, width):
    return lax.broadcasted_iota(jnp.int32, (rows, width), 0)


def attend_kernel(shards, groups, place, lengths, x_ref, bias_ref, *refs):
    count = piece_count(shards, 3 * groups)
    pieces, refs = refs[:count], refs[count:]
    qkv_ref, context_ref, logsum_ref, joined_ref, weight, sems = refs
    join = pltpu.make_async_copy(weight, joined_ref, sems.at[count])
    step, group = pl.program_id(0), pl.program_id(1)

    @pl.when((step == 0) & (group == 0))
    def _():
        load_pieces(place, (pieces, head_columns(groups), weight, sems))
        join.start()

    @pl.when((step == pl.num_programs(0) - 1) & (group == groups - 1))
    def _():
        join.wait()

    length = lengths[step]
    seq_len = x_ref.shape[0]
    no_bias = jnp.zeros((1, GROUP), f32)
    columns = pl.ds(pl.multiple_of(group * GROUP, GROUP), GROUP)
    bias = jnp.concatenate([bias_ref[0:1, columns], no_bias, bias_ref[1:2, columns]], axis=1)
    columns = pl.ds(pl.multiple_of(group * 3 * GROUP, GROUP), 3 * GROUP)
    qkv = (product(x_ref[...], weight[:, columns]) + bias).astype(bf16)
    qkv_ref[...] = qkv
    lane = lanes(seq_len, PAIR)
    padded = rows_of(seq_len, PAIR) >= length
    totals = jnp.ones((seq_len, PAIR), f32)
    highests = jnp.zeros((seq_len, PAIR), f32)
    sums = []
    for pair in range(GROUP_HEADS // 2):
        at = pair * PAIR
        queries = qkv[:, at : at + PAIR].astype(f32) * SCALE
        keys = qkv[:, GROUP + at : GROUP + at + PAIR].astype(f32)
        values = qkv[:, 2 * GROUP + at : 2 * GROUP + at + PAIR].astype(f32)
        for head in range(2):
            own = (lane >= HEAD_DIM) == (head == 1)
            free = lane == free_lane(pair, head)
            one = jnp.where(free, 1.0, 0.0)
            q = jnp.where(own, queries, one).astype(bf16)
            k = jnp.where(own, keys, jnp.where(padded, one * masked_score, 0.0)).astype(bf16)
            v = jnp.where(own, values, one).astype(bf16)
            scores = product_right_t(q, k)
            highest = jnp.max(scores, axis=-1, keepdims=True)
            exponent = jnp.exp(scores - highest).astype(bf16)
            summed = product(exponent, v)
            totals = jnp.where(free, summed, totals)
            highests = jnp.where(free, highest, highests)
            sums.append(summed)
    logsum_ref[...] = highests + jnp.log(totals)
    inverse = 1.0 / totals
    for pair in range(GROUP_HEADS // 2):
        halves = []
        for head in range(2):
            free = free_lane(pair, head)
            halves.append(sums[2 * pair + head] * inverse[:, free : free + 1])
        context = jnp.where(lane < HEAD_DIM, halves[0], halves[1])
        context_ref[:, pair * PAIR : (pair + 1) * PAIR] = context.astype(bf16)


def free_lane(pair, head):
    return HEAD_DIM * (1 - head) + pair


def head_columns(groups):
    return [(group * GROUP, GROUP) for group in range(groups) for _ in range(3)]


def attend(place, lengths, x, bias, pieces, shards, seq_len):
    rows, width = x.shape
    groups = width // GROUP

    def spec(columns):
        return pl.BlockSpec((seq_len, columns), lambda i, group, *_: (i, group))

    return kernel_call(
        partial(attend_kernel, shards, groups),
        "attend",
        (rows // seq_len, groups),
        [pl.BlockSpec((seq_len, width), lambda i, *_: (i, 0)), whole_spec(8, width)]
        + anywhere(len(pieces)),
        [spec(3 * GROUP), spec(GROUP), spec(PAIR)] + anywhere(1),
        [
            shaped((rows, 3 * width), bf16),
            shaped((rows, width), bf16),
            shaped((rows, groups * PAIR), f32),
            shaped((width, 3 * width), bf16),
        ],
        [
            pltpu.VMEM((width, 3 * width), bf16),
            pltpu.SemaphoreType.DMA((piece_count(shards, 3 * groups) + 1,)),
        ],
        groups * (2 * rows * width * 3 * GROUP + 16 * rows * seq_len * PAIR * GROUP_HEADS),
        groups * rows * (width + 6 * GROUP) * 2,
    )(place, lengths, x, bias, *pieces)


def split_low(value):
    high = value.astype(bf16).astype(f32)
    return high, value - high


def query_value_lines(before, sums):
    row = rows_of(EXTRA, GROUP)
    parts = [
        jnp.where(row == 0, one[:, :GROUP], jnp.where(row == 1, one[:, 2 * GROUP :], 0.0))
        for one in [ref[0:1, :] for ref in before] + [sums]
    ]
    return jnp.concatenate(parts, axis=1)


def vector_lines(lengths, own_sums, sums, squares, expand_sums, columns):
    width = own_sums.shape[1]
    positions = 0
    for seq in range(lengths.shape[0]):
        positions = positions + lengths[seq]
    lines = [own_sums[at : at + 1, :] for at in (0, 1, 2)]
    lines += [sums[at : at + 1, :] for at in (3, 1, 2)]
    lines += [squares[0:1, :], squares[1:2, :], sums[0:1, :]]
    lines += [expand_sums[0:1, at : at + width] for at in range(0, expand_sums.shape[1], width)]
    row = rows_of(EXTRA, width)
    extra = jnp.zeros((EXTRA, width), f32) + positions.astype(f32)
    for at, line in enumerate(lines):
        extra = jnp.where(row == at, line, extra)
    return jnp.concatenate([extra, jnp.zeros((EXTRA, columns - width), f32)], axis=1)


def attend_back_kernel(
    shards,
    before_count,
    with_out,
    place,
    lengths,
    x_ref,
    qkv_ref,
    context_ref,
    grad_ref,
    logsum_ref,
    *refs,
):
    before, refs = refs[:before_count], refs[before_count:]
    if with_out:
        (contexts, grad_low_ref, own_sums, sums_ref, squares, expand_sums, colbert) = refs[:7]
        refs = refs[7:]
    grads_ref, bias_ref, mine_ref, peer_ref, kept, total = refs
    step = pl.program_id(0)
    length = lengths[step]
    seq_len = qkv_ref.shape[0]
    lane = lanes(seq_len, PAIR)
    padded = rows_of(seq_len, PAIR) >= length
    for pair in range(GROUP_HEADS // 2):
        at = pair * PAIR
        queries = qkv_ref[:, at : at + PAIR].astype(f32) * SCALE
        keys = qkv_ref[:, GROUP + at : GROUP + at + PAIR].astype(f32)
        values = qkv_ref[:, 2 * GROUP + at : 2 * GROUP + at + PAIR].astype(f32)
        context = context_ref[:, at : at + PAIR].astype(f32)
        grad_low = grad_ref[:, at : at + PAIR]
        grad = grad_low.astype(f32)
        grad_context = grad * context
        grad_q, grad_k, grad_v = 0.0, [], []
        for head in range(2):
            own = (lane >= HEAD_DIM) == (head == 1)
            free = HEAD_DIM * (1 - head)
            first, second, third = lane == free, lane == free + 1, lane == free + 2
            source = free_lane(pair, head)
            logsum = logsum_ref[:, source : source + 1]
            delta = jnp.sum(jnp.where(own, grad_context, 0.0), axis=-1, keepdims=True)
            log_high, log_low = split_low(logsum)
            delta_high, delta_low = split_low(delta)
            one = jnp.where(first, 1.0, 0.0)
            other = jnp.where(second | third, 1.0, 0.0)
            low_lanes = jnp.where(second, -log_high, jnp.where(third, -log_low, one))
            q = jnp.where(own, queries, low_lanes).astype(bf16)
            k_lanes = jnp.where(padded, one * masked_score, 0.0) + other
            k = jnp.where(own, keys, k_lanes).astype(bf16)
            low_lanes = jnp.where(second, -delta_high, jnp.where(third, -delta_low, 0.0))
            g = jnp.where(own, grad, low_lanes).astype(bf16)
            v = jnp.where(own, values, other).astype(bf16)
            weights = jnp.exp(product_right_t(k, q))
            weights_low = weights.astype(bf16)
            grad_scores = (weights * product_right_t(v, g)).astype(bf16)
            grad_v.append(product(weights_low, grad_low))
            grad_k.append(product(grad_scores, q))
            only = jnp.where(own, keys, 0.0).astype(bf16)
            grad_q = grad_q + product_left_t(grad_scores, only)
        pieces = (
            grad_q * SCALE,
            jnp.where(lane < HEAD_DIM, grad_k[0], grad_k[1]),
            jnp.where(lane < HEAD_DIM, grad_v[0], grad_v[1]),
        )
        for which, piece in enumerate(pieces):
            columns = slice(which * GROUP + at, which * GROUP + at + PAIR)
            grads_ref[:, columns] = piece.astype(bf16)
    kept[pl.ds(pl.multiple_of(step * seq_len, 16), seq_len), :] = grads_ref[...]

    @pl.when(step == pl.num_programs(0) - 1)
    def _():
        grads = kept[...]
        sums = jnp.sum(grads.astype(f32), axis=0, keepdims=True)
        bias_ref[...] = jnp.broadcast_to(sums, bias_ref.shape)
        width = x_ref.shape[1]
        total[:, : 3 * GROUP] = product_left_t(x_ref[...], grads)
        extra = None
        if with_out:
            at = 3 * GROUP
            total[:, at : at + width] = product_left_t(contexts[...], grad_low_ref[...])
            total[:, at + width :] = colbert[...]
            extra = vector_lines(
                lengths, own_sums, sums_ref, squares, expand_sums, total.shape[1]
            ).astype(bf16)
        elif before_count:
            extra = query_value_lines(before, sums).astype(bf16)
        store_pieces(place[0], place[1], total, mine_ref, peer_ref, extra)


def attend_back(
    place, lengths, x, qkv, context, grad, logsum, group, before, with_out, shards, seq_len
):
    rows, width = x.shape
    half = width // (2 * shards) + (EXTRA if before or with_out else 0)
    columns = 3 * GROUP + (width + with_out[-1].shape[1] if with_out else 0)
    piece = shaped((shards, half, columns), bf16)
    return kernel_call(
        partial(attend_back_kernel, shards, len(before), bool(with_out)),
        "attend_back",
        (rows // seq_len,),
        [
            whole_spec(rows, width),
            rows_spec(seq_len, 3 * GROUP, group),
            rows_spec(seq_len, GROUP, group),
            rows_spec(seq_len, GROUP, group),
            rows_spec(seq_len, PAIR, group),
        ]
        + [whole_spec(*one.shape) for one in (*before, *with_out)],
        [
            rows_spec(seq_len, 3 * GROUP),
            whole_spec(8, 3 * GROUP),
            whole_spec(*piece.shape),
            whole_spec(*piece.shape),
        ],
        [shaped((rows, 3 * GROUP), bf16), shaped((8, 3 * GROUP), f32), piece, piece],
        [pltpu.VMEM((rows, 3 * GROUP), bf16), pltpu.VMEM((width, columns), f32)],
        2 * rows * width * columns + 40 * rows * seq_len * PAIR * GROUP_HEADS,
        rows * (2 * width + 9 * GROUP) * 2,
    )(place, lengths, x, qkv, context, grad, logsum, *before, *with_out)


def gelu_and_slope(u):
    share = 0.5 * lax.erf(u * 0.7071067811865476) + 0.5
    return u * share, share + (u * 0.3989422804014327) * jnp.exp(-0.5 * (u * u))


def valid_rows(lengths, step, rows, seq_len):
    first = step * rows
    seq = first // seq_len
    at = rows_of(rows, 1) + (first - seq * seq_len)
    return (at < lengths[seq]).astype(f32)


def out_expand_copies(place, near, far, out_w, expand_w, sems):
    width, ff = out_w.shape[1], expand_w.shape[1]
    first = near.shape[2] - ff
    copies = halves_copies(place[1], near, far, pl.ds(0, width), out_w, sems.at[0])
    return copies + halves_copies(place[1], near, far, pl.ds(first, ff), expand_w, sems.at[1])


def expand_kernel(shards, seq_len, place, lengths, x_ref, heads_ref, small_ref, expand_b, *refs):
    near, far, refs = refs[0], refs[1], refs[2:]
    normed_ref, inverse_ref, low_ref, active_ref, slope_ref, squares_ref = refs[:6]
    out_w, expand_w, sems = refs[6:]
    step = pl.program_id(0)
    width = x_ref.shape[1]

    @pl.when(step == 0)
    def _():
        copies = out_expand_copies(place, near, far, out_w, expand_w, sems)
        for copy in copies:
            copy.start()
        for copy in copies[: len(copies) // 2]:
            copy.wait()
        squares_ref[...] = jnp.zeros_like(squares_ref)

    rows = x_ref.shape[0]
    attended = product(heads_ref[...], out_w[...]) + small_ref[2:3, :]
    x = x_ref[...].astype(f32)
    valid = valid_rows(lengths, step, rows, seq_len)
    squares_ref[0:1, :] += jnp.sum(x * x * valid, axis=0, keepdims=True)
    squares_ref[1:2, :] += jnp.sum(attended * attended * valid, axis=0, keepdims=True)
    summed = x + attended
    center = summed - jnp.mean(summed, axis=-1, keepdims=True)
    inverse = lax.rsqrt(jnp.mean(center * center, axis=-1, keepdims=True) + norm_epsilon)
    normed = center * inverse
    normed_ref[...] = normed
    inverse_ref[...] = inverse
    low = (normed * small_ref[3:4, :] + small_ref[4:5, :]).astype(bf16)
    low_ref[...] = low

    @pl.when(step == 0)
    def _():
        copies = out_expand_copies(place, near, far, out_w, expand_w, sems)
        for copy in copies[len(copies) // 2 :]:
            copy.wait()

    for at in range(0, expand_w.shape[1], CHUNK):
        columns = slice(at, at + CHUNK)
        active, slope = gelu_and_slope(product(low, expand_w[:, columns]) + expand_b[0:1, columns])
        active_ref[:, columns] = active.astype(bf16)
        slope_ref[:, columns] = slope.astype(bf16)


def expand(place, lengths, x, context, small, expand_b, halves, shards, seq_len):
    rows, width = x.shape
    ff = expand_b.shape[1]
    return kernel_call(
        partial(expand_kernel, shards, seq_len),
        "expand",
        (rows // BLOCK,),
        [rows_spec(BLOCK, width)] * 2
        + [whole_spec(*small.shape), whole_spec(*expand_b.shape)]
        + anywhere(len(halves)),
        [
            rows_spec(BLOCK, width),
            rows_spec(BLOCK, 1),
            rows_spec(BLOCK, width),
            rows_spec(BLOCK, ff),
            rows_spec(BLOCK, ff),
            whole_spec(8, width),
        ],
        [
            shaped((rows, width), f32),
            shaped((rows, 1), f32),
            shaped((rows, width), bf16),
            shaped((rows, ff), bf16),
            shaped((rows, ff), bf16),
            shaped((8, width), f32),
        ],
        [
            pltpu.VMEM((width, width), bf16),
            pltpu.VMEM((width, ff), bf16),
            pltpu.SemaphoreType.DMA((2, 2 * shards)),
        ],
        6 * rows * width * (width + ff),
        rows * (6 * width + 2 * ff) * 2,
    )(place, lengths, x, context, small, expand_b, *halves)


def contract_kernel(
    shards, seq_len, place, lengths, active_ref, slope_ref, normed_ref, small_ref, cotangent_ref, *refs
):
    near, far = refs[:2]
    count = piece_count(shards, 1)
    pieces, refs = refs[2 : 2 + count], refs[2 + count :]
    embed_ref, sum_ref, low_ref, grad_ref, sums_ref, colbert_ref = refs[:6]
    contract_w, colbert_w, sems = refs[6:]
    step = pl.program_id(0)
    rows, width = normed_ref.shape
    out = colbert_w.shape[1]

    @pl.when(step == 0)
    def _():
        copies = piece_copies(place, pieces, [None], contract_w, sems.at[0])
        columns = pl.ds(width, out)
        load_all(copies + halves_copies(place[1], near, far, columns, colbert_w, sems.at[1]))
        sums_ref[...] = jnp.zeros_like(sums_ref)
        colbert_ref[...] = jnp.zeros_like(colbert_ref)

    gain_one, shift_one, bias = small_ref[3:4, :], small_ref[4:5, :], small_ref[5:6, :]
    gain, shift = small_ref[6:7, :], small_ref[7:8, :]
    blocks = [slice(at, at + BLOCK) for at in range(0, rows, BLOCK)]
    width = contract_w.shape[1]
    contracted, lows = {}, {}
    totals = [0.0, 0.0, 0.0, 0.0]

    def forward(at):
        parts = []
        for columns in range(0, width, GROUP):
            part = product(active_ref[blocks[at], :], contract_w[:, columns : columns + GROUP])
            parts.append(part)
            yield
        contracted[at] = jnp.concatenate(parts, axis=1) + bias

    def norm(at):
        block = blocks[at]
        valid = valid_rows(lengths, step * len(blocks) + at, BLOCK, seq_len)
        totals[0] += jnp.sum(contracted[at] * contracted[at] * valid, axis=0, keepdims=True)
        summed = normed_ref[block, :] * gain_one + shift_one + contracted[at]
        center = summed - jnp.mean(summed, axis=-1, keepdims=True)
        yield
        inverse = lax.rsqrt(jnp.mean(center * center, axis=-1, keepdims=True) + norm_epsilon)
        normed = center * inverse
        hidden_low = (normed * gain + shift).astype(bf16)
        projected = product(hidden_low, colbert_w[...])
        yield
        inverse_len = lax.rsqrt(
            jnp.sum(projected * projected, axis=-1, keepdims=True) + norm_epsilon
        )
        normalized = projected * inverse_len
        embed_ref[block, :] = (normalized * valid).astype(bf16)
        grad_norm = cotangent_ref[block, :].astype(f32) * valid
        grad_projected = (
            inverse_len
            * (grad_norm - normalized * jnp.sum(normalized * grad_norm, axis=-1, keepdims=True))
        ).astype(bf16)
        yield
        grad_hidden = product_right_t(grad_projected, colbert_w[...])
        colbert_ref[...] += product_left_t(hidden_low, grad_projected)
        yield
        grad_normed = grad_hidden * normed
        totals[1] += jnp.sum(grad_normed, axis=0, keepdims=True)
        totals[2] += jnp.sum(grad_hidden, axis=0, keepdims=True)
        scaled = grad_hidden * gain
        yield
        grad_sum = inverse * (
            scaled
            - jnp.mean(scaled, axis=-1, keepdims=True)
            - normed * jnp.mean(grad_normed * gain, axis=-1, keepdims=True)
        )
        sum_ref[block, :] = grad_sum
        low = grad_sum.astype(bf16)
        low_ref[block, :] = low
        totals[3] += jnp.sum(low.astype(f32), axis=0, keepdims=True)
        lows[at] = low

    def backward(at):
        for columns in range(0, contract_w.shape[0], CHUNK):
            columns = slice(columns, columns + CHUNK)
            grad = product_right_t(lows[at], contract_w[columns, :])
            slope = slope_ref[blocks[at], columns].astype(f32)
            grad_ref[blocks[at], columns] = (grad * slope).astype(bf16)
            yield

    def together(*parts):
        parts = list(parts)
        while parts:
            parts = [part for part in parts if next(part, parts) is not parts]

    together(forward(0))
    for at in range(len(blocks)):
        beside = [forward(at + 1)] if at + 1 < len(blocks) else []
        together(norm(at), *beside, *([backward(at - 1)] if at else []))
    together(backward(len(blocks) - 1))
    for at, total in enumerate(totals):
        sums_ref[at : at + 1, :] += total


def contract(
    place, lengths, active, slope, normed, small, cotangent, halves, pieces, shards, seq_len
):
    rows, width = normed.shape
    ff = active.shape[1]
    out = cotangent.shape[1]
    return kernel_call(
        partial(contract_kernel, shards, seq_len),
        "contract",
        (rows // (2 * BLOCK),),
        [
            rows_spec(2 * BLOCK, ff),
            rows_spec(2 * BLOCK, ff),
            rows_spec(2 * BLOCK, width),
            whole_spec(*small.shape),
            rows_spec(2 * BLOCK, out),
        ]
        + anywhere(len(halves) + len(pieces)),
        [
            rows_spec(2 * BLOCK, out),
            rows_spec(2 * BLOCK, width),
            rows_spec(2 * BLOCK, width),
            rows_spec(2 * BLOCK, ff),
            whole_spec(8, width),
            whole_spec(width, out),
        ],
        [
            shaped((rows, out), bf16),
            shaped((rows, width), f32),
            shaped((rows, width), bf16),
            shaped((rows, ff), bf16),
            shaped((8, width), f32),
            shaped((width, out), f32),
        ],
        [
            pltpu.VMEM((ff, width), bf16),
            pltpu.VMEM((width, out), bf16),
            pltpu.SemaphoreType.DMA((2, 2 * shards)),
        ],
        4 * rows * width * (ff + 2 * out),
        rows * (6 * width + 3 * ff) * 2,
    )(place, lengths, active, slope, normed, small, cotangent, *halves, *pieces)


def contract_grad_kernel(place, active_ref, grad_ref, mine_ref, peer_ref, total):
    total[...] = product_left_t(active_ref[...], grad_ref[...])
    half = mine_ref.shape[1]
    for ref, which in ((mine_ref, place[1]), (peer_ref, 1 - place[1])):
        ref[0] = total[pl.ds(pl.multiple_of(which * half, 8), half), :].astype(bf16)


def contract_grad(place, active, grad, shards):
    rows, ff = active.shape
    width = grad.shape[1]
    part = ff // shards
    piece = shaped((shards, part // 2, width), bf16)
    spec = pl.BlockSpec((1, part // 2, width), lambda i, *_: (i, 0, 0))
    return kernel_call(
        contract_grad_kernel,
        "contract_grad",
        (shards,),
        [pl.BlockSpec((rows, part), lambda i, *_: (0, i)), whole_spec(rows, width)],
        [spec, spec],
        [piece, piece],
        [pltpu.VMEM((part, width), f32)],
        2 * rows * width * ff,
        (rows * (width + ff) + width * ff) * 2,
        prefetch=1,
    )(place, active, grad)


def expand_grad_kernel(shards, place, low_ref, grad_ref, mine_ref, peer_ref, sums_ref, turned, total):
    width = low_ref.shape[1]

    @pl.when(pl.program_id(0) == 0)
    def _():
        turned[:width, :] = low_ref[...].T
        turned[width:, :] = jnp.ones((EXTRA, low_ref.shape[0]), bf16)

    total[...] = product(turned[...], grad_ref[...])
    sums_ref[...] = total[width : width + 8, :]
    store_pieces(place[0], place[1], total.at[:width], mine_ref, peer_ref)


def expand_grad(place, low, grad, shards):
    rows, ff = grad.shape
    width = low.shape[1]
    half = width // (2 * shards)
    piece = shaped((shards, half, ff), bf16)
    spec = pl.BlockSpec((shards, half, CHUNK), lambda i, *_: (0, 0, i))
    return kernel_call(
        partial(expand_grad_kernel, shards),
        "expand_grad",
        (ff // CHUNK,),
        [whole_spec(rows, width), pl.BlockSpec((rows, CHUNK), lambda i, *_: (0, i))],
        [spec, spec, pl.BlockSpec((8, CHUNK), lambda i, *_: (0, i))],
        [piece, piece, shaped((8, ff), f32)],
        [pltpu.VMEM((width + EXTRA, rows), bf16), pltpu.VMEM((width + EXTRA, CHUNK), f32)],
        2 * rows * width * ff,
        (rows * (width + ff) + width * ff) * 2,
        prefetch=1,
    )(place, low, grad)


def attended_grad_kernel(
    shards, place, sum_ref, grad_ref, normed_ref, inverse_ref, small_ref, *refs
):
    near, far, refs = refs[0], refs[1], refs[2:]
    next_ref, low_ref, context_ref, sums_ref = refs[:4]
    expand_w, out_w, sems = refs[4:]
    width = normed_ref.shape[1]

    @pl.when(pl.program_id(0) == 0)
    def _():
        load_all(out_expand_copies(place, near, far, out_w, expand_w, sems))
        sums_ref[...] = jnp.zeros_like(sums_ref)

    normed = normed_ref[...]
    grad_hidden = sum_ref[...] + product_right_t(grad_ref[...], expand_w[...])
    grad_normed = grad_hidden * normed
    gain = small_ref[3:4, :]
    sums_ref[1:2, :] += jnp.sum(grad_normed, axis=0, keepdims=True)
    sums_ref[2:3, :] += jnp.sum(grad_hidden, axis=0, keepdims=True)
    scaled = grad_hidden * gain
    grad_sum = inverse_ref[...] * (
        scaled
        - jnp.mean(scaled, axis=-1, keepdims=True)
        - normed * jnp.mean(grad_normed * gain, axis=-1, keepdims=True)
    )
    next_ref[...] = grad_sum
    low = grad_sum.astype(bf16)
    low_ref[...] = low
    sums_ref[0:1, :] += jnp.sum(low.astype(f32), axis=0, keepdims=True)
    context_ref[...] = product_right_t(low, out_w[...]).astype(bf16)


def attended_grad(
    place, grad_sum, grad, normed, inverse, small, halves, shards
):
    rows, width = normed.shape
    ff = grad.shape[1]
    return kernel_call(
        partial(attended_grad_kernel, shards),
        "attended_grad",
        (rows // BLOCK,),
        [
            rows_spec(BLOCK, width),
            rows_spec(BLOCK, ff),
            rows_spec(BLOCK, width),
            rows_spec(BLOCK, 1),
            whole_spec(*small.shape),
        ]
        + anywhere(len(halves)),
        [
            rows_spec(BLOCK, width),
            rows_spec(BLOCK, width),
            rows_spec(BLOCK, width),
            whole_spec(8, width),
        ],
        [
            shaped((rows, width), f32),
            shaped((rows, width), bf16),
            shaped((rows, width), bf16),
            shaped((8, width), f32),
        ],
        [
            pltpu.VMEM((width, ff), bf16),
            pltpu.VMEM((width, width), bf16),
            pltpu.SemaphoreType.DMA((2, 2 * shards)),
        ],
        2 * rows * width * (ff + width),
        rows * (8 * width + ff) * 2,
        prefetch=1,
    )(place, grad_sum, grad, normed, inverse, small, *halves)


def tokens_grad_kernel(sum_ref, g0, g1, g2, weight_ref, out_ref):
    grad = sum_ref[...]
    for group, ref in enumerate((g0, g1, g2)):
        columns = slice(group * 3 * GROUP, (group + 1) * 3 * GROUP)
        grad = grad + product_right_t(ref[...], weight_ref[:, columns])
    out_ref[...] = grad.astype(bf16)


def tokens_grad(grad_sum, grads, weight, part, parts):
    rows, width = grad_sum.shape
    rows //= parts
    steps = rows // BLOCK

    def later(width):
        return pl.BlockSpec((BLOCK, width), lambda i: (part * steps + i, 0))

    return kernel_call(
        tokens_grad_kernel,
        "tokens_grad",
        (steps,),
        [later(width)] + [later(3 * GROUP)] * 3 + [whole_spec(*weight.shape)],
        rows_spec(BLOCK, width),
        shaped((rows, width), bf16),
        [],
        0,
        0,
        prefetch=0,
    )(grad_sum, *grads, weight)


def split_sum_kernel(axis, counts, kept, given, upper, held, *refs):
    others, outs = refs[: len(counts)], refs[len(counts) :]
    found = [(ref, at) for ref, count in zip(others, counts) for at in range(count)]
    for out, blocks in zip(outs, [kept, *given]):
        for to, block in enumerate(blocks):
            source, at = found[block]
            if axis is None:
                one, other = held[block], source[at]
            else:
                half = held.shape[axis] // 2
                which = upper[0] if out is outs[0] else 1 - upper[0]
                half_at = pl.ds(pl.multiple_of(which * half, 128 if axis == 2 else 16), half)
                where = (half_at, slice(None)) if axis == 1 else (slice(None), half_at)
                one, other = held[(block, *where)], source[(at, *where)]
            out[to] = (one.astype(f32) + other.astype(f32)).astype(bf16)


def split_sum(held, others, kept, given, axis, upper):
    shape = list(held.shape[1:])
    if axis is not None:
        shape[axis - 1] //= 2
        if shape[axis - 1] % (128 if axis == 2 else 16):
            total = low_sum(held, jnp.concatenate(others))
            size = shape[axis - 1]
            first, second = [
                lax.dynamic_slice_in_dim(total, at * size, size, axis) for at in (upper, 1 - upper)
            ]
            return first, [jnp.stack([second[block] for block in blocks]) for blocks in given]
    outs = [shaped((len(blocks), *shape), bf16) for blocks in [kept, *given]]
    if axis is None:
        columns = 768 if shape[1] % 768 == 0 else shape[1]

        def spec(one):
            return pl.BlockSpec((one.shape[0], shape[0], columns), lambda i, *_: (0, 0, i))

        first, *rest = kernel_call(
            partial(split_sum_kernel, axis, [one.shape[0] for one in others], kept, given),
            "split_sum",
            (shape[1] // columns,),
            [spec(one) for one in (held, *others)],
            [spec(one) for one in outs],
            outs,
            [],
            0,
            0,
            prefetch=1,
        )(upper.reshape(1), held, *others)
        return first, rest
    vmem = pl.BlockSpec(memory_space=pltpu.VMEM)
    first, *rest = pl.pallas_call(
        partial(split_sum_kernel, axis, [one.shape[0] for one in others], kept, given),
        name="split_sum",
        in_specs=[pl.BlockSpec(memory_space=pltpu.SMEM)] + [vmem] * (1 + len(others)),
        out_specs=[vmem] * len(outs),
        out_shape=outs,
        compiler_params=pltpu.CompilerParams(vmem_limit_bytes=VMEM_LIMIT),
        cost_estimate=pl.CostEstimate(flops=0, bytes_accessed=0, transcendentals=0),
    )(upper.reshape(1), held, *others)
    return first, rest


def low_sum(one, other):
    return (one.astype(f32) + other.astype(f32)).astype(bf16)


def replica_bits():
    distance, bits = 2, []
    while distance < lax.axis_size("replica"):
        bits.append(distance)
        distance *= 2
    return bits


def shard_terms(mine, peer):
    hold = yield [peer]
    other = after(lax.ppermute(peer, "replica", replica_partners(1)), hold)
    distances = range(1, mine.shape[0])
    own, given = split_sum(mine, [other], [0], [[d] for d in distances], None, jnp.int32(0))
    terms = {0: own}
    hold = yield given
    bits = shard_bits()
    for distances in (bits, [d for d in distances if d not in bits]):
        for d in distances:
            terms[d] = after(lax.ppermute(given[d - 1], "shard", shard_partners(d)), hold)
        if distances == bits:
            hold = yield [terms[d] for d in distances]
    terms = [terms[d] for d in range(mine.shape[0])]
    yield (terms, terms[-1])


def join_kernel(upper, contract_ref, *refs):
    terms, (kept_ref, given_ref) = refs[:-2], refs[-2:]
    rows, width = terms[0].shape[1], contract_ref.shape[1]

    def write(sum_ref, other_ref):
        for at in range(terms[0].shape[2] // width):
            columns = slice(at * width, (at + 1) * width)
            total = terms[0][0, :, columns].astype(f32)
            for ref in terms[1:]:
                total = total + ref[0, :, columns].astype(f32)
            sum_ref[0, at * rows : (at + 1) * rows, :] = total.astype(bf16)
        other_ref[0] = contract_ref[...]

    @pl.when(upper[0] == 0)
    def _():
        write(kept_ref, given_ref)

    @pl.when(upper[0] != 0)
    def _():
        write(given_ref, kept_ref)


def replica_sum(contract, terms):
    at = lax.axis_index("replica")
    vmem = pl.BlockSpec(memory_space=pltpu.VMEM)
    bits = replica_bits()
    uppers = [((at & bit) != 0).astype(jnp.int32) for bit in bits]
    shape = shaped((1, *contract.shape), bf16)
    held, given = pl.pallas_call(
        join_kernel,
        name="join",
        in_specs=[pl.BlockSpec(memory_space=pltpu.SMEM)] + [vmem] * (1 + len(terms)),
        out_specs=[vmem] * 2,
        out_shape=[shape, shape],
        cost_estimate=pl.CostEstimate(flops=0, bytes_accessed=0, transcendentals=0),
    )(uppers[0].reshape(1), contract, *terms)
    for step, bit in enumerate(bits):
        if step:
            held, (given,) = split_sum(held, [other], [0], [[0]], 1, uppers[step])
        hold = yield [given]
        other = after(lax.ppermute(given, "replica", replica_partners(bit)), hold)
    low = low_sum(held, other)[0]
    for bit in reversed(bits):
        hold = yield [low]
        other = after(lax.ppermute(low, "replica", replica_partners(bit)), hold)
        upper = (at & bit) != 0
        low = jnp.concatenate([jnp.where(upper, other, low), jnp.where(upper, low, other)])
    hold = yield [low]
    yield (low, after(lax.ppermute(low, "replica", replica_partners(1)), hold))


def reduction(mine, peer, stages, halved_axis, parted=0, whole=True):
    at = lax.axis_index("replica")
    held = mine
    hold = yield [peer]
    others = [after(lax.ppermute(peer, "replica", replica_partners(1)), hold)]
    distances = list(range(held.shape[0]))
    for step, (axis, bit) in enumerate(stages):
        partners = (shard_partners if axis == "shard" else replica_partners)(bit)
        if axis == "shard" or halved_axis:
            blocks = list(range(len(distances)))
            kept = sent = blocks
            if axis == "shard":
                kept = [i for i in blocks if not distances[i] & bit]
                sent = [i for i in blocks if distances[i] & bit]
                distances = [distances[i] for i in kept]
            half = len(sent) // 2
            given = [sent[:half], sent[half:]] if step < parted and half else [sent]
            upper = ((at & bit) != 0).astype(jnp.int32)
            held, given = split_sum(
                held, others, kept, given, None if axis == "shard" else halved_axis, upper
            )
        else:
            held = low_sum(held, others[0])
            given = [held]
        hold = yield given
        others = []
        for piece in given:
            if others:
                hold = yield others
            others.append(after(lax.ppermute(piece, axis, partners), hold))
    low = low_sum(held, others[0])[0]
    if not whole:
        yield (low, low)
    if halved_axis:
        for bit in [bit for axis, bit in reversed(stages) if axis == "replica"]:
            hold = yield [low]
            other = after(lax.ppermute(low, "replica", replica_partners(bit)), hold)
            upper = (at & bit) != 0
            low = jnp.concatenate(
                [jnp.where(upper, other, low), jnp.where(upper, low, other)], axis=halved_axis - 1
            )
    hold = yield [low]
    yield (low, after(lax.ppermute(low, "replica", replica_partners(1)), hold))


def pack_kernel(place, *refs):
    weights, vectors, outs, sems = refs[:7], refs[7:16], refs[16:19], refs[19]
    part, width = weights[0].shape
    groups = width // GROUP
    copies = []

    def add(source, columns, target):
        half = source.shape[0] // 2
        rows = pl.ds(pl.multiple_of(place[1] * half, 16), half)
        source = source.at[rows] if columns is None else source.at[rows, columns]
        copies.append(pltpu.make_async_copy(source, target, sems.at[len(copies)]))

    for group in range(groups):
        for at in range(3):
            to = (group * 3 + at) * GROUP
            target = outs[0].at[pl.ds(0, part // 2), pl.ds(to, GROUP)]
            add(weights[at], pl.ds(group * GROUP, GROUP), target)
    to = 0
    for at in (3, 6, 4):
        columns = weights[at].shape[1]
        add(weights[at], None, outs[1].at[:, pl.ds(to, columns)])
        to += columns
    add(weights[5], None, outs[2])
    for copy in copies:
        copy.start()
    long = vectors[8][...].astype(f32).reshape(1, -1)
    lines = [ref[...].astype(f32).reshape(1, -1) for ref in vectors[:8]]
    lines += [long[:, at : at + part] for at in range(0, long.shape[1], part)]
    row = rows_of(EXTRA, part)
    block = jnp.zeros((EXTRA, part), f32)
    for at, line in enumerate(lines):
        block = jnp.where(row == at, line, block)
    blank = jnp.zeros((EXTRA, outs[0].shape[1] - part), f32)
    outs[0][part // 2 :, :] = jnp.concatenate([block, blank], axis=1).astype(bf16)
    for copy in copies:
        copy.wait()


def pack(place, weights, vectors):
    part, width = weights[0].shape
    groups = width // GROUP
    half = part // 2
    shapes = [(half + EXTRA, 3 * width)]
    shapes += [(half, sum(weights[at].shape[1] for at in (3, 4, 6)))]
    shapes += [(weights[5].shape[0] // 2, weights[5].shape[1])]
    vmem = pl.BlockSpec(memory_space=pltpu.VMEM)
    return pl.pallas_call(
        pack_kernel,
        name="pack",
        in_specs=[pl.BlockSpec(memory_space=pltpu.SMEM)] + anywhere(7) + [vmem] * 9,
        out_specs=[vmem] * len(shapes),
        out_shape=[shaped(shape, bf16) for shape in shapes],
        scratch_shapes=[pltpu.SemaphoreType.DMA((3 * groups + 4,))],
    )(place, *weights, *vectors)


def vectors_kernel(part, place, *refs):
    parts, (small_ref, expand_ref, held, sems) = refs[:-4], refs[-4:]
    shards = len(parts)
    copies = [
        pltpu.make_async_copy(
            ref.at[pl.ds(ref.shape[0] - EXTRA, EXTRA), pl.ds(0, held.shape[2])],
            held.at[place[0] ^ d],
            sems.at[d],
        )
        for d, ref in enumerate(parts)
    ]
    for copy in copies:
        copy.start()
    for copy in copies:
        copy.wait()
    total = 0.0
    count = expand_ref.shape[1] // shards
    for shard in range(shards):
        block = held[shard].astype(f32)
        total = total + (pltpu.roll(block, shard * part, 1) if shard else block)
        line = 0.0
        for at in range(count // part):
            one = jnp.broadcast_to(block[8 + at : 9 + at, :], (8, block.shape[1]))
            line = line + (pltpu.roll(one, at * part, 1) if at else one)
        expand_ref[:, shard * count : (shard + 1) * count] = line[:, :count]
    small_ref[...] = total[:8]


def gather_vectors(place, parts, part, ff):
    vmem = pl.BlockSpec(memory_space=pltpu.VMEM)
    width = part * len(parts)
    return pl.pallas_call(
        partial(vectors_kernel, part),
        name="gather_vectors",
        in_specs=[pl.BlockSpec(memory_space=pltpu.SMEM)] + anywhere(len(parts)),
        out_specs=[vmem, vmem],
        out_shape=[shaped((8, width), f32), shaped((8, ff), f32)],
        scratch_shapes=[
            pltpu.VMEM((len(parts), EXTRA, width), bf16),
            pltpu.SemaphoreType.DMA((len(parts),)),
        ],
    )(place, *parts)


def join_halves(place, low_ref, other_ref, columns, out_ref):
    half = out_ref.shape[0] // 2
    for ref, which in ((low_ref, place[1]), (other_ref, 1 - place[1])):
        rows = pl.ds(pl.multiple_of(which * half, 8), half)
        out_ref[rows, :] = ref[0:half, columns].astype(f32)


def finish_ffn_kernel(place, low, other, expand_ref, contract_ref):
    half = contract_ref.shape[0] // 2
    width = low.shape[1]
    count = expand_ref.shape[1] // width
    size = half // count
    for ref, which in ((low, place[1]), (other, 1 - place[1])):
        to = pl.ds(pl.multiple_of(which * half, 8), half)
        contract_ref[to, :] = ref[half:, :].astype(f32)
        to = pl.ds(pl.multiple_of(which * size, 8), size)
        for at in range(count):
            columns = slice(at * width, (at + 1) * width)
            expand_ref[to, columns] = ref[at * size : (at + 1) * size, :].astype(f32)


def finish_ffn(place, low, other):
    vmem = pl.BlockSpec(memory_space=pltpu.VMEM)
    rows, width = low.shape
    parts = 4
    shapes = [(rows // parts, parts * width), (rows, width)]
    return pl.pallas_call(
        finish_ffn_kernel,
        name="finish_ffn",
        in_specs=[pl.BlockSpec(memory_space=pltpu.SMEM)] + [vmem] * 2,
        out_specs=[vmem] * 2,
        out_shape=[shaped(shape, f32) for shape in shapes],
        compiler_params=pltpu.CompilerParams(vmem_limit_bytes=VMEM_LIMIT),
    )(place, low, other)


def finish_attn_kernel(part, ff, place, *refs):
    pairs, refs = refs[:6], refs[6:]
    query, key, value, attn_out, colbert, rms = refs[:6]
    vectors = refs[6:]
    half = query.shape[0] // 2
    width = query.shape[1]
    for group in range(3):
        columns = slice(group * GROUP, (group + 1) * GROUP)
        for at, ref in enumerate((query, key, value)):
            source = slice(at * GROUP, (at + 1) * GROUP)
            join_halves(place, *pairs[2 * group : 2 * group + 2], source, ref.at[:, columns])
    at = 3 * GROUP
    join_halves(place, *pairs[:2], slice(at, at + width), attn_out)
    join_halves(place, *pairs[:2], slice(at + width, None), colbert)
    extra = pairs[0][half:, :width].astype(f32)
    lines = ff // width
    parts = width // part

    def own(block):
        return pltpu.roll(block, lax.rem(width - place[0] * part, width), 1)

    turned = own(extra)
    for at, ref in enumerate(vectors[2:8]):
        ref[...] = turned[at : at + 1, :part].reshape(part)
    size = ff // parts
    first = place[0] * size
    line = first // width
    row = rows_of(EXTRA, width)
    chosen = jnp.sum(jnp.where(row == 9 + line, extra, 0.0), axis=0, keepdims=True)
    chosen = jnp.broadcast_to(chosen, (8, width))
    chosen = pltpu.roll(chosen, lax.rem(width - lax.rem(first, width), width), 1)
    vectors[8][...] = chosen[0:1, :size].reshape(size)
    count = jnp.sum(jnp.where(row == 9 + lines, extra, 0.0)) / width
    lane = lanes(8, PAIR)
    squares = jnp.zeros((8, PAIR), f32)
    for at in range(3):
        total = jnp.sum(jnp.where(row == 6 + at, extra, 0.0))
        squares = jnp.where(lane == at, total, squares)
    rms[...] = jnp.sqrt(squares / (count * width))
    extra = own(pairs[4][half:, :width].astype(f32))
    for at, ref in enumerate(vectors[:2]):
        ref[...] = extra[at : at + 1, :part].reshape(part)


def finish_attn(place, sums, part, width, ff, out):
    vmem = pl.BlockSpec(memory_space=pltpu.VMEM)
    shapes = [(part, width)] * 4 + [(part, out), (8, PAIR)] + [(part,)] * 8
    shapes += [(ff * part // width,)]
    return pl.pallas_call(
        partial(finish_attn_kernel, part, ff),
        name="finish_attn",
        in_specs=[pl.BlockSpec(memory_space=pltpu.SMEM)] + [vmem] * 6,
        out_specs=[vmem] * len(shapes),
        out_shape=[shaped(shape, f32) for shape in shapes],
        compiler_params=pltpu.CompilerParams(vmem_limit_bytes=VMEM_LIMIT),
    )(place, *[one for pair in sums for one in pair])


def per_device(
    tokens,
    lengths,
    w_query,
    b_query,
    w_key,
    w_value,
    b_value,
    w_attn_out,
    b_attn_out,
    gain_one,
    shift_one,
    w_expand,
    b_expand,
    w_contract,
    b_contract,
    gain_two,
    shift_two,
    w_colbert,
    cotangent,
):
    seq_count, seq_len, width = tokens.shape
    rows = seq_count * seq_len
    shards = lax.axis_size("shard")
    part = width // shards
    half = part // 2
    mine = lax.axis_index("shard")
    core = lax.axis_index("replica") % 2
    ff = b_expand.shape[0] * shards
    out = w_colbert.shape[1]
    groups = width // GROUP
    place = jnp.stack([mine, core]).astype(jnp.int32)
    x = tokens.reshape(rows, width)

    vectors = (b_query, b_value, b_attn_out, gain_one, shift_one, b_contract, gain_two, shift_two)
    attn_weights = (w_query, w_key, w_value)
    bits = shard_bits()
    sent = pack(
        place,
        (*attn_weights, w_attn_out, w_expand, w_contract, w_colbert),
        (*vectors, b_expand),
    )
    attn_gather = Gather(attn_weights * groups, sent[0])
    contract_gather = Gather((w_contract,), sent[2])
    attn_gather.start()
    out_near = gather_halves(sent[1])
    attn_gather.swap()
    small, expand_b = gather_vectors(
        place, [sent[0]] + [attn_gather.near[d] for d in range(1, shards)], part, ff
    )
    attn_pieces = attn_gather.pieces()
    qkv, context, logsum, joined = attend(place, lengths, x, small, attn_pieces, shards, seq_len)
    out_halves = other_halves(after(out_near, logsum))
    contract_gather.start(logsum)
    normed, inverse, hidden_low, active, slope, squares = expand(
        place,
        lengths,
        x,
        context,
        small,
        expand_b,
        out_halves,
        shards,
        seq_len,
    )
    contract_gather.swap(squares)
    embeddings, grad_sum, grad_contracted, grad_expanded, sums, colbert = contract(
        place,
        lengths,
        active,
        slope,
        normed,
        small,
        cotangent.reshape(rows, out),
        out_halves,
        contract_gather.pieces(),
        shards,
        seq_len,
    )
    running, finals, token = {}, {}, []

    shard_stages = [("shard", bit) for bit in bits]
    replica_stages = [("replica", bit) for bit in replica_bits()]

    def begin(name, pieces, *how):
        running[name] = reduction(*pieces, *how)
        return next(running[name])

    def advance(*names):
        sent = []
        for name in names:
            value = running[name].send(token)
            if isinstance(value, tuple):
                finals[name] = value
                sent.append(value[1])
            else:
                sent += value
        return sent

    def scatter(mine, peer, hold):
        taken = after(lax.ppermute(peer, "replica", replica_partners(1)), hold)
        total = low_sum(mine, taken)
        total = total.reshape(-1, total.shape[-1])
        return total, lax.psum_scatter(total, "shard", scatter_dimension=0, tiled=True)

    contract_parts = contract_grad(place, active, grad_contracted, shards)
    *expand_parts, expand_sums = expand_grad(
        place, after(hidden_low, contract_parts), grad_expanded, shards
    )
    running["expand"] = shard_terms(*expand_parts)
    sent = next(running["expand"])
    token, low_c = scatter(*contract_parts, expand_sums)
    grad_sum, grad_low, grad_context, own_sums = attended_grad(
        place, after(grad_sum, token, sent), grad_expanded, normed, inverse, small, out_halves, shards
    )
    token = [own_sums]
    token = advance("expand")
    grads, biases = [], []
    plan = (("expand",), (0,), ("ffn", 0, 1))
    with_out = [context, grad_low, own_sums, sums, squares, expand_sums, colbert]
    last = groups - 1
    for group in range(groups):
        grad, bias, *pieces = attend_back(
            place,
            lengths,
            x,
            qkv,
            context,
            after(grad_context, token),
            logsum,
            group,
            biases if group == last else [],
            [] if group else with_out,
            shards,
            seq_len,
        )
        grads.append(grad)
        biases.append(bias)
        stages = shard_stages if group == last else shard_stages[::-1]
        sent = begin(group, pieces, stages + replica_stages, None if group else 2)
        token = [bias]
        if group == 1:
            low_c = after(low_c, token)
            advance("expand")
            running["ffn"] = replica_sum(low_c, finals.pop("expand")[0])
            del running["expand"]
            sent += next(running["ffn"])
        token = sent + advance(*plan[group])
    parts = 2
    grad_tokens = []
    for part_at in range(parts):
        grad_tokens.append(
            tokens_grad(after(grad_sum, token), grads, joined, part_at, parts)
        )
        token = [grad_tokens[-1]]
        token = advance(last, "ffn", 0, 1)
    grad_tokens = jnp.stack(grad_tokens)
    while len(finals) < len(running):
        token = advance(*[name for name in (last, "ffn", 0, 1) if name not in finals])
    r_we, r_wc = finish_ffn(place, *finals["ffn"])
    r_wq, r_wk, r_wv, r_wo, r_wp, rms_values, *r_small = finish_attn(
        place, [finals[group] for group in range(groups)], part, width, ff, out
    )
    r_bq, r_bv, r_bo, r_ga, r_sa, r_bc, r_gb, r_sb, r_be = r_small
    return (
        embeddings.reshape(seq_count, seq_len, out),
        grad_tokens.reshape(seq_count, seq_len, width),
        r_wq,
        r_bq,
        r_wk,
        r_wv,
        r_bv,
        r_wo,
        r_bo,
        r_ga,
        r_sa,
        r_we,
        r_be,
        r_wc,
        r_bc,
        r_gb,
        r_sb,
        r_wp,
        rms_values[0, :3],
    )


def solution(mesh):
    rows = P(("replica", "shard"), None, None)
    matrix, vector = P("shard", None), P("shard")
    weights = (
        matrix,
        vector,
        matrix,
        matrix,
        vector,
        matrix,
        vector,
        vector,
        vector,
        matrix,
        vector,
        matrix,
        vector,
        vector,
        vector,
        matrix,
    )
    return jax.shard_map(
        per_device,
        mesh=mesh,
        in_specs=(rows, P(("replica", "shard")), *weights, rows),
        out_specs=(rows, rows, *weights, P()),
        check_vma=False,
    )
```

```python
from functools import partial

import jax
import jax.numpy as jnp
from jax import lax
from jax.experimental import pallas as pl
from jax.experimental.pallas import tpu as pltpu
from jax.sharding import PartitionSpec as P

HEADS = 12
HEAD_DIM = 64
GROUP_HEADS = 4
GROUP = GROUP_HEADS * HEAD_DIM
PAIR = 2 * HEAD_DIM
EXTRA = 16
BLOCK = 256
CHUNK = 512
SCALE = HEAD_DIM**-0.5
VMEM_LIMIT = 52 * 1024 * 1024

norm_epsilon = 1e-12
masked_score = -1e30
f32 = jnp.float32
bf16 = jnp.bfloat16


def product(left, right):
    return jnp.dot(left, right, preferred_element_type=f32)


def product_left_t(left, right):
    return lax.dot_general(left, right, (((0,), (0,)), ((), ())), preferred_element_type=f32)


def product_right_t(left, right):
    return lax.dot_general(left, right, (((1,), (1,)), ((), ())), preferred_element_type=f32)


def shard_partners(distance):
    return [(i, i ^ distance) for i in range(lax.axis_size("shard"))]


def replica_partners(distance):
    return [(i, i ^ distance) for i in range(lax.axis_size("replica"))]


def after(value, *earlier):
    return lax.optimization_barrier((value, *jax.tree.leaves(earlier)))[0]


def shard_bits():
    distance, bits = 1, []
    while distance < lax.axis_size("shard"):
        bits.append(distance)
        distance *= 2
    return bits


def gather_halves(sent):
    return lax.all_gather(sent, "shard", axis=0)


def other_halves(near):
    return near, lax.ppermute(near, "replica", replica_partners(1))


def halves_copies(core, near, far, columns, target, sems):
    shards, half = near.shape[:2]
    copies = []
    for shard in range(shards):
        for ref, which in ((near, core), (far, 1 - core)):
            rows = pl.ds(pl.multiple_of((2 * shard + which) * half, 16), half)
            copies.append(
                pltpu.make_async_copy(
                    ref.at[shard, :, columns], target.at[rows], sems.at[len(copies)]
                )
            )
    return copies


class Gather:
    def __init__(self, own, sent, order=None):
        self.own = own
        self.sent = sent
        self.order = order
        self.near = {}
        self.far = {}

    def start(self, *earlier):
        sent = after(self.sent, *earlier)
        distances = self.order or range(1, lax.axis_size("shard"))
        for d in distances:
            self.near[d] = lax.ppermute(sent, "shard", shard_partners(d))

    def relay(self, *earlier):
        known = [self.order[0]]
        for distance in self.order[1:]:
            for d in known:
                piece = after(self.near[d], *earlier)
                self.near[d | distance] = lax.ppermute(piece, "shard", shard_partners(distance))
            known += [distance] + [d | distance for d in known]

    def swap(self, *earlier, distances=None):
        for d in distances or [d for d in self.near if d not in self.far]:
            piece = after(self.near[d], *earlier)
            self.far[d] = lax.ppermute(piece, "replica", replica_partners(1))

    def pieces(self):
        distances = range(1, lax.axis_size("shard"))
        return (*self.own, *[self.near[d] for d in distances], *[self.far[d] for d in distances])


def piece_count(shards, own):
    return own + 2 * (shards - 1)


def piece_copies(place, pieces, own, target, sems, first=0):
    mine, core = place[0], place[1]
    near = pieces[len(own) :]
    shards = len(near) // 2 + 1
    rows = pieces[0].shape[0]
    half = rows // 2
    copies = []

    def add(source, target):
        copies.append(pltpu.make_async_copy(source, target, sems.at[len(copies)]))

    place_at = 0
    for ref, columns in zip(pieces, own):
        at, width = columns or (0, ref.shape[1])
        if width != ref.shape[1]:
            ref = ref.at[:, pl.ds(at, width)]
        start = pl.multiple_of(mine * rows, 16)
        add(ref, target.at[pl.ds(start, rows), pl.ds(place_at, width)])
        place_at += width
    for d in range(1, shards):
        start = (mine ^ d) * rows
        for ref, which in ((near[d - 1], core), (near[shards + d - 2], 1 - core)):
            if ref.shape != (half, place_at):
                ref = ref.at[pl.ds(0, half), pl.ds(first, place_at)]
            add(ref, target.at[pl.ds(pl.multiple_of(start + which * half, 16), half)])
    return copies


def load_all(copies):
    for copy in copies:
        copy.start()
    for copy in copies:
        copy.wait()


def load_pieces(place, *sets):
    load_all([copy for one in sets for copy in piece_copies(place, *one)])


def store_pieces(mine, core, total, mine_ref, peer_ref, extra=None):
    shards = mine_ref.shape[0]
    half = total.shape[0] // (2 * shards)
    for d in range(shards):
        start = (mine ^ d) * 2
        for ref, which in ((mine_ref, core), (peer_ref, 1 - core)):
            at = pl.multiple_of((start + which) * half, 8)
            ref[d, 0:half] = total[pl.ds(at, half), :].astype(bf16)
            if extra is not None:
                ref[d, half:] = extra


def kernel_call(body, name, grid, in_specs, out_specs, out_shape, scratch, flops, moved, prefetch=2):
    return pl.pallas_call(
        body,
        name=name,
        grid_spec=pltpu.PrefetchScalarGridSpec(
            num_scalar_prefetch=prefetch,
            grid=grid,
            in_specs=in_specs,
            out_specs=out_specs,
            scratch_shapes=scratch,
        ),
        out_shape=out_shape,
        compiler_params=pltpu.CompilerParams(
            dimension_semantics=("arbitrary",) * len(grid), vmem_limit_bytes=VMEM_LIMIT
        ),
        cost_estimate=pl.CostEstimate(flops=flops, bytes_accessed=moved, transcendentals=0),
    )


def anywhere(count):
    return [pl.BlockSpec(memory_space=pl.ANY)] * count


def rows_spec(rows, width, column=0):
    return pl.BlockSpec((rows, width), lambda i, *_: (i, column))


def whole_spec(*shape):
    return pl.BlockSpec(shape, lambda *_: (0,) * len(shape))


def shaped(shape, dtype):
    return jax.ShapeDtypeStruct(shape, dtype)


def lanes(rows, width):
    return lax.broadcasted_iota(jnp.int32, (rows, width), 1)


def rows_of(rows, width):
    return lax.broadcasted_iota(jnp.int32, (rows, width), 0)


def attend_kernel(shards, groups, place, lengths, x_ref, bias_ref, *refs):
    count = piece_count(shards, 3 * groups)
    pieces, refs = refs[:count], refs[count:]
    qkv_ref, context_ref, logsum_ref, joined_ref, weight, sems = refs
    join = pltpu.make_async_copy(weight, joined_ref, sems.at[count])
    step, group = pl.program_id(0), pl.program_id(1)

    @pl.when((step == 0) & (group == 0))
    def _():
        load_pieces(place, (pieces, head_columns(groups), weight, sems))
        join.start()

    @pl.when((step == pl.num_programs(0) - 1) & (group == groups - 1))
    def _():
        join.wait()

    length = lengths[step]
    seq_len = x_ref.shape[0]
    no_bias = jnp.zeros((1, GROUP), f32)
    columns = pl.ds(pl.multiple_of(group * GROUP, GROUP), GROUP)
    bias = jnp.concatenate([bias_ref[0:1, columns], no_bias, bias_ref[1:2, columns]], axis=1)
    columns = pl.ds(pl.multiple_of(group * 3 * GROUP, GROUP), 3 * GROUP)
    qkv = (product(x_ref[...], weight[:, columns]) + bias).astype(bf16)
    qkv_ref[...] = qkv
    lane = lanes(seq_len, PAIR)
    padded = rows_of(seq_len, PAIR) >= length
    totals = jnp.ones((seq_len, PAIR), f32)
    highests = jnp.zeros((seq_len, PAIR), f32)
    sums = []
    for pair in range(GROUP_HEADS // 2):
        at = pair * PAIR
        queries = qkv[:, at : at + PAIR].astype(f32) * SCALE
        keys = qkv[:, GROUP + at : GROUP + at + PAIR].astype(f32)
        values = qkv[:, 2 * GROUP + at : 2 * GROUP + at + PAIR].astype(f32)
        for head in range(2):
            own = (lane >= HEAD_DIM) == (head == 1)
            free = lane == free_lane(pair, head)
            one = jnp.where(free, 1.0, 0.0)
            q = jnp.where(own, queries, one).astype(bf16)
            k = jnp.where(own, keys, jnp.where(padded, one * masked_score, 0.0)).astype(bf16)
            v = jnp.where(own, values, one).astype(bf16)
            scores = product_right_t(q, k)
            highest = jnp.max(scores, axis=-1, keepdims=True)
            exponent = jnp.exp(scores - highest).astype(bf16)
            summed = product(exponent, v)
            totals = jnp.where(free, summed, totals)
            highests = jnp.where(free, highest, highests)
            sums.append(summed)
    logsum_ref[...] = highests + jnp.log(totals)
    inverse = 1.0 / totals
    for pair in range(GROUP_HEADS // 2):
        halves = []
        for head in range(2):
            free = free_lane(pair, head)
            halves.append(sums[2 * pair + head] * inverse[:, free : free + 1])
        context = jnp.where(lane < HEAD_DIM, halves[0], halves[1])
        context_ref[:, pair * PAIR : (pair + 1) * PAIR] = context.astype(bf16)


def free_lane(pair, head):
    return HEAD_DIM * (1 - head) + pair


def head_columns(groups):
    return [(group * GROUP, GROUP) for group in range(groups) for _ in range(3)]


def attend(place, lengths, x, bias, pieces, shards, seq_len):
    rows, width = x.shape
    groups = width // GROUP

    def spec(columns):
        return pl.BlockSpec((seq_len, columns), lambda i, group, *_: (i, group))

    return kernel_call(
        partial(attend_kernel, shards, groups),
        "attend",
        (rows // seq_len, groups),
        [pl.BlockSpec((seq_len, width), lambda i, *_: (i, 0)), whole_spec(8, width)]
        + anywhere(len(pieces)),
        [spec(3 * GROUP), spec(GROUP), spec(PAIR)] + anywhere(1),
        [
            shaped((rows, 3 * width), bf16),
            shaped((rows, width), bf16),
            shaped((rows, groups * PAIR), f32),
            shaped((width, 3 * width), bf16),
        ],
        [
            pltpu.VMEM((width, 3 * width), bf16),
            pltpu.SemaphoreType.DMA((piece_count(shards, 3 * groups) + 1,)),
        ],
        groups * (2 * rows * width * 3 * GROUP + 16 * rows * seq_len * PAIR * GROUP_HEADS),
        groups * rows * (width + 6 * GROUP) * 2,
    )(place, lengths, x, bias, *pieces)


def split_low(value):
    high = value.astype(bf16).astype(f32)
    return high, value - high


def query_value_lines(before, sums):
    row = rows_of(EXTRA, GROUP)
    parts = [
        jnp.where(row == 0, one[:, :GROUP], jnp.where(row == 1, one[:, 2 * GROUP :], 0.0))
        for one in [ref[0:1, :] for ref in before] + [sums]
    ]
    return jnp.concatenate(parts, axis=1)


def vector_lines(lengths, own_sums, sums, squares, expand_sums, columns):
    width = own_sums.shape[1]
    positions = 0
    for seq in range(lengths.shape[0]):
        positions = positions + lengths[seq]
    lines = [own_sums[at : at + 1, :] for at in (0, 1, 2)]
    lines += [sums[at : at + 1, :] for at in (3, 1, 2)]
    lines += [squares[0:1, :], squares[1:2, :], sums[0:1, :]]
    lines += [expand_sums[0:1, at : at + width] for at in range(0, expand_sums.shape[1], width)]
    row = rows_of(EXTRA, width)
    extra = jnp.zeros((EXTRA, width), f32) + positions.astype(f32)
    for at, line in enumerate(lines):
        extra = jnp.where(row == at, line, extra)
    return jnp.concatenate([extra, jnp.zeros((EXTRA, columns - width), f32)], axis=1)


def attend_back_kernel(
    shards,
    before_count,
    with_out,
    place,
    lengths,
    x_ref,
    qkv_ref,
    context_ref,
    grad_ref,
    logsum_ref,
    *refs,
):
    before, refs = refs[:before_count], refs[before_count:]
    if with_out:
        (contexts, grad_low_ref, own_sums, sums_ref, squares, expand_sums, colbert) = refs[:7]
        refs = refs[7:]
    grads_ref, bias_ref, mine_ref, peer_ref, kept, total = refs
    step = pl.program_id(0)
    length = lengths[step]
    seq_len = qkv_ref.shape[0]
    lane = lanes(seq_len, PAIR)
    padded = rows_of(seq_len, PAIR) >= length
    for pair in range(GROUP_HEADS // 2):
        at = pair * PAIR
        queries = qkv_ref[:, at : at + PAIR].astype(f32) * SCALE
        keys = qkv_ref[:, GROUP + at : GROUP + at + PAIR].astype(f32)
        values = qkv_ref[:, 2 * GROUP + at : 2 * GROUP + at + PAIR].astype(f32)
        context = context_ref[:, at : at + PAIR].astype(f32)
        grad_low = grad_ref[:, at : at + PAIR]
        grad = grad_low.astype(f32)
        grad_context = grad * context
        grad_q, grad_k, grad_v = 0.0, [], []
        for head in range(2):
            own = (lane >= HEAD_DIM) == (head == 1)
            free = HEAD_DIM * (1 - head)
            first, second, third = lane == free, lane == free + 1, lane == free + 2
            source = free_lane(pair, head)
            logsum = logsum_ref[:, source : source + 1]
            delta = jnp.sum(jnp.where(own, grad_context, 0.0), axis=-1, keepdims=True)
            log_high, log_low = split_low(logsum)
            delta_high, delta_low = split_low(delta)
            one = jnp.where(first, 1.0, 0.0)
            other = jnp.where(second | third, 1.0, 0.0)
            low_lanes = jnp.where(second, -log_high, jnp.where(third, -log_low, one))
            q = jnp.where(own, queries, low_lanes).astype(bf16)
            k_lanes = jnp.where(padded, one * masked_score, 0.0) + other
            k = jnp.where(own, keys, k_lanes).astype(bf16)
            low_lanes = jnp.where(second, -delta_high, jnp.where(third, -delta_low, 0.0))
            g = jnp.where(own, grad, low_lanes).astype(bf16)
            v = jnp.where(own, values, other).astype(bf16)
            weights = jnp.exp(product_right_t(k, q))
            weights_low = weights.astype(bf16)
            grad_scores = (weights * product_right_t(v, g)).astype(bf16)
            grad_v.append(product(weights_low, grad_low))
            grad_k.append(product(grad_scores, q))
            only = jnp.where(own, keys, 0.0).astype(bf16)
            grad_q = grad_q + product_left_t(grad_scores, only)
        pieces = (
            grad_q * SCALE,
            jnp.where(lane < HEAD_DIM, grad_k[0], grad_k[1]),
            jnp.where(lane < HEAD_DIM, grad_v[0], grad_v[1]),
        )
        for which, piece in enumerate(pieces):
            columns = slice(which * GROUP + at, which * GROUP + at + PAIR)
            grads_ref[:, columns] = piece.astype(bf16)
    kept[pl.ds(pl.multiple_of(step * seq_len, 16), seq_len), :] = grads_ref[...]

    @pl.when(step == pl.num_programs(0) - 1)
    def _():
        grads = kept[...]
        sums = jnp.sum(grads.astype(f32), axis=0, keepdims=True)
        bias_ref[...] = jnp.broadcast_to(sums, bias_ref.shape)
        width = x_ref.shape[1]
        total[:, : 3 * GROUP] = product_left_t(x_ref[...], grads)
        extra = None
        if with_out:
            at = 3 * GROUP
            total[:, at : at + width] = product_left_t(contexts[...], grad_low_ref[...])
            total[:, at + width :] = colbert[...]
            extra = vector_lines(
                lengths, own_sums, sums_ref, squares, expand_sums, total.shape[1]
            ).astype(bf16)
        elif before_count:
            extra = query_value_lines(before, sums).astype(bf16)
        store_pieces(place[0], place[1], total, mine_ref, peer_ref, extra)


def attend_back(
    place, lengths, x, qkv, context, grad, logsum, group, before, with_out, shards, seq_len
):
    rows, width = x.shape
    half = width // (2 * shards) + (EXTRA if before or with_out else 0)
    columns = 3 * GROUP + (width + with_out[-1].shape[1] if with_out else 0)
    piece = shaped((shards, half, columns), bf16)
    return kernel_call(
        partial(attend_back_kernel, shards, len(before), bool(with_out)),
        "attend_back",
        (rows // seq_len,),
        [
            whole_spec(rows, width),
            rows_spec(seq_len, 3 * GROUP, group),
            rows_spec(seq_len, GROUP, group),
            rows_spec(seq_len, GROUP, group),
            rows_spec(seq_len, PAIR, group),
        ]
        + [whole_spec(*one.shape) for one in (*before, *with_out)],
        [
            rows_spec(seq_len, 3 * GROUP),
            whole_spec(8, 3 * GROUP),
            whole_spec(*piece.shape),
            whole_spec(*piece.shape),
        ],
        [shaped((rows, 3 * GROUP), bf16), shaped((8, 3 * GROUP), f32), piece, piece],
        [pltpu.VMEM((rows, 3 * GROUP), bf16), pltpu.VMEM((width, columns), f32)],
        2 * rows * width * columns + 40 * rows * seq_len * PAIR * GROUP_HEADS,
        rows * (2 * width + 9 * GROUP) * 2,
    )(place, lengths, x, qkv, context, grad, logsum, *before, *with_out)


def gelu_and_slope(u):
    share = 0.5 * lax.erf(u * 0.7071067811865476) + 0.5
    return u * share, share + (u * 0.3989422804014327) * jnp.exp(-0.5 * (u * u))


def valid_rows(lengths, step, rows, seq_len):
    first = step * rows
    seq = first // seq_len
    at = rows_of(rows, 1) + (first - seq * seq_len)
    return (at < lengths[seq]).astype(f32)


def out_expand_copies(place, near, far, out_w, expand_w, sems):
    width, ff = out_w.shape[1], expand_w.shape[1]
    first = near.shape[2] - ff
    copies = halves_copies(place[1], near, far, pl.ds(0, width), out_w, sems.at[0])
    return copies + halves_copies(place[1], near, far, pl.ds(first, ff), expand_w, sems.at[1])


def expand_kernel(shards, seq_len, place, lengths, x_ref, heads_ref, small_ref, expand_b, *refs):
    near, far, refs = refs[0], refs[1], refs[2:]
    normed_ref, inverse_ref, low_ref, active_ref, slope_ref, squares_ref = refs[:6]
    out_w, expand_w, sems = refs[6:]
    step = pl.program_id(0)
    width = x_ref.shape[1]

    @pl.when(step == 0)
    def _():
        copies = out_expand_copies(place, near, far, out_w, expand_w, sems)
        for copy in copies:
            copy.start()
        for copy in copies[: len(copies) // 2]:
            copy.wait()
        squares_ref[...] = jnp.zeros_like(squares_ref)

    rows = x_ref.shape[0]
    attended = product(heads_ref[...], out_w[...]) + small_ref[2:3, :]
    x = x_ref[...].astype(f32)
    valid = valid_rows(lengths, step, rows, seq_len)
    squares_ref[0:1, :] += jnp.sum(x * x * valid, axis=0, keepdims=True)
    squares_ref[1:2, :] += jnp.sum(attended * attended * valid, axis=0, keepdims=True)
    summed = x + attended
    center = summed - jnp.mean(summed, axis=-1, keepdims=True)
    inverse = lax.rsqrt(jnp.mean(center * center, axis=-1, keepdims=True) + norm_epsilon)
    normed = center * inverse
    normed_ref[...] = normed
    inverse_ref[...] = inverse
    low = (normed * small_ref[3:4, :] + small_ref[4:5, :]).astype(bf16)
    low_ref[...] = low

    @pl.when(step == 0)
    def _():
        copies = out_expand_copies(place, near, far, out_w, expand_w, sems)
        for copy in copies[len(copies) // 2 :]:
            copy.wait()

    for at in range(0, expand_w.shape[1], CHUNK):
        columns = slice(at, at + CHUNK)
        active, slope = gelu_and_slope(product(low, expand_w[:, columns]) + expand_b[0:1, columns])
        active_ref[:, columns] = active.astype(bf16)
        slope_ref[:, columns] = slope.astype(bf16)


def expand(place, lengths, x, context, small, expand_b, halves, shards, seq_len):
    rows, width = x.shape
    ff = expand_b.shape[1]
    return kernel_call(
        partial(expand_kernel, shards, seq_len),
        "expand",
        (rows // BLOCK,),
        [rows_spec(BLOCK, width)] * 2
        + [whole_spec(*small.shape), whole_spec(*expand_b.shape)]
        + anywhere(len(halves)),
        [
            rows_spec(BLOCK, width),
            rows_spec(BLOCK, 1),
            rows_spec(BLOCK, width),
            rows_spec(BLOCK, ff),
            rows_spec(BLOCK, ff),
            whole_spec(8, width),
        ],
        [
            shaped((rows, width), f32),
            shaped((rows, 1), f32),
            shaped((rows, width), bf16),
            shaped((rows, ff), bf16),
            shaped((rows, ff), bf16),
            shaped((8, width), f32),
        ],
        [
            pltpu.VMEM((width, width), bf16),
            pltpu.VMEM((width, ff), bf16),
            pltpu.SemaphoreType.DMA((2, 2 * shards)),
        ],
        6 * rows * width * (width + ff),
        rows * (6 * width + 2 * ff) * 2,
    )(place, lengths, x, context, small, expand_b, *halves)


def contract_kernel(
    shards, seq_len, place, lengths, active_ref, slope_ref, normed_ref, small_ref, cotangent_ref, *refs
):
    near, far = refs[:2]
    count = piece_count(shards, 1)
    pieces, refs = refs[2 : 2 + count], refs[2 + count :]
    embed_ref, sum_ref, low_ref, grad_ref, sums_ref, colbert_ref = refs[:6]
    contract_w, colbert_w, sems = refs[6:]
    step = pl.program_id(0)
    rows, width = normed_ref.shape
    out = colbert_w.shape[1]

    @pl.when(step == 0)
    def _():
        copies = piece_copies(place, pieces, [None], contract_w, sems.at[0])
        columns = pl.ds(width, out)
        load_all(copies + halves_copies(place[1], near, far, columns, colbert_w, sems.at[1]))
        sums_ref[...] = jnp.zeros_like(sums_ref)
        colbert_ref[...] = jnp.zeros_like(colbert_ref)

    gain_one, shift_one, bias = small_ref[3:4, :], small_ref[4:5, :], small_ref[5:6, :]
    gain, shift = small_ref[6:7, :], small_ref[7:8, :]
    blocks = [slice(at, at + BLOCK) for at in range(0, rows, BLOCK)]
    width = contract_w.shape[1]
    contracted, lows = {}, {}
    totals = [0.0, 0.0, 0.0, 0.0]

    def forward(at):
        parts = []
        for columns in range(0, width, GROUP):
            part = product(active_ref[blocks[at], :], contract_w[:, columns : columns + GROUP])
            parts.append(part)
            yield
        contracted[at] = jnp.concatenate(parts, axis=1) + bias

    def norm(at):
        block = blocks[at]
        valid = valid_rows(lengths, step * len(blocks) + at, BLOCK, seq_len)
        totals[0] += jnp.sum(contracted[at] * contracted[at] * valid, axis=0, keepdims=True)
        summed = normed_ref[block, :] * gain_one + shift_one + contracted[at]
        center = summed - jnp.mean(summed, axis=-1, keepdims=True)
        yield
        inverse = lax.rsqrt(jnp.mean(center * center, axis=-1, keepdims=True) + norm_epsilon)
        normed = center * inverse
        hidden_low = (normed * gain + shift).astype(bf16)
        projected = product(hidden_low, colbert_w[...])
        yield
        inverse_len = lax.rsqrt(
            jnp.sum(projected * projected, axis=-1, keepdims=True) + norm_epsilon
        )
        normalized = projected * inverse_len
        embed_ref[block, :] = (normalized * valid).astype(bf16)
        grad_norm = cotangent_ref[block, :].astype(f32) * valid
        grad_projected = (
            inverse_len
            * (grad_norm - normalized * jnp.sum(normalized * grad_norm, axis=-1, keepdims=True))
        ).astype(bf16)
        yield
        grad_hidden = product_right_t(grad_projected, colbert_w[...])
        colbert_ref[...] += product_left_t(hidden_low, grad_projected)
        yield
        grad_normed = grad_hidden * normed
        totals[1] += jnp.sum(grad_normed, axis=0, keepdims=True)
        totals[2] += jnp.sum(grad_hidden, axis=0, keepdims=True)
        scaled = grad_hidden * gain
        yield
        grad_sum = inverse * (
            scaled
            - jnp.mean(scaled, axis=-1, keepdims=True)
            - normed * jnp.mean(grad_normed * gain, axis=-1, keepdims=True)
        )
        sum_ref[block, :] = grad_sum
        low = grad_sum.astype(bf16)
        low_ref[block, :] = low
        totals[3] += jnp.sum(low.astype(f32), axis=0, keepdims=True)
        lows[at] = low

    def backward(at):
        for columns in range(0, contract_w.shape[0], CHUNK):
            columns = slice(columns, columns + CHUNK)
            grad = product_right_t(lows[at], contract_w[columns, :])
            slope = slope_ref[blocks[at], columns].astype(f32)
            grad_ref[blocks[at], columns] = (grad * slope).astype(bf16)
            yield

    def together(*parts):
        parts = list(parts)
        while parts:
            parts = [part for part in parts if next(part, parts) is not parts]

    together(forward(0))
    for at in range(len(blocks)):
        beside = [forward(at + 1)] if at + 1 < len(blocks) else []
        together(norm(at), *beside, *([backward(at - 1)] if at else []))
    together(backward(len(blocks) - 1))
    for at, total in enumerate(totals):
        sums_ref[at : at + 1, :] += total


def contract(
    place, lengths, active, slope, normed, small, cotangent, halves, pieces, shards, seq_len
):
    rows, width = normed.shape
    ff = active.shape[1]
    out = cotangent.shape[1]
    return kernel_call(
        partial(contract_kernel, shards, seq_len),
        "contract",
        (rows // (2 * BLOCK),),
        [
            rows_spec(2 * BLOCK, ff),
            rows_spec(2 * BLOCK, ff),
            rows_spec(2 * BLOCK, width),
            whole_spec(*small.shape),
            rows_spec(2 * BLOCK, out),
        ]
        + anywhere(len(halves) + len(pieces)),
        [
            rows_spec(2 * BLOCK, out),
            rows_spec(2 * BLOCK, width),
            rows_spec(2 * BLOCK, width),
            rows_spec(2 * BLOCK, ff),
            whole_spec(8, width),
            whole_spec(width, out),
        ],
        [
            shaped((rows, out), bf16),
            shaped((rows, width), f32),
            shaped((rows, width), bf16),
            shaped((rows, ff), bf16),
            shaped((8, width), f32),
            shaped((width, out), f32),
        ],
        [
            pltpu.VMEM((ff, width), bf16),
            pltpu.VMEM((width, out), bf16),
            pltpu.SemaphoreType.DMA((2, 2 * shards)),
        ],
        4 * rows * width * (ff + 2 * out),
        rows * (6 * width + 3 * ff) * 2,
    )(place, lengths, active, slope, normed, small, cotangent, *halves, *pieces)


def contract_grad_kernel(place, active_ref, grad_ref, mine_ref, peer_ref, total):
    total[...] = product_left_t(active_ref[...], grad_ref[...])
    half = mine_ref.shape[1]
    for ref, which in ((mine_ref, place[1]), (peer_ref, 1 - place[1])):
        ref[0] = total[pl.ds(pl.multiple_of(which * half, 8), half), :].astype(bf16)


def contract_grad(place, active, grad, shards):
    rows, ff = active.shape
    width = grad.shape[1]
    part = ff // shards
    piece = shaped((shards, part // 2, width), bf16)
    spec = pl.BlockSpec((1, part // 2, width), lambda i, *_: (i, 0, 0))
    return kernel_call(
        contract_grad_kernel,
        "contract_grad",
        (shards,),
        [pl.BlockSpec((rows, part), lambda i, *_: (0, i)), whole_spec(rows, width)],
        [spec, spec],
        [piece, piece],
        [pltpu.VMEM((part, width), f32)],
        2 * rows * width * ff,
        (rows * (width + ff) + width * ff) * 2,
        prefetch=1,
    )(place, active, grad)


def expand_grad_kernel(shards, place, low_ref, grad_ref, mine_ref, peer_ref, sums_ref, turned, total):
    width = low_ref.shape[1]

    @pl.when(pl.program_id(0) == 0)
    def _():
        turned[:width, :] = low_ref[...].T
        turned[width:, :] = jnp.ones((EXTRA, low_ref.shape[0]), bf16)

    total[...] = product(turned[...], grad_ref[...])
    sums_ref[...] = total[width : width + 8, :]
    store_pieces(place[0], place[1], total.at[:width], mine_ref, peer_ref)


def expand_grad(place, low, grad, shards):
    rows, ff = grad.shape
    width = low.shape[1]
    half = width // (2 * shards)
    piece = shaped((shards, half, ff), bf16)
    spec = pl.BlockSpec((shards, half, CHUNK), lambda i, *_: (0, 0, i))
    return kernel_call(
        partial(expand_grad_kernel, shards),
        "expand_grad",
        (ff // CHUNK,),
        [whole_spec(rows, width), pl.BlockSpec((rows, CHUNK), lambda i, *_: (0, i))],
        [spec, spec, pl.BlockSpec((8, CHUNK), lambda i, *_: (0, i))],
        [piece, piece, shaped((8, ff), f32)],
        [pltpu.VMEM((width + EXTRA, rows), bf16), pltpu.VMEM((width + EXTRA, CHUNK), f32)],
        2 * rows * width * ff,
        (rows * (width + ff) + width * ff) * 2,
        prefetch=1,
    )(place, low, grad)


def attended_grad_kernel(
    shards, place, sum_ref, grad_ref, normed_ref, inverse_ref, small_ref, *refs
):
    near, far, refs = refs[0], refs[1], refs[2:]
    next_ref, low_ref, context_ref, sums_ref = refs[:4]
    expand_w, out_w, sems = refs[4:]
    width = normed_ref.shape[1]

    @pl.when(pl.program_id(0) == 0)
    def _():
        load_all(out_expand_copies(place, near, far, out_w, expand_w, sems))
        sums_ref[...] = jnp.zeros_like(sums_ref)

    normed = normed_ref[...]
    grad_hidden = sum_ref[...] + product_right_t(grad_ref[...], expand_w[...])
    grad_normed = grad_hidden * normed
    gain = small_ref[3:4, :]
    sums_ref[1:2, :] += jnp.sum(grad_normed, axis=0, keepdims=True)
    sums_ref[2:3, :] += jnp.sum(grad_hidden, axis=0, keepdims=True)
    scaled = grad_hidden * gain
    grad_sum = inverse_ref[...] * (
        scaled
        - jnp.mean(scaled, axis=-1, keepdims=True)
        - normed * jnp.mean(grad_normed * gain, axis=-1, keepdims=True)
    )
    next_ref[...] = grad_sum
    low = grad_sum.astype(bf16)
    low_ref[...] = low
    sums_ref[0:1, :] += jnp.sum(low.astype(f32), axis=0, keepdims=True)
    context_ref[...] = product_right_t(low, out_w[...]).astype(bf16)


def attended_grad(
    place, grad_sum, grad, normed, inverse, small, halves, shards
):
    rows, width = normed.shape
    ff = grad.shape[1]
    return kernel_call(
        partial(attended_grad_kernel, shards),
        "attended_grad",
        (rows // BLOCK,),
        [
            rows_spec(BLOCK, width),
            rows_spec(BLOCK, ff),
            rows_spec(BLOCK, width),
            rows_spec(BLOCK, 1),
            whole_spec(*small.shape),
        ]
        + anywhere(len(halves)),
        [
            rows_spec(BLOCK, width),
            rows_spec(BLOCK, width),
            rows_spec(BLOCK, width),
            whole_spec(8, width),
        ],
        [
            shaped((rows, width), f32),
            shaped((rows, width), bf16),
            shaped((rows, width), bf16),
            shaped((8, width), f32),
        ],
        [
            pltpu.VMEM((width, ff), bf16),
            pltpu.VMEM((width, width), bf16),
            pltpu.SemaphoreType.DMA((2, 2 * shards)),
        ],
        2 * rows * width * (ff + width),
        rows * (8 * width + ff) * 2,
        prefetch=1,
    )(place, grad_sum, grad, normed, inverse, small, *halves)


def tokens_grad_kernel(sum_ref, g0, g1, g2, weight_ref, out_ref):
    grad = sum_ref[...]
    for group, ref in enumerate((g0, g1, g2)):
        columns = slice(group * 3 * GROUP, (group + 1) * 3 * GROUP)
        grad = grad + product_right_t(ref[...], weight_ref[:, columns])
    out_ref[...] = grad.astype(bf16)


def tokens_grad(grad_sum, grads, weight, part, parts):
    rows, width = grad_sum.shape
    rows //= parts
    steps = rows // BLOCK

    def later(width):
        return pl.BlockSpec((BLOCK, width), lambda i: (part * steps + i, 0))

    return kernel_call(
        tokens_grad_kernel,
        "tokens_grad",
        (steps,),
        [later(width)] + [later(3 * GROUP)] * 3 + [whole_spec(*weight.shape)],
        rows_spec(BLOCK, width),
        shaped((rows, width), bf16),
        [],
        0,
        0,
        prefetch=0,
    )(grad_sum, *grads, weight)


def split_sum_kernel(axis, counts, kept, given, upper, held, *refs):
    others, outs = refs[: len(counts)], refs[len(counts) :]
    found = [(ref, at) for ref, count in zip(others, counts) for at in range(count)]
    for out, blocks in zip(outs, [kept, *given]):
        for to, block in enumerate(blocks):
            source, at = found[block]
            if axis is None:
                one, other = held[block], source[at]
            else:
                half = held.shape[axis] // 2
                which = upper[0] if out is outs[0] else 1 - upper[0]
                half_at = pl.ds(pl.multiple_of(which * half, 128 if axis == 2 else 16), half)
                where = (half_at, slice(None)) if axis == 1 else (slice(None), half_at)
                one, other = held[(block, *where)], source[(at, *where)]
            out[to] = (one.astype(f32) + other.astype(f32)).astype(bf16)


def split_sum(held, others, kept, given, axis, upper):
    shape = list(held.shape[1:])
    if axis is not None:
        shape[axis - 1] //= 2
        if shape[axis - 1] % (128 if axis == 2 else 16):
            total = low_sum(held, jnp.concatenate(others))
            size = shape[axis - 1]
            first, second = [
                lax.dynamic_slice_in_dim(total, at * size, size, axis) for at in (upper, 1 - upper)
            ]
            return first, [jnp.stack([second[block] for block in blocks]) for blocks in given]
    outs = [shaped((len(blocks), *shape), bf16) for blocks in [kept, *given]]
    if axis is None:
        columns = 768 if shape[1] % 768 == 0 else shape[1]

        def spec(one):
            return pl.BlockSpec((one.shape[0], shape[0], columns), lambda i, *_: (0, 0, i))

        first, *rest = kernel_call(
            partial(split_sum_kernel, axis, [one.shape[0] for one in others], kept, given),
            "split_sum",
            (shape[1] // columns,),
            [spec(one) for one in (held, *others)],
            [spec(one) for one in outs],
            outs,
            [],
            0,
            0,
            prefetch=1,
        )(upper.reshape(1), held, *others)
        return first, rest
    vmem = pl.BlockSpec(memory_space=pltpu.VMEM)
    first, *rest = pl.pallas_call(
        partial(split_sum_kernel, axis, [one.shape[0] for one in others], kept, given),
        name="split_sum",
        in_specs=[pl.BlockSpec(memory_space=pltpu.SMEM)] + [vmem] * (1 + len(others)),
        out_specs=[vmem] * len(outs),
        out_shape=outs,
        compiler_params=pltpu.CompilerParams(vmem_limit_bytes=VMEM_LIMIT),
        cost_estimate=pl.CostEstimate(flops=0, bytes_accessed=0, transcendentals=0),
    )(upper.reshape(1), held, *others)
    return first, rest


def low_sum(one, other):
    return (one.astype(f32) + other.astype(f32)).astype(bf16)


def replica_bits():
    distance, bits = 2, []
    while distance < lax.axis_size("replica"):
        bits.append(distance)
        distance *= 2
    return bits


def shard_terms(mine, peer):
    hold = yield [peer]
    other = after(lax.ppermute(peer, "replica", replica_partners(1)), hold)
    distances = range(1, mine.shape[0])
    own, given = split_sum(mine, [other], [0], [[d] for d in distances], None, jnp.int32(0))
    terms = {0: own}
    hold = yield given
    bits = shard_bits()
    for distances in (bits, [d for d in distances if d not in bits]):
        for d in distances:
            terms[d] = after(lax.ppermute(given[d - 1], "shard", shard_partners(d)), hold)
        if distances == bits:
            hold = yield [terms[d] for d in distances]
    terms = [terms[d] for d in range(mine.shape[0])]
    yield (terms, terms[-1])


def join_kernel(upper, contract_ref, *refs):
    terms, (kept_ref, given_ref) = refs[:-2], refs[-2:]
    rows, width = terms[0].shape[1], contract_ref.shape[1]

    def write(sum_ref, other_ref):
        for at in range(terms[0].shape[2] // width):
            columns = slice(at * width, (at + 1) * width)
            total = terms[0][0, :, columns].astype(f32)
            for ref in terms[1:]:
                total = total + ref[0, :, columns].astype(f32)
            sum_ref[0, at * rows : (at + 1) * rows, :] = total.astype(bf16)
        other_ref[0] = contract_ref[...]

    @pl.when(upper[0] == 0)
    def _():
        write(kept_ref, given_ref)

    @pl.when(upper[0] != 0)
    def _():
        write(given_ref, kept_ref)


def replica_sum(contract, terms):
    at = lax.axis_index("replica")
    vmem = pl.BlockSpec(memory_space=pltpu.VMEM)
    bits = replica_bits()
    uppers = [((at & bit) != 0).astype(jnp.int32) for bit in bits]
    shape = shaped((1, *contract.shape), bf16)
    held, given = pl.pallas_call(
        join_kernel,
        name="join",
        in_specs=[pl.BlockSpec(memory_space=pltpu.SMEM)] + [vmem] * (1 + len(terms)),
        out_specs=[vmem] * 2,
        out_shape=[shape, shape],
        cost_estimate=pl.CostEstimate(flops=0, bytes_accessed=0, transcendentals=0),
    )(uppers[0].reshape(1), contract, *terms)
    for step, bit in enumerate(bits):
        if step:
            held, (given,) = split_sum(held, [other], [0], [[0]], 1, uppers[step])
        hold = yield [given]
        other = after(lax.ppermute(given, "replica", replica_partners(bit)), hold)
    low = low_sum(held, other)[0]
    for bit in reversed(bits):
        hold = yield [low]
        other = after(lax.ppermute(low, "replica", replica_partners(bit)), hold)
        upper = (at & bit) != 0
        low = jnp.concatenate([jnp.where(upper, other, low), jnp.where(upper, low, other)])
    hold = yield [low]
    yield (low, after(lax.ppermute(low, "replica", replica_partners(1)), hold))


def reduction(mine, peer, stages, halved_axis, parted=0, whole=True):
    at = lax.axis_index("replica")
    held = mine
    hold = yield [peer]
    others = [after(lax.ppermute(peer, "replica", replica_partners(1)), hold)]
    distances = list(range(held.shape[0]))
    for step, (axis, bit) in enumerate(stages):
        partners = (shard_partners if axis == "shard" else replica_partners)(bit)
        if axis == "shard" or halved_axis:
            blocks = list(range(len(distances)))
            kept = sent = blocks
            if axis == "shard":
                kept = [i for i in blocks if not distances[i] & bit]
                sent = [i for i in blocks if distances[i] & bit]
                distances = [distances[i] for i in kept]
            half = len(sent) // 2
            given = [sent[:half], sent[half:]] if step < parted and half else [sent]
            upper = ((at & bit) != 0).astype(jnp.int32)
            held, given = split_sum(
                held, others, kept, given, None if axis == "shard" else halved_axis, upper
            )
        else:
            held = low_sum(held, others[0])
            given = [held]
        hold = yield given
        others = []
        for piece in given:
            if others:
                hold = yield others
            others.append(after(lax.ppermute(piece, axis, partners), hold))
    low = low_sum(held, others[0])[0]
    if not whole:
        yield (low, low)
    if halved_axis:
        for bit in [bit for axis, bit in reversed(stages) if axis == "replica"]:
            hold = yield [low]
            other = after(lax.ppermute(low, "replica", replica_partners(bit)), hold)
            upper = (at & bit) != 0
            low = jnp.concatenate(
                [jnp.where(upper, other, low), jnp.where(upper, low, other)], axis=halved_axis - 1
            )
    hold = yield [low]
    yield (low, after(lax.ppermute(low, "replica", replica_partners(1)), hold))


def pack_kernel(place, *refs):
    weights, vectors, outs, sems = refs[:7], refs[7:16], refs[16:19], refs[19]
    part, width = weights[0].shape
    groups = width // GROUP
    copies = []

    def add(source, columns, target):
        half = source.shape[0] // 2
        rows = pl.ds(pl.multiple_of(place[1] * half, 16), half)
        source = source.at[rows] if columns is None else source.at[rows, columns]
        copies.append(pltpu.make_async_copy(source, target, sems.at[len(copies)]))

    for group in range(groups):
        for at in range(3):
            to = (group * 3 + at) * GROUP
            target = outs[0].at[pl.ds(0, part // 2), pl.ds(to, GROUP)]
            add(weights[at], pl.ds(group * GROUP, GROUP), target)
    to = 0
    for at in (3, 6, 4):
        columns = weights[at].shape[1]
        add(weights[at], None, outs[1].at[:, pl.ds(to, columns)])
        to += columns
    add(weights[5], None, outs[2])
    for copy in copies:
        copy.start()
    long = vectors[8][...].astype(f32).reshape(1, -1)
    lines = [ref[...].astype(f32).reshape(1, -1) for ref in vectors[:8]]
    lines += [long[:, at : at + part] for at in range(0, long.shape[1], part)]
    row = rows_of(EXTRA, part)
    block = jnp.zeros((EXTRA, part), f32)
    for at, line in enumerate(lines):
        block = jnp.where(row == at, line, block)
    blank = jnp.zeros((EXTRA, outs[0].shape[1] - part), f32)
    outs[0][part // 2 :, :] = jnp.concatenate([block, blank], axis=1).astype(bf16)
    for copy in copies:
        copy.wait()


def pack(place, weights, vectors):
    part, width = weights[0].shape
    groups = width // GROUP
    half = part // 2
    shapes = [(half + EXTRA, 3 * width)]
    shapes += [(half, sum(weights[at].shape[1] for at in (3, 4, 6)))]
    shapes += [(weights[5].shape[0] // 2, weights[5].shape[1])]
    vmem = pl.BlockSpec(memory_space=pltpu.VMEM)
    return pl.pallas_call(
        pack_kernel,
        name="pack",
        in_specs=[pl.BlockSpec(memory_space=pltpu.SMEM)] + anywhere(7) + [vmem] * 9,
        out_specs=[vmem] * len(shapes),
        out_shape=[shaped(shape, bf16) for shape in shapes],
        scratch_shapes=[pltpu.SemaphoreType.DMA((3 * groups + 4,))],
    )(place, *weights, *vectors)


def vectors_kernel(part, place, *refs):
    parts, (small_ref, expand_ref, held, sems) = refs[:-4], refs[-4:]
    shards = len(parts)
    copies = [
        pltpu.make_async_copy(
            ref.at[pl.ds(ref.shape[0] - EXTRA, EXTRA), pl.ds(0, held.shape[2])],
            held.at[place[0] ^ d],
            sems.at[d],
        )
        for d, ref in enumerate(parts)
    ]
    for copy in copies:
        copy.start()
    for copy in copies:
        copy.wait()
    total = 0.0
    count = expand_ref.shape[1] // shards
    for shard in range(shards):
        block = held[shard].astype(f32)
        total = total + (pltpu.roll(block, shard * part, 1) if shard else block)
        line = 0.0
        for at in range(count // part):
            one = jnp.broadcast_to(block[8 + at : 9 + at, :], (8, block.shape[1]))
            line = line + (pltpu.roll(one, at * part, 1) if at else one)
        expand_ref[:, shard * count : (shard + 1) * count] = line[:, :count]
    small_ref[...] = total[:8]


def gather_vectors(place, parts, part, ff):
    vmem = pl.BlockSpec(memory_space=pltpu.VMEM)
    width = part * len(parts)
    return pl.pallas_call(
        partial(vectors_kernel, part),
        name="gather_vectors",
        in_specs=[pl.BlockSpec(memory_space=pltpu.SMEM)] + anywhere(len(parts)),
        out_specs=[vmem, vmem],
        out_shape=[shaped((8, width), f32), shaped((8, ff), f32)],
        scratch_shapes=[
            pltpu.VMEM((len(parts), EXTRA, width), bf16),
            pltpu.SemaphoreType.DMA((len(parts),)),
        ],
    )(place, *parts)


def join_halves(place, low_ref, other_ref, columns, out_ref):
    half = out_ref.shape[0] // 2
    for ref, which in ((low_ref, place[1]), (other_ref, 1 - place[1])):
        rows = pl.ds(pl.multiple_of(which * half, 8), half)
        out_ref[rows, :] = ref[0:half, columns].astype(f32)


def finish_ffn_kernel(place, low, other, expand_ref, contract_ref):
    half = contract_ref.shape[0] // 2
    width = low.shape[1]
    count = expand_ref.shape[1] // width
    size = half // count
    for ref, which in ((low, place[1]), (other, 1 - place[1])):
        to = pl.ds(pl.multiple_of(which * half, 8), half)
        contract_ref[to, :] = ref[half:, :].astype(f32)
        to = pl.ds(pl.multiple_of(which * size, 8), size)
        for at in range(count):
            columns = slice(at * width, (at + 1) * width)
            expand_ref[to, columns] = ref[at * size : (at + 1) * size, :].astype(f32)


def finish_ffn(place, low, other):
    vmem = pl.BlockSpec(memory_space=pltpu.VMEM)
    rows, width = low.shape
    parts = 4
    shapes = [(rows // parts, parts * width), (rows, width)]
    return pl.pallas_call(
        finish_ffn_kernel,
        name="finish_ffn",
        in_specs=[pl.BlockSpec(memory_space=pltpu.SMEM)] + [vmem] * 2,
        out_specs=[vmem] * 2,
        out_shape=[shaped(shape, f32) for shape in shapes],
        compiler_params=pltpu.CompilerParams(vmem_limit_bytes=VMEM_LIMIT),
    )(place, low, other)


def finish_attn_kernel(part, ff, place, *refs):
    pairs, refs = refs[:6], refs[6:]
    query, key, value, attn_out, colbert, rms = refs[:6]
    vectors = refs[6:]
    half = query.shape[0] // 2
    width = query.shape[1]
    for group in range(3):
        columns = slice(group * GROUP, (group + 1) * GROUP)
        for at, ref in enumerate((query, key, value)):
            source = slice(at * GROUP, (at + 1) * GROUP)
            join_halves(place, *pairs[2 * group : 2 * group + 2], source, ref.at[:, columns])
    at = 3 * GROUP
    join_halves(place, *pairs[:2], slice(at, at + width), attn_out)
    join_halves(place, *pairs[:2], slice(at + width, None), colbert)
    extra = pairs[0][half:, :width].astype(f32)
    lines = ff // width
    parts = width // part

    def own(block):
        return pltpu.roll(block, lax.rem(width - place[0] * part, width), 1)

    turned = own(extra)
    for at, ref in enumerate(vectors[2:8]):
        ref[...] = turned[at : at + 1, :part].reshape(part)
    size = ff // parts
    first = place[0] * size
    line = first // width
    row = rows_of(EXTRA, width)
    chosen = jnp.sum(jnp.where(row == 9 + line, extra, 0.0), axis=0, keepdims=True)
    chosen = jnp.broadcast_to(chosen, (8, width))
    chosen = pltpu.roll(chosen, lax.rem(width - lax.rem(first, width), width), 1)
    vectors[8][...] = chosen[0:1, :size].reshape(size)
    count = jnp.sum(jnp.where(row == 9 + lines, extra, 0.0)) / width
    lane = lanes(8, PAIR)
    squares = jnp.zeros((8, PAIR), f32)
    for at in range(3):
        total = jnp.sum(jnp.where(row == 6 + at, extra, 0.0))
        squares = jnp.where(lane == at, total, squares)
    rms[...] = jnp.sqrt(squares / (count * width))
    extra = own(pairs[4][half:, :width].astype(f32))
    for at, ref in enumerate(vectors[:2]):
        ref[...] = extra[at : at + 1, :part].reshape(part)


def finish_attn(place, sums, part, width, ff, out):
    vmem = pl.BlockSpec(memory_space=pltpu.VMEM)
    shapes = [(part, width)] * 4 + [(part, out), (8, PAIR)] + [(part,)] * 8
    shapes += [(ff * part // width,)]
    return pl.pallas_call(
        partial(finish_attn_kernel, part, ff),
        name="finish_attn",
        in_specs=[pl.BlockSpec(memory_space=pltpu.SMEM)] + [vmem] * 6,
        out_specs=[vmem] * len(shapes),
        out_shape=[shaped(shape, f32) for shape in shapes],
        compiler_params=pltpu.CompilerParams(vmem_limit_bytes=VMEM_LIMIT),
    )(place, *[one for pair in sums for one in pair])


def per_device(
    tokens,
    lengths,
    w_query,
    b_query,
    w_key,
    w_value,
    b_value,
    w_attn_out,
    b_attn_out,
    gain_one,
    shift_one,
    w_expand,
    b_expand,
    w_contract,
    b_contract,
    gain_two,
    shift_two,
    w_colbert,
    cotangent,
):
    seq_count, seq_len, width = tokens.shape
    rows = seq_count * seq_len
    shards = lax.axis_size("shard")
    part = width // shards
    half = part // 2
    mine = lax.axis_index("shard")
    core = lax.axis_index("replica") % 2
    ff = b_expand.shape[0] * shards
    out = w_colbert.shape[1]
    groups = width // GROUP
    place = jnp.stack([mine, core]).astype(jnp.int32)
    x = tokens.reshape(rows, width)

    vectors = (b_query, b_value, b_attn_out, gain_one, shift_one, b_contract, gain_two, shift_two)
    attn_weights = (w_query, w_key, w_value)
    bits = shard_bits()
    sent = pack(
        place,
        (*attn_weights, w_attn_out, w_expand, w_contract, w_colbert),
        (*vectors, b_expand),
    )
    attn_gather = Gather(attn_weights * groups, sent[0])
    contract_gather = Gather((w_contract,), sent[2])
    attn_gather.start()
    out_near = gather_halves(sent[1])
    attn_gather.swap()
    small, expand_b = gather_vectors(
        place, [sent[0]] + [attn_gather.near[d] for d in range(1, shards)], part, ff
    )
    attn_pieces = attn_gather.pieces()
    qkv, context, logsum, joined = attend(place, lengths, x, small, attn_pieces, shards, seq_len)
    out_halves = other_halves(after(out_near, logsum))
    contract_gather.start(logsum)
    normed, inverse, hidden_low, active, slope, squares = expand(
        place,
        lengths,
        x,
        context,
        small,
        expand_b,
        out_halves,
        shards,
        seq_len,
    )
    contract_gather.swap(squares)
    embeddings, grad_sum, grad_contracted, grad_expanded, sums, colbert = contract(
        place,
        lengths,
        active,
        slope,
        normed,
        small,
        cotangent.reshape(rows, out),
        out_halves,
        contract_gather.pieces(),
        shards,
        seq_len,
    )
    running, finals, token = {}, {}, []

    shard_stages = [("shard", bit) for bit in bits]
    replica_stages = [("replica", bit) for bit in replica_bits()]

    def begin(name, pieces, *how):
        running[name] = reduction(*pieces, *how)
        return next(running[name])

    def advance(*names):
        sent = []
        for name in names:
            value = running[name].send(token)
            if isinstance(value, tuple):
                finals[name] = value
                sent.append(value[1])
            else:
                sent += value
        return sent

    def scatter(mine, peer, hold):
        taken = after(lax.ppermute(peer, "replica", replica_partners(1)), hold)
        total = low_sum(mine, taken)
        total = total.reshape(-1, total.shape[-1])
        return total, lax.psum_scatter(total, "shard", scatter_dimension=0, tiled=True)

    contract_parts = contract_grad(place, active, grad_contracted, shards)
    *expand_parts, expand_sums = expand_grad(
        place, after(hidden_low, contract_parts), grad_expanded, shards
    )
    running["expand"] = shard_terms(*expand_parts)
    sent = next(running["expand"])
    token, low_c = scatter(*contract_parts, expand_sums)
    grad_sum, grad_low, grad_context, own_sums = attended_grad(
        place, after(grad_sum, token, sent), grad_expanded, normed, inverse, small, out_halves, shards
    )
    token = [own_sums]
    token = advance("expand")
    grads, biases = [], []
    plan = (("expand",), (0,), ("ffn", 0, 1))
    with_out = [context, grad_low, own_sums, sums, squares, expand_sums, colbert]
    last = groups - 1
    for group in range(groups):
        grad, bias, *pieces = attend_back(
            place,
            lengths,
            x,
            qkv,
            context,
            after(grad_context, token),
            logsum,
            group,
            biases if group == last else [],
            [] if group else with_out,
            shards,
            seq_len,
        )
        grads.append(grad)
        biases.append(bias)
        stages = shard_stages if group == last else shard_stages[::-1]
        sent = begin(group, pieces, stages + replica_stages, None)
        token = [bias]
        if group == 1:
            low_c = after(low_c, token)
            advance("expand")
            running["ffn"] = replica_sum(low_c, finals.pop("expand")[0])
            del running["expand"]
            sent += next(running["ffn"])
        token = sent + advance(*plan[group])
    parts = 2
    grad_tokens = []
    for part_at in range(parts):
        grad_tokens.append(
            tokens_grad(after(grad_sum, token), grads, joined, part_at, parts)
        )
        token = [grad_tokens[-1]]
        token = advance(last, "ffn", 0, 1)
    grad_tokens = jnp.stack(grad_tokens)
    r_ffn = None
    while len(finals) < len(running):
        token = advance(*[name for name in (last, "ffn", 0, 1) if name not in finals])
        if "ffn" in finals and r_ffn is None:
            r_ffn = finish_ffn(place, *finals["ffn"])
            token = token + [r_ffn[0]]
    r_we, r_wc = r_ffn
    r_wq, r_wk, r_wv, r_wo, r_wp, rms_values, *r_small = finish_attn(
        place, [finals[group] for group in range(groups)], part, width, ff, out
    )
    r_bq, r_bv, r_bo, r_ga, r_sa, r_bc, r_gb, r_sb, r_be = r_small
    return (
        embeddings.reshape(seq_count, seq_len, out),
        grad_tokens.reshape(seq_count, seq_len, width),
        r_wq,
        r_bq,
        r_wk,
        r_wv,
        r_bv,
        r_wo,
        r_bo,
        r_ga,
        r_sa,
        r_we,
        r_be,
        r_wc,
        r_bc,
        r_gb,
        r_sb,
        r_wp,
        rms_values[0, :3],
    )


def solution(mesh):
    rows = P(("replica", "shard"), None, None)
    matrix, vector = P("shard", None), P("shard")
    weights = (
        matrix,
        vector,
        matrix,
        matrix,
        vector,
        matrix,
        vector,
        vector,
        vector,
        matrix,
        vector,
        matrix,
        vector,
        vector,
        vector,
        matrix,
    )
    return jax.shard_map(
        per_device,
        mesh=mesh,
        in_specs=(rows, P(("replica", "shard")), *weights, rows),
        out_specs=(rows, rows, *weights, P()),
        check_vma=False,
    )
```

```python
from functools import partial

import jax
import jax.numpy as jnp
from jax import lax
from jax.experimental import pallas as pl
from jax.experimental.pallas import tpu as pltpu
from jax.sharding import PartitionSpec as P

HEADS = 12
HEAD_DIM = 64
GROUP_HEADS = 4
GROUP = GROUP_HEADS * HEAD_DIM
PAIR = 2 * HEAD_DIM
EXTRA = 16
BLOCK = 256
CHUNK = 1024
SCALE = HEAD_DIM**-0.5
VMEM_LIMIT = 52 * 1024 * 1024

norm_epsilon = 1e-12
masked_score = -1e30
f32 = jnp.float32
bf16 = jnp.bfloat16


def product(left, right):
    return jnp.dot(left, right, preferred_element_type=f32)


def product_left_t(left, right):
    return lax.dot_general(left, right, (((0,), (0,)), ((), ())), preferred_element_type=f32)


def product_right_t(left, right):
    return lax.dot_general(left, right, (((1,), (1,)), ((), ())), preferred_element_type=f32)


def shard_partners(distance):
    return [(i, i ^ distance) for i in range(lax.axis_size("shard"))]


def replica_partners(distance):
    return [(i, i ^ distance) for i in range(lax.axis_size("replica"))]


def after(value, *earlier):
    return lax.optimization_barrier((value, *jax.tree.leaves(earlier)))[0]


def shard_bits():
    distance, bits = 1, []
    while distance < lax.axis_size("shard"):
        bits.append(distance)
        distance *= 2
    return bits


def gather_halves(sent):
    return lax.all_gather(sent, "shard", axis=0)


def other_halves(near):
    return near, lax.ppermute(near, "replica", replica_partners(1))


def halves_copies(core, near, far, columns, target, sems):
    shards, half = near.shape[:2]
    copies = []
    for shard in range(shards):
        for ref, which in ((near, core), (far, 1 - core)):
            rows = pl.ds(pl.multiple_of((2 * shard + which) * half, 16), half)
            copies.append(
                pltpu.make_async_copy(
                    ref.at[shard, :, columns], target.at[rows], sems.at[len(copies)]
                )
            )
    return copies


class Gather:
    def __init__(self, own, sent, order=None):
        self.own = own
        self.sent = sent
        self.order = order
        self.near = {}
        self.far = {}

    def start(self, *earlier):
        sent = after(self.sent, *earlier)
        distances = self.order or range(1, lax.axis_size("shard"))
        for d in distances:
            self.near[d] = lax.ppermute(sent, "shard", shard_partners(d))

    def relay(self, *earlier):
        known = [self.order[0]]
        for distance in self.order[1:]:
            for d in known:
                piece = after(self.near[d], *earlier)
                self.near[d | distance] = lax.ppermute(piece, "shard", shard_partners(distance))
            known += [distance] + [d | distance for d in known]

    def swap(self, *earlier, distances=None):
        for d in distances or [d for d in self.near if d not in self.far]:
            piece = after(self.near[d], *earlier)
            self.far[d] = lax.ppermute(piece, "replica", replica_partners(1))

    def pieces(self):
        distances = range(1, lax.axis_size("shard"))
        return (*self.own, *[self.near[d] for d in distances], *[self.far[d] for d in distances])


def piece_count(shards, own):
    return own + 2 * (shards - 1)


def piece_copies(place, pieces, own, target, sems, first=0):
    mine, core = place[0], place[1]
    near = pieces[len(own) :]
    shards = len(near) // 2 + 1
    rows = pieces[0].shape[0]
    half = rows // 2
    copies = []

    def add(source, target):
        copies.append(pltpu.make_async_copy(source, target, sems.at[len(copies)]))

    place_at = 0
    for ref, columns in zip(pieces, own):
        at, width = columns or (0, ref.shape[1])
        if width != ref.shape[1]:
            ref = ref.at[:, pl.ds(at, width)]
        start = pl.multiple_of(mine * rows, 16)
        add(ref, target.at[pl.ds(start, rows), pl.ds(place_at, width)])
        place_at += width
    for d in range(1, shards):
        start = (mine ^ d) * rows
        for ref, which in ((near[d - 1], core), (near[shards + d - 2], 1 - core)):
            if ref.shape != (half, place_at):
                ref = ref.at[pl.ds(0, half), pl.ds(first, place_at)]
            add(ref, target.at[pl.ds(pl.multiple_of(start + which * half, 16), half)])
    return copies


def load_all(copies):
    for copy in copies:
        copy.start()
    for copy in copies:
        copy.wait()


def load_pieces(place, *sets):
    load_all([copy for one in sets for copy in piece_copies(place, *one)])


def store_pieces(mine, core, total, mine_ref, peer_ref, extra=None):
    shards = mine_ref.shape[0]
    half = total.shape[0] // (2 * shards)
    for d in range(shards):
        start = (mine ^ d) * 2
        for ref, which in ((mine_ref, core), (peer_ref, 1 - core)):
            at = pl.multiple_of((start + which) * half, 8)
            ref[d, 0:half] = total[pl.ds(at, half), :].astype(bf16)
            if extra is not None:
                ref[d, half:] = extra


def kernel_call(body, name, grid, in_specs, out_specs, out_shape, scratch, flops, moved, prefetch=2):
    return pl.pallas_call(
        body,
        name=name,
        grid_spec=pltpu.PrefetchScalarGridSpec(
            num_scalar_prefetch=prefetch,
            grid=grid,
            in_specs=in_specs,
            out_specs=out_specs,
            scratch_shapes=scratch,
        ),
        out_shape=out_shape,
        compiler_params=pltpu.CompilerParams(
            dimension_semantics=("arbitrary",) * len(grid), vmem_limit_bytes=VMEM_LIMIT
        ),
        cost_estimate=pl.CostEstimate(flops=flops, bytes_accessed=moved, transcendentals=0),
    )


def anywhere(count):
    return [pl.BlockSpec(memory_space=pl.ANY)] * count


def rows_spec(rows, width, column=0):
    return pl.BlockSpec((rows, width), lambda i, *_: (i, column))


def whole_spec(*shape):
    return pl.BlockSpec(shape, lambda *_: (0,) * len(shape))


def shaped(shape, dtype):
    return jax.ShapeDtypeStruct(shape, dtype)


def lanes(rows, width):
    return lax.broadcasted_iota(jnp.int32, (rows, width), 1)


def rows_of(rows, width):
    return lax.broadcasted_iota(jnp.int32, (rows, width), 0)


def attend_kernel(shards, groups, place, lengths, x_ref, bias_ref, *refs):
    count = piece_count(shards, 3 * groups)
    pieces, refs = refs[:count], refs[count:]
    qkv_ref, context_ref, logsum_ref, joined_ref, weight, sems = refs
    join = pltpu.make_async_copy(weight, joined_ref, sems.at[count])
    step, group = pl.program_id(0), pl.program_id(1)

    @pl.when((step == 0) & (group == 0))
    def _():
        load_pieces(place, (pieces, head_columns(groups), weight, sems))
        join.start()

    @pl.when((step == pl.num_programs(0) - 1) & (group == groups - 1))
    def _():
        join.wait()

    length = lengths[step]
    seq_len = x_ref.shape[0]
    no_bias = jnp.zeros((1, GROUP), f32)
    columns = pl.ds(pl.multiple_of(group * GROUP, GROUP), GROUP)
    bias = jnp.concatenate([bias_ref[0:1, columns], no_bias, bias_ref[1:2, columns]], axis=1)
    columns = pl.ds(pl.multiple_of(group * 3 * GROUP, GROUP), 3 * GROUP)
    qkv = (product(x_ref[...], weight[:, columns]) + bias).astype(bf16)
    qkv_ref[...] = qkv
    lane = lanes(seq_len, PAIR)
    padded = rows_of(seq_len, PAIR) >= length
    totals = jnp.ones((seq_len, PAIR), f32)
    highests = jnp.zeros((seq_len, PAIR), f32)
    sums = []
    for pair in range(GROUP_HEADS // 2):
        at = pair * PAIR
        queries = qkv[:, at : at + PAIR].astype(f32) * SCALE
        keys = qkv[:, GROUP + at : GROUP + at + PAIR].astype(f32)
        values = qkv[:, 2 * GROUP + at : 2 * GROUP + at + PAIR].astype(f32)
        for head in range(2):
            own = (lane >= HEAD_DIM) == (head == 1)
            free = lane == free_lane(pair, head)
            one = jnp.where(free, 1.0, 0.0)
            q = jnp.where(own, queries, one).astype(bf16)
            k = jnp.where(own, keys, jnp.where(padded, one * masked_score, 0.0)).astype(bf16)
            v = jnp.where(own, values, one).astype(bf16)
            scores = product_right_t(q, k)
            highest = jnp.max(scores, axis=-1, keepdims=True)
            exponent = jnp.exp(scores - highest).astype(bf16)
            summed = product(exponent, v)
            totals = jnp.where(free, summed, totals)
            highests = jnp.where(free, highest, highests)
            sums.append(summed)
    logsum_ref[...] = highests + jnp.log(totals)
    inverse = 1.0 / totals
    for pair in range(GROUP_HEADS // 2):
        halves = []
        for head in range(2):
            free = free_lane(pair, head)
            halves.append(sums[2 * pair + head] * inverse[:, free : free + 1])
        context = jnp.where(lane < HEAD_DIM, halves[0], halves[1])
        context_ref[:, pair * PAIR : (pair + 1) * PAIR] = context.astype(bf16)


def free_lane(pair, head):
    return HEAD_DIM * (1 - head) + pair


def head_columns(groups):
    return [(group * GROUP, GROUP) for group in range(groups) for _ in range(3)]


def attend(place, lengths, x, bias, pieces, shards, seq_len):
    rows, width = x.shape
    groups = width // GROUP

    def spec(columns):
        return pl.BlockSpec((seq_len, columns), lambda i, group, *_: (i, group))

    return kernel_call(
        partial(attend_kernel, shards, groups),
        "attend",
        (rows // seq_len, groups),
        [pl.BlockSpec((seq_len, width), lambda i, *_: (i, 0)), whole_spec(8, width)]
        + anywhere(len(pieces)),
        [spec(3 * GROUP), spec(GROUP), spec(PAIR)] + anywhere(1),
        [
            shaped((rows, 3 * width), bf16),
            shaped((rows, width), bf16),
            shaped((rows, groups * PAIR), f32),
            shaped((width, 3 * width), bf16),
        ],
        [
            pltpu.VMEM((width, 3 * width), bf16),
            pltpu.SemaphoreType.DMA((piece_count(shards, 3 * groups) + 1,)),
        ],
        groups * (2 * rows * width * 3 * GROUP + 16 * rows * seq_len * PAIR * GROUP_HEADS),
        groups * rows * (width + 6 * GROUP) * 2,
    )(place, lengths, x, bias, *pieces)


def split_low(value):
    high = value.astype(bf16).astype(f32)
    return high, value - high


def query_value_lines(before, sums):
    row = rows_of(EXTRA, GROUP)
    parts = [
        jnp.where(row == 0, one[:, :GROUP], jnp.where(row == 1, one[:, 2 * GROUP :], 0.0))
        for one in [ref[0:1, :] for ref in before] + [sums]
    ]
    return jnp.concatenate(parts, axis=1)


def vector_lines(lengths, own_sums, sums, squares, expand_sums, columns):
    width = own_sums.shape[1]
    positions = 0
    for seq in range(lengths.shape[0]):
        positions = positions + lengths[seq]
    lines = [own_sums[at : at + 1, :] for at in (0, 1, 2)]
    lines += [sums[at : at + 1, :] for at in (3, 1, 2)]
    lines += [squares[0:1, :], squares[1:2, :], sums[0:1, :]]
    lines += [expand_sums[0:1, at : at + width] for at in range(0, expand_sums.shape[1], width)]
    row = rows_of(EXTRA, width)
    extra = jnp.zeros((EXTRA, width), f32) + positions.astype(f32)
    for at, line in enumerate(lines):
        extra = jnp.where(row == at, line, extra)
    return jnp.concatenate([extra, jnp.zeros((EXTRA, columns - width), f32)], axis=1)


def attend_back_kernel(
    shards,
    before_count,
    with_out,
    place,
    lengths,
    x_ref,
    qkv_ref,
    context_ref,
    grad_ref,
    logsum_ref,
    *refs,
):
    before, refs = refs[:before_count], refs[before_count:]
    if with_out:
        (contexts, grad_low_ref, own_sums, sums_ref, squares, expand_sums, colbert) = refs[:7]
        refs = refs[7:]
    grads_ref, bias_ref, mine_ref, peer_ref, kept, total = refs
    step = pl.program_id(0)
    length = lengths[step]
    seq_len = qkv_ref.shape[0]
    lane = lanes(seq_len, PAIR)
    padded = rows_of(seq_len, PAIR) >= length
    for pair in range(GROUP_HEADS // 2):
        at = pair * PAIR
        queries = qkv_ref[:, at : at + PAIR].astype(f32) * SCALE
        keys = qkv_ref[:, GROUP + at : GROUP + at + PAIR].astype(f32)
        values = qkv_ref[:, 2 * GROUP + at : 2 * GROUP + at + PAIR].astype(f32)
        context = context_ref[:, at : at + PAIR].astype(f32)
        grad_low = grad_ref[:, at : at + PAIR]
        grad = grad_low.astype(f32)
        grad_context = grad * context
        grad_q, grad_k, grad_v = 0.0, [], []
        for head in range(2):
            own = (lane >= HEAD_DIM) == (head == 1)
            free = HEAD_DIM * (1 - head)
            first, second, third = lane == free, lane == free + 1, lane == free + 2
            source = free_lane(pair, head)
            logsum = logsum_ref[:, source : source + 1]
            delta = jnp.sum(jnp.where(own, grad_context, 0.0), axis=-1, keepdims=True)
            log_high, log_low = split_low(logsum)
            delta_high, delta_low = split_low(delta)
            one = jnp.where(first, 1.0, 0.0)
            other = jnp.where(second | third, 1.0, 0.0)
            low_lanes = jnp.where(second, -log_high, jnp.where(third, -log_low, one))
            q = jnp.where(own, queries, low_lanes).astype(bf16)
            k_lanes = jnp.where(padded, one * masked_score, 0.0) + other
            k = jnp.where(own, keys, k_lanes).astype(bf16)
            low_lanes = jnp.where(second, -delta_high, jnp.where(third, -delta_low, 0.0))
            g = jnp.where(own, grad, low_lanes).astype(bf16)
            v = jnp.where(own, values, other).astype(bf16)
            weights = jnp.exp(product_right_t(k, q))
            weights_low = weights.astype(bf16)
            grad_scores = (weights * product_right_t(v, g)).astype(bf16)
            grad_v.append(product(weights_low, grad_low))
            grad_k.append(product(grad_scores, q))
            only = jnp.where(own, keys, 0.0).astype(bf16)
            grad_q = grad_q + product_left_t(grad_scores, only)
        pieces = (
            grad_q * SCALE,
            jnp.where(lane < HEAD_DIM, grad_k[0], grad_k[1]),
            jnp.where(lane < HEAD_DIM, grad_v[0], grad_v[1]),
        )
        for which, piece in enumerate(pieces):
            columns = slice(which * GROUP + at, which * GROUP + at + PAIR)
            grads_ref[:, columns] = piece.astype(bf16)
    kept[pl.ds(pl.multiple_of(step * seq_len, 16), seq_len), :] = grads_ref[...]

    @pl.when(step == pl.num_programs(0) - 1)
    def _():
        grads = kept[...]
        sums = jnp.sum(grads.astype(f32), axis=0, keepdims=True)
        bias_ref[...] = jnp.broadcast_to(sums, bias_ref.shape)
        width = x_ref.shape[1]
        total[:, : 3 * GROUP] = product_left_t(x_ref[...], grads)
        extra = None
        if with_out:
            at = 3 * GROUP
            total[:, at : at + width] = product_left_t(contexts[...], grad_low_ref[...])
            total[:, at + width :] = colbert[...]
            extra = vector_lines(
                lengths, own_sums, sums_ref, squares, expand_sums, total.shape[1]
            ).astype(bf16)
        elif before_count:
            extra = query_value_lines(before, sums).astype(bf16)
        store_pieces(place[0], place[1], total, mine_ref, peer_ref, extra)


def attend_back(
    place, lengths, x, qkv, context, grad, logsum, group, before, with_out, shards, seq_len
):
    rows, width = x.shape
    half = width // (2 * shards) + (EXTRA if before or with_out else 0)
    columns = 3 * GROUP + (width + with_out[-1].shape[1] if with_out else 0)
    piece = shaped((shards, half, columns), bf16)
    return kernel_call(
        partial(attend_back_kernel, shards, len(before), bool(with_out)),
        "attend_back",
        (rows // seq_len,),
        [
            whole_spec(rows, width),
            rows_spec(seq_len, 3 * GROUP, group),
            rows_spec(seq_len, GROUP, group),
            rows_spec(seq_len, GROUP, group),
            rows_spec(seq_len, PAIR, group),
        ]
        + [whole_spec(*one.shape) for one in (*before, *with_out)],
        [
            rows_spec(seq_len, 3 * GROUP),
            whole_spec(8, 3 * GROUP),
            whole_spec(*piece.shape),
            whole_spec(*piece.shape),
        ],
        [shaped((rows, 3 * GROUP), bf16), shaped((8, 3 * GROUP), f32), piece, piece],
        [pltpu.VMEM((rows, 3 * GROUP), bf16), pltpu.VMEM((width, columns), f32)],
        2 * rows * width * columns + 40 * rows * seq_len * PAIR * GROUP_HEADS,
        rows * (2 * width + 9 * GROUP) * 2,
    )(place, lengths, x, qkv, context, grad, logsum, *before, *with_out)


def gelu_and_slope(u):
    share = 0.5 * lax.erf(u * 0.7071067811865476) + 0.5
    return u * share, share + (u * 0.3989422804014327) * jnp.exp(-0.5 * (u * u))


def valid_rows(lengths, step, rows, seq_len):
    first = step * rows
    seq = first // seq_len
    at = rows_of(rows, 1) + (first - seq * seq_len)
    return (at < lengths[seq]).astype(f32)


def out_expand_copies(place, near, far, out_w, expand_w, sems):
    width, ff = out_w.shape[1], expand_w.shape[1]
    first = near.shape[2] - ff
    copies = halves_copies(place[1], near, far, pl.ds(0, width), out_w, sems.at[0])
    return copies + halves_copies(place[1], near, far, pl.ds(first, ff), expand_w, sems.at[1])


def expand_kernel(shards, seq_len, place, lengths, x_ref, heads_ref, small_ref, expand_b, *refs):
    near, far, refs = refs[0], refs[1], refs[2:]
    normed_ref, inverse_ref, low_ref, active_ref, slope_ref, squares_ref = refs[:6]
    out_w, expand_w, sems = refs[6:]
    step = pl.program_id(0)
    width = x_ref.shape[1]

    @pl.when(step == 0)
    def _():
        copies = out_expand_copies(place, near, far, out_w, expand_w, sems)
        for copy in copies:
            copy.start()
        for copy in copies[: len(copies) // 2]:
            copy.wait()
        squares_ref[...] = jnp.zeros_like(squares_ref)

    rows = x_ref.shape[0]
    attended = product(heads_ref[...], out_w[...]) + small_ref[2:3, :]
    x = x_ref[...].astype(f32)
    valid = valid_rows(lengths, step, rows, seq_len)
    squares_ref[0:1, :] += jnp.sum(x * x * valid, axis=0, keepdims=True)
    squares_ref[1:2, :] += jnp.sum(attended * attended * valid, axis=0, keepdims=True)
    summed = x + attended
    center = summed - jnp.mean(summed, axis=-1, keepdims=True)
    inverse = lax.rsqrt(jnp.mean(center * center, axis=-1, keepdims=True) + norm_epsilon)
    normed = center * inverse
    normed_ref[...] = normed
    inverse_ref[...] = inverse
    low = (normed * small_ref[3:4, :] + small_ref[4:5, :]).astype(bf16)
    low_ref[...] = low

    @pl.when(step == 0)
    def _():
        copies = out_expand_copies(place, near, far, out_w, expand_w, sems)
        for copy in copies[len(copies) // 2 :]:
            copy.wait()

    for at in range(0, expand_w.shape[1], CHUNK):
        columns = slice(at, at + CHUNK)
        active, slope = gelu_and_slope(product(low, expand_w[:, columns]) + expand_b[0:1, columns])
        active_ref[:, columns] = active.astype(bf16)
        slope_ref[:, columns] = slope.astype(bf16)


def expand(place, lengths, x, context, small, expand_b, halves, shards, seq_len):
    rows, width = x.shape
    ff = expand_b.shape[1]
    return kernel_call(
        partial(expand_kernel, shards, seq_len),
        "expand",
        (rows // BLOCK,),
        [rows_spec(BLOCK, width)] * 2
        + [whole_spec(*small.shape), whole_spec(*expand_b.shape)]
        + anywhere(len(halves)),
        [
            rows_spec(BLOCK, width),
            rows_spec(BLOCK, 1),
            rows_spec(BLOCK, width),
            rows_spec(BLOCK, ff),
            rows_spec(BLOCK, ff),
            whole_spec(8, width),
        ],
        [
            shaped((rows, width), f32),
            shaped((rows, 1), f32),
            shaped((rows, width), bf16),
            shaped((rows, ff), bf16),
            shaped((rows, ff), bf16),
            shaped((8, width), f32),
        ],
        [
            pltpu.VMEM((width, width), bf16),
            pltpu.VMEM((width, ff), bf16),
            pltpu.SemaphoreType.DMA((2, 2 * shards)),
        ],
        6 * rows * width * (width + ff),
        rows * (6 * width + 2 * ff) * 2,
    )(place, lengths, x, context, small, expand_b, *halves)


def contract_kernel(
    shards, seq_len, place, lengths, active_ref, slope_ref, normed_ref, small_ref, cotangent_ref, *refs
):
    near, far = refs[:2]
    count = piece_count(shards, 1)
    pieces, refs = refs[2 : 2 + count], refs[2 + count :]
    embed_ref, sum_ref, low_ref, grad_ref, sums_ref, colbert_ref = refs[:6]
    contract_w, colbert_w, sems = refs[6:]
    step = pl.program_id(0)
    rows, width = normed_ref.shape
    out = colbert_w.shape[1]

    @pl.when(step == 0)
    def _():
        copies = piece_copies(place, pieces, [None], contract_w, sems.at[0])
        columns = pl.ds(width, out)
        load_all(copies + halves_copies(place[1], near, far, columns, colbert_w, sems.at[1]))
        sums_ref[...] = jnp.zeros_like(sums_ref)
        colbert_ref[...] = jnp.zeros_like(colbert_ref)

    gain_one, shift_one, bias = small_ref[3:4, :], small_ref[4:5, :], small_ref[5:6, :]
    gain, shift = small_ref[6:7, :], small_ref[7:8, :]
    blocks = [slice(at, at + BLOCK) for at in range(0, rows, BLOCK)]
    width = contract_w.shape[1]
    contracted, lows = {}, {}
    totals = [0.0, 0.0, 0.0, 0.0]

    def forward(at):
        parts = []
        for columns in range(0, width, GROUP):
            part = product(active_ref[blocks[at], :], contract_w[:, columns : columns + GROUP])
            parts.append(part)
            yield
        contracted[at] = jnp.concatenate(parts, axis=1) + bias

    def norm(at):
        block = blocks[at]
        valid = valid_rows(lengths, step * len(blocks) + at, BLOCK, seq_len)
        totals[0] += jnp.sum(contracted[at] * contracted[at] * valid, axis=0, keepdims=True)
        summed = normed_ref[block, :] * gain_one + shift_one + contracted[at]
        center = summed - jnp.mean(summed, axis=-1, keepdims=True)
        yield
        inverse = lax.rsqrt(jnp.mean(center * center, axis=-1, keepdims=True) + norm_epsilon)
        normed = center * inverse
        hidden_low = (normed * gain + shift).astype(bf16)
        projected = product(hidden_low, colbert_w[...])
        yield
        inverse_len = lax.rsqrt(
            jnp.sum(projected * projected, axis=-1, keepdims=True) + norm_epsilon
        )
        normalized = projected * inverse_len
        embed_ref[block, :] = (normalized * valid).astype(bf16)
        grad_norm = cotangent_ref[block, :].astype(f32) * valid
        grad_projected = (
            inverse_len
            * (grad_norm - normalized * jnp.sum(normalized * grad_norm, axis=-1, keepdims=True))
        ).astype(bf16)
        yield
        grad_hidden = product_right_t(grad_projected, colbert_w[...])
        colbert_ref[...] += product_left_t(hidden_low, grad_projected)
        yield
        grad_normed = grad_hidden * normed
        totals[1] += jnp.sum(grad_normed, axis=0, keepdims=True)
        totals[2] += jnp.sum(grad_hidden, axis=0, keepdims=True)
        scaled = grad_hidden * gain
        yield
        grad_sum = inverse * (
            scaled
            - jnp.mean(scaled, axis=-1, keepdims=True)
            - normed * jnp.mean(grad_normed * gain, axis=-1, keepdims=True)
        )
        sum_ref[block, :] = grad_sum
        low = grad_sum.astype(bf16)
        low_ref[block, :] = low
        totals[3] += jnp.sum(low.astype(f32), axis=0, keepdims=True)
        lows[at] = low

    def backward(at):
        for columns in range(0, contract_w.shape[0], CHUNK):
            columns = slice(columns, columns + CHUNK)
            grad = product_right_t(lows[at], contract_w[columns, :])
            slope = slope_ref[blocks[at], columns].astype(f32)
            grad_ref[blocks[at], columns] = (grad * slope).astype(bf16)
            yield

    def together(*parts):
        parts = list(parts)
        while parts:
            parts = [part for part in parts if next(part, parts) is not parts]

    together(forward(0))
    for at in range(len(blocks)):
        beside = [forward(at + 1)] if at + 1 < len(blocks) else []
        together(norm(at), *beside, *([backward(at - 1)] if at else []))
    together(backward(len(blocks) - 1))
    for at, total in enumerate(totals):
        sums_ref[at : at + 1, :] += total


def contract(
    place, lengths, active, slope, normed, small, cotangent, halves, pieces, shards, seq_len
):
    rows, width = normed.shape
    ff = active.shape[1]
    out = cotangent.shape[1]
    return kernel_call(
        partial(contract_kernel, shards, seq_len),
        "contract",
        (rows // (2 * BLOCK),),
        [
            rows_spec(2 * BLOCK, ff),
            rows_spec(2 * BLOCK, ff),
            rows_spec(2 * BLOCK, width),
            whole_spec(*small.shape),
            rows_spec(2 * BLOCK, out),
        ]
        + anywhere(len(halves) + len(pieces)),
        [
            rows_spec(2 * BLOCK, out),
            rows_spec(2 * BLOCK, width),
            rows_spec(2 * BLOCK, width),
            rows_spec(2 * BLOCK, ff),
            whole_spec(8, width),
            whole_spec(width, out),
        ],
        [
            shaped((rows, out), bf16),
            shaped((rows, width), f32),
            shaped((rows, width), bf16),
            shaped((rows, ff), bf16),
            shaped((8, width), f32),
            shaped((width, out), f32),
        ],
        [
            pltpu.VMEM((ff, width), bf16),
            pltpu.VMEM((width, out), bf16),
            pltpu.SemaphoreType.DMA((2, 2 * shards)),
        ],
        4 * rows * width * (ff + 2 * out),
        rows * (6 * width + 3 * ff) * 2,
    )(place, lengths, active, slope, normed, small, cotangent, *halves, *pieces)


def contract_grad_kernel(place, active_ref, grad_ref, mine_ref, peer_ref, total):
    total[...] = product_left_t(active_ref[...], grad_ref[...])
    half = mine_ref.shape[1]
    for ref, which in ((mine_ref, place[1]), (peer_ref, 1 - place[1])):
        ref[0] = total[pl.ds(pl.multiple_of(which * half, 8), half), :].astype(bf16)


def contract_grad(place, active, grad, shards):
    rows, ff = active.shape
    width = grad.shape[1]
    part = ff // shards
    piece = shaped((shards, part // 2, width), bf16)
    spec = pl.BlockSpec((1, part // 2, width), lambda i, *_: (i, 0, 0))
    return kernel_call(
        contract_grad_kernel,
        "contract_grad",
        (shards,),
        [pl.BlockSpec((rows, part), lambda i, *_: (0, i)), whole_spec(rows, width)],
        [spec, spec],
        [piece, piece],
        [pltpu.VMEM((part, width), f32)],
        2 * rows * width * ff,
        (rows * (width + ff) + width * ff) * 2,
        prefetch=1,
    )(place, active, grad)


def expand_grad_kernel(shards, place, low_ref, grad_ref, mine_ref, peer_ref, sums_ref, turned, total):
    width = low_ref.shape[1]

    @pl.when(pl.program_id(0) == 0)
    def _():
        turned[:width, :] = low_ref[...].T
        turned[width:, :] = jnp.ones((EXTRA, low_ref.shape[0]), bf16)

    total[...] = product(turned[...], grad_ref[...])
    sums_ref[...] = total[width : width + 8, :]
    store_pieces(place[0], place[1], total.at[:width], mine_ref, peer_ref)


def expand_grad(place, low, grad, shards):
    rows, ff = grad.shape
    width = low.shape[1]
    half = width // (2 * shards)
    piece = shaped((shards, half, ff), bf16)
    spec = pl.BlockSpec((shards, half, CHUNK), lambda i, *_: (0, 0, i))
    return kernel_call(
        partial(expand_grad_kernel, shards),
        "expand_grad",
        (ff // CHUNK,),
        [whole_spec(rows, width), pl.BlockSpec((rows, CHUNK), lambda i, *_: (0, i))],
        [spec, spec, pl.BlockSpec((8, CHUNK), lambda i, *_: (0, i))],
        [piece, piece, shaped((8, ff), f32)],
        [pltpu.VMEM((width + EXTRA, rows), bf16), pltpu.VMEM((width + EXTRA, CHUNK), f32)],
        2 * rows * width * ff,
        (rows * (width + ff) + width * ff) * 2,
        prefetch=1,
    )(place, low, grad)


def attended_grad_kernel(
    shards, place, sum_ref, grad_ref, normed_ref, inverse_ref, small_ref, *refs
):
    near, far, refs = refs[0], refs[1], refs[2:]
    next_ref, low_ref, context_ref, sums_ref = refs[:4]
    expand_w, out_w, sems = refs[4:]
    width = normed_ref.shape[1]

    @pl.when(pl.program_id(0) == 0)
    def _():
        load_all(out_expand_copies(place, near, far, out_w, expand_w, sems))
        sums_ref[...] = jnp.zeros_like(sums_ref)

    normed = normed_ref[...]
    grad_hidden = sum_ref[...] + product_right_t(grad_ref[...], expand_w[...])
    grad_normed = grad_hidden * normed
    gain = small_ref[3:4, :]
    sums_ref[1:2, :] += jnp.sum(grad_normed, axis=0, keepdims=True)
    sums_ref[2:3, :] += jnp.sum(grad_hidden, axis=0, keepdims=True)
    scaled = grad_hidden * gain
    grad_sum = inverse_ref[...] * (
        scaled
        - jnp.mean(scaled, axis=-1, keepdims=True)
        - normed * jnp.mean(grad_normed * gain, axis=-1, keepdims=True)
    )
    next_ref[...] = grad_sum
    low = grad_sum.astype(bf16)
    low_ref[...] = low
    sums_ref[0:1, :] += jnp.sum(low.astype(f32), axis=0, keepdims=True)
    context_ref[...] = product_right_t(low, out_w[...]).astype(bf16)


def attended_grad(
    place, grad_sum, grad, normed, inverse, small, halves, shards
):
    rows, width = normed.shape
    ff = grad.shape[1]
    return kernel_call(
        partial(attended_grad_kernel, shards),
        "attended_grad",
        (rows // BLOCK,),
        [
            rows_spec(BLOCK, width),
            rows_spec(BLOCK, ff),
            rows_spec(BLOCK, width),
            rows_spec(BLOCK, 1),
            whole_spec(*small.shape),
        ]
        + anywhere(len(halves)),
        [
            rows_spec(BLOCK, width),
            rows_spec(BLOCK, width),
            rows_spec(BLOCK, width),
            whole_spec(8, width),
        ],
        [
            shaped((rows, width), f32),
            shaped((rows, width), bf16),
            shaped((rows, width), bf16),
            shaped((8, width), f32),
        ],
        [
            pltpu.VMEM((width, ff), bf16),
            pltpu.VMEM((width, width), bf16),
            pltpu.SemaphoreType.DMA((2, 2 * shards)),
        ],
        2 * rows * width * (ff + width),
        rows * (8 * width + ff) * 2,
        prefetch=1,
    )(place, grad_sum, grad, normed, inverse, small, *halves)


def tokens_grad_kernel(sum_ref, g0, g1, g2, weight_ref, out_ref):
    grad = sum_ref[...]
    for group, ref in enumerate((g0, g1, g2)):
        columns = slice(group * 3 * GROUP, (group + 1) * 3 * GROUP)
        grad = grad + product_right_t(ref[...], weight_ref[:, columns])
    out_ref[...] = grad.astype(bf16)


def tokens_grad(grad_sum, grads, weight, part, parts):
    rows, width = grad_sum.shape
    rows //= parts
    steps = rows // BLOCK

    def later(width):
        return pl.BlockSpec((BLOCK, width), lambda i: (part * steps + i, 0))

    return kernel_call(
        tokens_grad_kernel,
        "tokens_grad",
        (steps,),
        [later(width)] + [later(3 * GROUP)] * 3 + [whole_spec(*weight.shape)],
        rows_spec(BLOCK, width),
        shaped((rows, width), bf16),
        [],
        0,
        0,
        prefetch=0,
    )(grad_sum, *grads, weight)


def split_sum_kernel(axis, counts, kept, given, upper, held, *refs):
    others, outs = refs[: len(counts)], refs[len(counts) :]
    found = [(ref, at) for ref, count in zip(others, counts) for at in range(count)]
    for out, blocks in zip(outs, [kept, *given]):
        for to, block in enumerate(blocks):
            source, at = found[block]
            if axis is None:
                one, other = held[block], source[at]
            else:
                half = held.shape[axis] // 2
                which = upper[0] if out is outs[0] else 1 - upper[0]
                half_at = pl.ds(pl.multiple_of(which * half, 128 if axis == 2 else 16), half)
                where = (half_at, slice(None)) if axis == 1 else (slice(None), half_at)
                one, other = held[(block, *where)], source[(at, *where)]
            out[to] = (one.astype(f32) + other.astype(f32)).astype(bf16)


def split_sum(held, others, kept, given, axis, upper):
    shape = list(held.shape[1:])
    if axis is not None:
        shape[axis - 1] //= 2
        if shape[axis - 1] % (128 if axis == 2 else 16):
            total = low_sum(held, jnp.concatenate(others))
            size = shape[axis - 1]
            first, second = [
                lax.dynamic_slice_in_dim(total, at * size, size, axis) for at in (upper, 1 - upper)
            ]
            return first, [jnp.stack([second[block] for block in blocks]) for blocks in given]
    outs = [shaped((len(blocks), *shape), bf16) for blocks in [kept, *given]]
    if axis is None:
        columns = 768 if shape[1] % 768 == 0 else shape[1]

        def spec(one):
            return pl.BlockSpec((one.shape[0], shape[0], columns), lambda i, *_: (0, 0, i))

        first, *rest = kernel_call(
            partial(split_sum_kernel, axis, [one.shape[0] for one in others], kept, given),
            "split_sum",
            (shape[1] // columns,),
            [spec(one) for one in (held, *others)],
            [spec(one) for one in outs],
            outs,
            [],
            0,
            0,
            prefetch=1,
        )(upper.reshape(1), held, *others)
        return first, rest
    vmem = pl.BlockSpec(memory_space=pltpu.VMEM)
    first, *rest = pl.pallas_call(
        partial(split_sum_kernel, axis, [one.shape[0] for one in others], kept, given),
        name="split_sum",
        in_specs=[pl.BlockSpec(memory_space=pltpu.SMEM)] + [vmem] * (1 + len(others)),
        out_specs=[vmem] * len(outs),
        out_shape=outs,
        compiler_params=pltpu.CompilerParams(vmem_limit_bytes=VMEM_LIMIT),
        cost_estimate=pl.CostEstimate(flops=0, bytes_accessed=0, transcendentals=0),
    )(upper.reshape(1), held, *others)
    return first, rest


def low_sum(one, other):
    return (one.astype(f32) + other.astype(f32)).astype(bf16)


def replica_bits():
    distance, bits = 2, []
    while distance < lax.axis_size("replica"):
        bits.append(distance)
        distance *= 2
    return bits


def shard_terms(mine, peer):
    hold = yield [peer]
    other = after(lax.ppermute(peer, "replica", replica_partners(1)), hold)
    distances = range(1, mine.shape[0])
    own, given = split_sum(mine, [other], [0], [[d] for d in distances], None, jnp.int32(0))
    terms = {0: own}
    hold = yield given
    bits = shard_bits()
    for distances in (bits, [d for d in distances if d not in bits]):
        for d in distances:
            terms[d] = after(lax.ppermute(given[d - 1], "shard", shard_partners(d)), hold)
        if distances == bits:
            hold = yield [terms[d] for d in distances]
    terms = [terms[d] for d in range(mine.shape[0])]
    yield (terms, terms[-1])


def join_kernel(upper, contract_ref, *refs):
    terms, (kept_ref, given_ref) = refs[:-2], refs[-2:]
    rows, width = terms[0].shape[1], contract_ref.shape[1]

    def write(sum_ref, other_ref):
        for at in range(terms[0].shape[2] // width):
            columns = slice(at * width, (at + 1) * width)
            total = terms[0][0, :, columns].astype(f32)
            for ref in terms[1:]:
                total = total + ref[0, :, columns].astype(f32)
            sum_ref[0, at * rows : (at + 1) * rows, :] = total.astype(bf16)
        other_ref[0] = contract_ref[...]

    @pl.when(upper[0] == 0)
    def _():
        write(kept_ref, given_ref)

    @pl.when(upper[0] != 0)
    def _():
        write(given_ref, kept_ref)


def replica_sum(contract, terms):
    at = lax.axis_index("replica")
    vmem = pl.BlockSpec(memory_space=pltpu.VMEM)
    bits = replica_bits()
    uppers = [((at & bit) != 0).astype(jnp.int32) for bit in bits]
    shape = shaped((1, *contract.shape), bf16)
    held, given = pl.pallas_call(
        join_kernel,
        name="join",
        in_specs=[pl.BlockSpec(memory_space=pltpu.SMEM)] + [vmem] * (1 + len(terms)),
        out_specs=[vmem] * 2,
        out_shape=[shape, shape],
        cost_estimate=pl.CostEstimate(flops=0, bytes_accessed=0, transcendentals=0),
    )(uppers[0].reshape(1), contract, *terms)
    for step, bit in enumerate(bits):
        if step:
            held, (given,) = split_sum(held, [other], [0], [[0]], 1, uppers[step])
        hold = yield [given]
        other = after(lax.ppermute(given, "replica", replica_partners(bit)), hold)
    low = low_sum(held, other)[0]
    for bit in reversed(bits):
        hold = yield [low]
        other = after(lax.ppermute(low, "replica", replica_partners(bit)), hold)
        upper = (at & bit) != 0
        low = jnp.concatenate([jnp.where(upper, other, low), jnp.where(upper, low, other)])
    hold = yield [low]
    yield (low, after(lax.ppermute(low, "replica", replica_partners(1)), hold))


def reduction(mine, peer, stages, halved_axis, parted=0, whole=True):
    at = lax.axis_index("replica")
    held = mine
    hold = yield [peer]
    others = [after(lax.ppermute(peer, "replica", replica_partners(1)), hold)]
    distances = list(range(held.shape[0]))
    for step, (axis, bit) in enumerate(stages):
        partners = (shard_partners if axis == "shard" else replica_partners)(bit)
        if axis == "shard" or halved_axis:
            blocks = list(range(len(distances)))
            kept = sent = blocks
            if axis == "shard":
                kept = [i for i in blocks if not distances[i] & bit]
                sent = [i for i in blocks if distances[i] & bit]
                distances = [distances[i] for i in kept]
            half = len(sent) // 2
            given = [sent[:half], sent[half:]] if step < parted and half else [sent]
            upper = ((at & bit) != 0).astype(jnp.int32)
            held, given = split_sum(
                held, others, kept, given, None if axis == "shard" else halved_axis, upper
            )
        else:
            held = low_sum(held, others[0])
            given = [held]
        hold = yield given
        others = []
        for piece in given:
            if others:
                hold = yield others
            others.append(after(lax.ppermute(piece, axis, partners), hold))
    low = low_sum(held, others[0])[0]
    if not whole:
        yield (low, low)
    if halved_axis:
        for bit in [bit for axis, bit in reversed(stages) if axis == "replica"]:
            hold = yield [low]
            other = after(lax.ppermute(low, "replica", replica_partners(bit)), hold)
            upper = (at & bit) != 0
            low = jnp.concatenate(
                [jnp.where(upper, other, low), jnp.where(upper, low, other)], axis=halved_axis - 1
            )
    hold = yield [low]
    yield (low, after(lax.ppermute(low, "replica", replica_partners(1)), hold))


def pack_kernel(place, *refs):
    weights, vectors, outs, sems = refs[:7], refs[7:16], refs[16:19], refs[19]
    part, width = weights[0].shape
    groups = width // GROUP
    copies = []

    def add(source, columns, target):
        half = source.shape[0] // 2
        rows = pl.ds(pl.multiple_of(place[1] * half, 16), half)
        source = source.at[rows] if columns is None else source.at[rows, columns]
        copies.append(pltpu.make_async_copy(source, target, sems.at[len(copies)]))

    for group in range(groups):
        for at in range(3):
            to = (group * 3 + at) * GROUP
            target = outs[0].at[pl.ds(0, part // 2), pl.ds(to, GROUP)]
            add(weights[at], pl.ds(group * GROUP, GROUP), target)
    to = 0
    for at in (3, 6, 4):
        columns = weights[at].shape[1]
        add(weights[at], None, outs[1].at[:, pl.ds(to, columns)])
        to += columns
    add(weights[5], None, outs[2])
    for copy in copies:
        copy.start()
    long = vectors[8][...].astype(f32).reshape(1, -1)
    lines = [ref[...].astype(f32).reshape(1, -1) for ref in vectors[:8]]
    lines += [long[:, at : at + part] for at in range(0, long.shape[1], part)]
    row = rows_of(EXTRA, part)
    block = jnp.zeros((EXTRA, part), f32)
    for at, line in enumerate(lines):
        block = jnp.where(row == at, line, block)
    blank = jnp.zeros((EXTRA, outs[0].shape[1] - part), f32)
    outs[0][part // 2 :, :] = jnp.concatenate([block, blank], axis=1).astype(bf16)
    for copy in copies:
        copy.wait()


def pack(place, weights, vectors):
    part, width = weights[0].shape
    groups = width // GROUP
    half = part // 2
    shapes = [(half + EXTRA, 3 * width)]
    shapes += [(half, sum(weights[at].shape[1] for at in (3, 4, 6)))]
    shapes += [(weights[5].shape[0] // 2, weights[5].shape[1])]
    vmem = pl.BlockSpec(memory_space=pltpu.VMEM)
    return pl.pallas_call(
        pack_kernel,
        name="pack",
        in_specs=[pl.BlockSpec(memory_space=pltpu.SMEM)] + anywhere(7) + [vmem] * 9,
        out_specs=[vmem] * len(shapes),
        out_shape=[shaped(shape, bf16) for shape in shapes],
        scratch_shapes=[pltpu.SemaphoreType.DMA((3 * groups + 4,))],
    )(place, *weights, *vectors)


def vectors_kernel(part, place, *refs):
    parts, (small_ref, expand_ref, held, sems) = refs[:-4], refs[-4:]
    shards = len(parts)
    copies = [
        pltpu.make_async_copy(
            ref.at[pl.ds(ref.shape[0] - EXTRA, EXTRA), pl.ds(0, held.shape[2])],
            held.at[place[0] ^ d],
            sems.at[d],
        )
        for d, ref in enumerate(parts)
    ]
    for copy in copies:
        copy.start()
    for copy in copies:
        copy.wait()
    total = 0.0
    count = expand_ref.shape[1] // shards
    for shard in range(shards):
        block = held[shard].astype(f32)
        total = total + (pltpu.roll(block, shard * part, 1) if shard else block)
        line = 0.0
        for at in range(count // part):
            one = jnp.broadcast_to(block[8 + at : 9 + at, :], (8, block.shape[1]))
            line = line + (pltpu.roll(one, at * part, 1) if at else one)
        expand_ref[:, shard * count : (shard + 1) * count] = line[:, :count]
    small_ref[...] = total[:8]


def gather_vectors(place, parts, part, ff):
    vmem = pl.BlockSpec(memory_space=pltpu.VMEM)
    width = part * len(parts)
    return pl.pallas_call(
        partial(vectors_kernel, part),
        name="gather_vectors",
        in_specs=[pl.BlockSpec(memory_space=pltpu.SMEM)] + anywhere(len(parts)),
        out_specs=[vmem, vmem],
        out_shape=[shaped((8, width), f32), shaped((8, ff), f32)],
        scratch_shapes=[
            pltpu.VMEM((len(parts), EXTRA, width), bf16),
            pltpu.SemaphoreType.DMA((len(parts),)),
        ],
    )(place, *parts)


def join_halves(place, low_ref, other_ref, columns, out_ref):
    half = out_ref.shape[0] // 2
    for ref, which in ((low_ref, place[1]), (other_ref, 1 - place[1])):
        rows = pl.ds(pl.multiple_of(which * half, 8), half)
        out_ref[rows, :] = ref[0:half, columns].astype(f32)


def finish_ffn_kernel(place, low, other, expand_ref, contract_ref):
    half = contract_ref.shape[0] // 2
    width = low.shape[1]
    count = expand_ref.shape[1] // width
    size = half // count
    for ref, which in ((low, place[1]), (other, 1 - place[1])):
        to = pl.ds(pl.multiple_of(which * half, 8), half)
        contract_ref[to, :] = ref[half:, :].astype(f32)
        to = pl.ds(pl.multiple_of(which * size, 8), size)
        for at in range(count):
            columns = slice(at * width, (at + 1) * width)
            expand_ref[to, columns] = ref[at * size : (at + 1) * size, :].astype(f32)


def finish_ffn(place, low, other):
    vmem = pl.BlockSpec(memory_space=pltpu.VMEM)
    rows, width = low.shape
    parts = 4
    shapes = [(rows // parts, parts * width), (rows, width)]
    return pl.pallas_call(
        finish_ffn_kernel,
        name="finish_ffn",
        in_specs=[pl.BlockSpec(memory_space=pltpu.SMEM)] + [vmem] * 2,
        out_specs=[vmem] * 2,
        out_shape=[shaped(shape, f32) for shape in shapes],
        compiler_params=pltpu.CompilerParams(vmem_limit_bytes=VMEM_LIMIT),
    )(place, low, other)


def finish_attn_kernel(part, ff, place, *refs):
    pairs, refs = refs[:6], refs[6:]
    query, key, value, attn_out, colbert, rms = refs[:6]
    vectors = refs[6:]
    half = query.shape[0] // 2
    width = query.shape[1]
    for group in range(3):
        columns = slice(group * GROUP, (group + 1) * GROUP)
        for at, ref in enumerate((query, key, value)):
            source = slice(at * GROUP, (at + 1) * GROUP)
            join_halves(place, *pairs[2 * group : 2 * group + 2], source, ref.at[:, columns])
    at = 3 * GROUP
    join_halves(place, *pairs[:2], slice(at, at + width), attn_out)
    join_halves(place, *pairs[:2], slice(at + width, None), colbert)
    extra = pairs[0][half:, :width].astype(f32)
    lines = ff // width
    parts = width // part

    def own(block):
        return pltpu.roll(block, lax.rem(width - place[0] * part, width), 1)

    turned = own(extra)
    for at, ref in enumerate(vectors[2:8]):
        ref[...] = turned[at : at + 1, :part].reshape(part)
    size = ff // parts
    first = place[0] * size
    line = first // width
    row = rows_of(EXTRA, width)
    chosen = jnp.sum(jnp.where(row == 9 + line, extra, 0.0), axis=0, keepdims=True)
    chosen = jnp.broadcast_to(chosen, (8, width))
    chosen = pltpu.roll(chosen, lax.rem(width - lax.rem(first, width), width), 1)
    vectors[8][...] = chosen[0:1, :size].reshape(size)
    count = jnp.sum(jnp.where(row == 9 + lines, extra, 0.0)) / width
    lane = lanes(8, PAIR)
    squares = jnp.zeros((8, PAIR), f32)
    for at in range(3):
        total = jnp.sum(jnp.where(row == 6 + at, extra, 0.0))
        squares = jnp.where(lane == at, total, squares)
    rms[...] = jnp.sqrt(squares / (count * width))
    extra = own(pairs[4][half:, :width].astype(f32))
    for at, ref in enumerate(vectors[:2]):
        ref[...] = extra[at : at + 1, :part].reshape(part)


def finish_attn(place, sums, part, width, ff, out):
    vmem = pl.BlockSpec(memory_space=pltpu.VMEM)
    shapes = [(part, width)] * 4 + [(part, out), (8, PAIR)] + [(part,)] * 8
    shapes += [(ff * part // width,)]
    return pl.pallas_call(
        partial(finish_attn_kernel, part, ff),
        name="finish_attn",
        in_specs=[pl.BlockSpec(memory_space=pltpu.SMEM)] + [vmem] * 6,
        out_specs=[vmem] * len(shapes),
        out_shape=[shaped(shape, f32) for shape in shapes],
        compiler_params=pltpu.CompilerParams(vmem_limit_bytes=VMEM_LIMIT),
    )(place, *[one for pair in sums for one in pair])


def per_device(
    tokens,
    lengths,
    w_query,
    b_query,
    w_key,
    w_value,
    b_value,
    w_attn_out,
    b_attn_out,
    gain_one,
    shift_one,
    w_expand,
    b_expand,
    w_contract,
    b_contract,
    gain_two,
    shift_two,
    w_colbert,
    cotangent,
):
    seq_count, seq_len, width = tokens.shape
    rows = seq_count * seq_len
    shards = lax.axis_size("shard")
    part = width // shards
    half = part // 2
    mine = lax.axis_index("shard")
    core = lax.axis_index("replica") % 2
    ff = b_expand.shape[0] * shards
    out = w_colbert.shape[1]
    groups = width // GROUP
    place = jnp.stack([mine, core]).astype(jnp.int32)
    x = tokens.reshape(rows, width)

    vectors = (b_query, b_value, b_attn_out, gain_one, shift_one, b_contract, gain_two, shift_two)
    attn_weights = (w_query, w_key, w_value)
    bits = shard_bits()
    sent = pack(
        place,
        (*attn_weights, w_attn_out, w_expand, w_contract, w_colbert),
        (*vectors, b_expand),
    )
    attn_gather = Gather(attn_weights * groups, sent[0])
    contract_gather = Gather((w_contract,), sent[2])
    attn_gather.start()
    out_near = gather_halves(sent[1])
    attn_gather.swap()
    small, expand_b = gather_vectors(
        place, [sent[0]] + [attn_gather.near[d] for d in range(1, shards)], part, ff
    )
    attn_pieces = attn_gather.pieces()
    qkv, context, logsum, joined = attend(place, lengths, x, small, attn_pieces, shards, seq_len)
    out_halves = other_halves(after(out_near, logsum))
    contract_gather.start(logsum)
    normed, inverse, hidden_low, active, slope, squares = expand(
        place,
        lengths,
        x,
        context,
        small,
        expand_b,
        out_halves,
        shards,
        seq_len,
    )
    contract_gather.swap(squares)
    embeddings, grad_sum, grad_contracted, grad_expanded, sums, colbert = contract(
        place,
        lengths,
        active,
        slope,
        normed,
        small,
        cotangent.reshape(rows, out),
        out_halves,
        contract_gather.pieces(),
        shards,
        seq_len,
    )
    running, finals, token = {}, {}, []

    shard_stages = [("shard", bit) for bit in bits]
    replica_stages = [("replica", bit) for bit in replica_bits()]

    def begin(name, pieces, *how):
        running[name] = reduction(*pieces, *how)
        return next(running[name])

    def advance(*names):
        sent = []
        for name in names:
            value = running[name].send(token)
            if isinstance(value, tuple):
                finals[name] = value
                sent.append(value[1])
            else:
                sent += value
        return sent

    def scatter(mine, peer, hold):
        taken = after(lax.ppermute(peer, "replica", replica_partners(1)), hold)
        total = low_sum(mine, taken)
        total = total.reshape(-1, total.shape[-1])
        return total, lax.psum_scatter(total, "shard", scatter_dimension=0, tiled=True)

    contract_parts = contract_grad(place, active, grad_contracted, shards)
    *expand_parts, expand_sums = expand_grad(
        place, after(hidden_low, contract_parts), grad_expanded, shards
    )
    running["expand"] = shard_terms(*expand_parts)
    sent = next(running["expand"])
    token, low_c = scatter(*contract_parts, expand_sums)
    grad_sum, grad_low, grad_context, own_sums = attended_grad(
        place, after(grad_sum, token, sent), grad_expanded, normed, inverse, small, out_halves, shards
    )
    token = [own_sums]
    token = advance("expand")
    grads, biases = [], []
    plan = (("expand",), (0,), ("ffn", 0, 1))
    with_out = [context, grad_low, own_sums, sums, squares, expand_sums, colbert]
    last = groups - 1
    for group in range(groups):
        grad, bias, *pieces = attend_back(
            place,
            lengths,
            x,
            qkv,
            context,
            after(grad_context, token),
            logsum,
            group,
            biases if group == last else [],
            [] if group else with_out,
            shards,
            seq_len,
        )
        grads.append(grad)
        biases.append(bias)
        stages = shard_stages[::-1] if group == 1 else shard_stages
        sent = begin(group, pieces, stages + replica_stages, None)
        token = [bias]
        if group == 1:
            low_c = after(low_c, token)
            advance("expand")
            running["ffn"] = replica_sum(low_c, finals.pop("expand")[0])
            del running["expand"]
            sent += next(running["ffn"])
        token = sent + advance(*plan[group])
    parts = 2
    grad_tokens = []
    for part_at in range(parts):
        grad_tokens.append(
            tokens_grad(after(grad_sum, token), grads, joined, part_at, parts)
        )
        token = [grad_tokens[-1]]
        token = advance(last, "ffn", 0, 1)
    grad_tokens = jnp.stack(grad_tokens)
    r_ffn = None
    while len(finals) < len(running):
        token = advance(*[name for name in (last, "ffn", 0, 1) if name not in finals])
        if "ffn" in finals and r_ffn is None:
            r_ffn = finish_ffn(place, *finals["ffn"])
            token = token + [r_ffn[0]]
    r_we, r_wc = r_ffn
    r_wq, r_wk, r_wv, r_wo, r_wp, rms_values, *r_small = finish_attn(
        place, [finals[group] for group in range(groups)], part, width, ff, out
    )
    r_bq, r_bv, r_bo, r_ga, r_sa, r_bc, r_gb, r_sb, r_be = r_small
    return (
        embeddings.reshape(seq_count, seq_len, out),
        grad_tokens.reshape(seq_count, seq_len, width),
        r_wq,
        r_bq,
        r_wk,
        r_wv,
        r_bv,
        r_wo,
        r_bo,
        r_ga,
        r_sa,
        r_we,
        r_be,
        r_wc,
        r_bc,
        r_gb,
        r_sb,
        r_wp,
        rms_values[0, :3],
    )


def solution(mesh):
    rows = P(("replica", "shard"), None, None)
    matrix, vector = P("shard", None), P("shard")
    weights = (
        matrix,
        vector,
        matrix,
        matrix,
        vector,
        matrix,
        vector,
        vector,
        vector,
        matrix,
        vector,
        matrix,
        vector,
        vector,
        vector,
        matrix,
    )
    return jax.shard_map(
        per_device,
        mesh=mesh,
        in_specs=(rows, P(("replica", "shard")), *weights, rows),
        out_specs=(rows, rows, *weights, P()),
        check_vma=False,
    )
```
